32 devices in a mesh: view: 4 (over z), tile: 8 (over y, x, core).
Axes of the slice: x: 2, y: 2, z: 4, core: 2. Of those that a mesh axis runs over, the one named last changes fastest.
Arguments:
- centres: float32 [3, 32768], P(None, ('view', 'tile')), may hold values from -6 to 6
- shape_raw: float32 [6, 32768], P(None, ('view', 'tile')), may hold values from -1 to 0.2
- opacity_logit: float32 [32768], P(('view', 'tile')), may hold values from -6 to -1
- colours: float32 [3, 32768], P(None, ('view', 'tile')), may hold values from -6 to 6
- camera: float32 [8, 2, 4], replicated, may hold values from -15 to 15
- target: float32 [8, 128, 3, 256], P('view', 'tile'), may hold values from -3 to 3
- intersection_ids: int32 [8, 128, 256], P('view', 'tile'), may hold values from 0 to 32767, as said below
- depth_order: int32 [8, 128, 256], P('view', 'tile'), may hold values from 0 to 255, each once within a row
- live_count: int32 [8, 128], P('view', 'tile'), may hold values from 1 to 256, as said below
Outputs:
- rendered: float32 [8, 128, 3, 256], P('view', 'tile')
- grad_centres: float32 [3, 32768], P(None, ('view', 'tile'))
- grad_shape: float32 [6, 32768], P(None, ('view', 'tile'))
- grad_opacity: float32 [32768], P(('view', 'tile'))
- grad_colours: float32 [3, 32768], P(None, ('view', 'tile'))
- next_owner: int32 [8, 128], P('view', 'tile')
The draws below stay inside these ranges and needn't reach their ends.
Inputs may be any that keep to these rules, and one draw needn't show every extreme that they name: `intersection_ids`: gaussian g is held by device g div 1024, devices counted along view+tile. Among the 2 x 16 x 256 slots held by one device at most 512 name Gaussians of any one device, and in every draw some device is named exactly 512 times by the slots of every device. `depth_order`: each tile's entries are a permutation of the slot numbers. Slot s of tile (v, t) is live when s < live_count[v, t]; every view has a tile with all 256 slots live.
All inputs are finite; a program needn't handle non-finite values.
Results may differ from the reference program's by a relative error of at most 0.0003.
Values sent between devices are 32-bit elements; how exact they have to be, the bound alone decides.
No kernel may reach another device: no remote copies, remote signals or barrier semaphores. Data moves between devices by JAX's collectives and lax.ppermute only.
A program may use at most 128 MiB of HBM per device.

```python
import math
import jax
import jax.numpy as jnp
from jax import lax

SIDE = 16
PIX = 256
K = 256
VG = 2
TILE_DEV = 16
G_DEV = 1024
VIEWS = 8
TILES = 128
G = 32768
CAP = 512
N_VIEW = 4
N_TILE = 8


def draw_intersection_ids(key, part):
    devices = N_VIEW * N_TILE
    slots_here = VG * TILE_DEV * K
    tiles_local = VG * TILE_DEV
    front_count = devices // 4
    front_slots = front_count * CAP
    back_slots = slots_here - front_slots
    key_hot, key_pool, key_local = jax.random.split(jax.random.fold_in(key, 17), 3)
    hottest = jax.random.randint(key_hot, (), 0, devices).astype(jnp.int32)

    def requester_owners(pair_key):
        first_key, second_key, third_key = jax.random.split(pair_key, 3)
        shuffled = jax.random.permutation(first_key, devices - 1).astype(jnp.int32)
        others = ((hottest + 1 + shuffled) % devices).astype(jnp.int32)
        front_owners = jnp.concatenate([hottest[None], others[:front_count - 1]])
        front_owners = jax.random.permutation(second_key, front_owners)
        front_run = front_owners[jnp.arange(front_slots, dtype=jnp.int32) // CAP]
        rest = others[front_count - 1:]
        pool_length = rest.shape[0] * CAP
        pool = rest[jnp.arange(pool_length, dtype=jnp.int32) // CAP]
        back_run = jax.random.permutation(third_key, pool)[:back_slots]
        ordered_run = jnp.concatenate([front_run, back_run])
        return jnp.transpose(ordered_run.reshape(K, tiles_local)).reshape(slots_here)
    owners = jax.vmap(requester_owners)(jax.random.split(key_pool, devices))
    local = jax.random.randint(key_local, (devices, slots_here), 0, G_DEV).astype(jnp.int32)
    named = (owners * G_DEV + local).astype(jnp.int32)
    named = named.reshape(N_VIEW, N_TILE, VG, TILE_DEV, K).transpose(0, 2, 1, 3, 4)
    return named.reshape(VG * N_VIEW, TILE_DEV * N_TILE, K)


def draw_live_count(key, part):
    key_base, key_hot = jax.random.split(jax.random.fold_in(key, 29))
    base = jax.random.randint(key_base, (VIEWS, TILES), 0, K).astype(jnp.int32)
    place = jnp.arange(TILES, dtype=jnp.int32)[None, :]
    grown = 1 + base * (TILES + 2 * place) // (3 * TILES)
    hottest = jax.random.randint(key_hot, (VIEWS, 1), 0, TILES).astype(jnp.int32)
    return jnp.where(place == hottest, K, grown).astype(jnp.int32)


def steps_of(rng, shape, pieces, low, high):
    def one(dim, blocks):
        draws = jax.random.uniform(jax.random.fold_in(jax.random.fold_in(rng, 6), dim), (blocks,), jnp.float32, low / len(pieces), high / len(pieces))
        return jnp.repeat(jnp.exp(draws), shape[dim] // blocks).reshape((-1,) + (1,) * (len(shape) - dim - 1))

    level = one(*pieces[0])
    for cut in pieces[1:]:
        level = level * one(*cut)
    return level


def centred(rng, dims, spread, bound, cuts=(), kind=jnp.bfloat16):
    array = spread * jax.random.normal(rng, dims, jnp.float32)
    if cuts:
        array = array * steps_of(rng, dims, cuts, -0.22, 0.18)
    return jnp.clip(array, -bound, bound).astype(kind)


def setup_inputs(seed: int = 0) -> dict:
    streams_of = jax.random.split(jax.random.key(seed), 10)
    return {
        "centres": centred(streams_of[0], (3, G), 1.0, 6.0, ((1, 32),), jnp.float32),
        "shape_raw": jnp.clip(-1.0 + 1.2 * jax.random.uniform(streams_of[1], (6, G), jnp.float32) ** steps_of(streams_of[1], (6, G), ((1, 32),), -0.2, 0.2), -1.0, 0.2),
        "opacity_logit": jnp.clip(-6.0 + 5.0 * jax.random.uniform(streams_of[2], (G,), jnp.float32) ** steps_of(streams_of[2], (G,), ((0, 32),), -0.2, 0.2), -6.0, -1.0),
        "colours": centred(streams_of[3], (3, G), 1.0, 6.0, ((1, 32),), jnp.float32),
        "camera": centred(streams_of[4], (VIEWS, 2, 4), 3.0, 15.0, (), jnp.float32),
        "target": centred(streams_of[5], (VIEWS, TILES, 3, PIX), 0.5, 3.0, ((0, 4), (1, 8)), jnp.float32),
        "intersection_ids": draw_intersection_ids(jax.random.fold_in(streams_of[9], 71), 0),
        "depth_order": jax.vmap(lambda own: jax.random.permutation(own, K))(jax.random.split(streams_of[7], VIEWS * TILES)).reshape((VIEWS, TILES, K)).astype(jnp.int32),
        "live_count": draw_live_count(jax.random.fold_in(streams_of[9], 71), 0),
    }


exact_mode = lax.Precision.HIGHEST

def lower_factor(shape_raw):
    empty_cells = jnp.zeros_like(shape_raw[0])
    first_row = jnp.stack([jnp.exp(shape_raw[0]), empty_cells, empty_cells])
    second_row = jnp.stack([shape_raw[1], jnp.exp(shape_raw[2]), empty_cells])
    third_row = jnp.stack([shape_raw[3], shape_raw[4], jnp.exp(shape_raw[5])])
    return jnp.stack([first_row, second_row, third_row])

def project(centres, shape_raw, opacity_logit, colours, camera):
    view_count = camera.shape[0]
    gaussians = centres.shape[1]
    linear = camera[:, :, 0:3]
    screen = jnp.einsum('vij,jg->vig', linear, centres, precision=exact_mode) + camera[:, :, 3][:, :, None]
    factor = jnp.einsum('vik,kjg->vijg', linear, lower_factor(shape_raw), precision=exact_mode)
    var_x = lax.optimization_barrier(jnp.sum(factor[:, 0] * factor[:, 0], axis=1)) + 0.3
    cov_xy = lax.optimization_barrier(jnp.sum(factor[:, 0] * factor[:, 1], axis=1))
    var_y = lax.optimization_barrier(jnp.sum(factor[:, 1] * factor[:, 1], axis=1)) + 0.3
    determinant = var_x * var_y - cov_xy * cov_xy
    opacity = 0.95 / (1.0 + jnp.exp(-opacity_logit))
    fields = [screen[:, 0], screen[:, 1], var_y / determinant, -cov_xy / determinant, var_x / determinant, jnp.broadcast_to(opacity, (view_count, gaussians))]
    for channel in range(3):
        fields.append(jnp.broadcast_to(colours[channel], (view_count, gaussians)))
    return jnp.stack(fields)

def pixel_offsets():
    pixel_index = jnp.arange(SIDE * SIDE, dtype=jnp.int32)
    across = (pixel_index % SIDE).astype(jnp.float32) - (SIDE - 1) / 2.0
    downward = (pixel_index // SIDE).astype(jnp.float32) - (SIDE - 1) / 2.0
    return (across, downward)

def render_tile(slot_rec, order, live_count):
    ordered = jnp.take(slot_rec, order, axis=1)
    active_slots = (order < live_count).astype(jnp.float32)
    across, downward = pixel_offsets()
    delta_x = across[:, None] - ordered[0][None, :]
    delta_y = downward[:, None] - ordered[1][None, :]
    radius = ordered[2] * delta_x * delta_x + 2.0 * ordered[3] * delta_x * delta_y + ordered[4] * delta_y * delta_y
    coverage = active_slots * ordered[5] * jnp.exp(-0.5 * radius)
    keep_log = jnp.log1p(-coverage)
    slot_count = order.shape[0]
    earlier = (lax.broadcasted_iota(jnp.int32, (slot_count, slot_count), 0) < lax.broadcasted_iota(jnp.int32, (slot_count, slot_count), 1)).astype(jnp.float32)
    through = jnp.exp(jnp.dot(keep_log, earlier, precision=exact_mode))
    weights = through * coverage
    return jnp.einsum('ck,pk->cp', ordered[6:9], weights, precision=exact_mode)

def render_block(slot_rec, order, live_count):
    return jax.vmap(render_tile)(slot_rec, order, live_count)

def render_all(slot_rec, order, live_count):
    lead_count, tile_count, slot_count = order.shape
    total_tiles = lead_count * tile_count
    block_size = math.gcd(total_tiles, 8)
    records = jnp.moveaxis(slot_rec, 0, 2).reshape(total_tiles // block_size, block_size, 9, slot_count)
    orders = order.reshape(total_tiles // block_size, block_size, slot_count)
    counts = live_count.reshape(total_tiles // block_size, block_size)
    blocked = jax.checkpoint(render_block)

    def one_block(packed):
        return blocked(packed[0], packed[1], packed[2])
    images = lax.map(one_block, (records, orders, counts))
    return images.reshape(lead_count, tile_count, 3, SIDE * SIDE)

def reference(centres, shape_raw, opacity_logit, colours, camera, target, intersection_ids, depth_order, live_count):

    def forward(centres, shape_raw, opacity_logit, colours):
        records = project(centres, shape_raw, opacity_logit, colours, camera)
        view_index = lax.broadcasted_iota(jnp.int32, intersection_ids.shape, 0)
        slot_rec = records[:, view_index, intersection_ids]
        return render_all(slot_rec, depth_order, live_count)
    rendered, pullback = jax.vjp(forward, centres, shape_raw, opacity_logit, colours)
    gradients = pullback(rendered - target)
    starts = (jnp.cumsum(live_count, axis=1) - live_count).astype(jnp.int32)
    totals = lax.optimization_barrier(jnp.sum(live_count, axis=1, keepdims=True)).astype(jnp.int32)
    next_owner = (starts * N_TILE // totals).astype(jnp.int32)
    return (rendered, gradients[0], gradients[1], gradients[2], gradients[3], next_owner)
```

```python
from functools import partial
import math

import jax
import jax.numpy as jnp
import numpy as np
from jax import lax
from jax.experimental import pallas as pl
from jax.experimental.pallas import tpu as pltpu
from jax.sharding import PartitionSpec as P

F32 = jnp.float32
BF16 = jnp.bfloat16
FIELDS = 13
GROUPS = 8
ACCS = 4
OFF = -1e4


def log2_of(n):
    bits = n.bit_length() - 1
    assert n == 1 << bits
    return bits


def pieces_of(value, count):
    out = []
    rest = value
    for _ in range(count - 1):
        piece = rest.astype(BF16).astype(F32)
        out.append(piece)
        rest = rest - piece
    out.append(rest)
    return out


def dot_nn(a, b):
    return lax.dot_general(a, b, (((1,), (0,)), ((), ())), preferred_element_type=F32)


def dot_nt(a, b):
    return lax.dot_general(a, b, (((1,), (1,)), ((), ())), preferred_element_type=F32)


def dot_tn(a, b):
    return lax.dot_general(a, b, (((0,), (0,)), ((), ())), preferred_element_type=F32)


def chunk_rows(live):
    return 2 * ((live + 15) >> 4)


def prep_kernel(dims, me_ref, ids_ref, order_ref, live_ref, row_ref, group_ref, piece_ref, rho_ref, code_ref, lhs_ref):
    own_bits, lane_bits, view_bits, tile_bits = dims
    tiles, slots = ids_ref.shape
    me = me_ref[0]
    live = live_ref[...]
    order = order_ref[...]
    active = order < live
    upper = (
        lax.broadcasted_iota(jnp.int32, (slots, slots), 0)
        < lax.broadcasted_iota(jnp.int32, (slots, slots), 1)
    ).astype(F32).astype(BF16)
    place = dot_nn(active.astype(F32).astype(BF16), upper).astype(jnp.int32)
    rows = jnp.broadcast_to(chunk_rows(live), (tiles, slots))
    chunk = jnp.zeros((tiles, slots), jnp.int32)
    for m in range(1, GROUPS):
        chunk = chunk + (place >= m * rows).astype(jnp.int32)
    rho_ref[...] = jnp.where(active, (place - chunk * rows) * GROUPS + chunk, -1)
    ids = ids_ref[...]
    owner = (ids >> own_bits) ^ me
    local = ids & ((1 << own_bits) - 1)
    xy_bits = tile_bits - 1
    core = owner & 1
    chip = (owner >> 1) & ((1 << xy_bits) - 1)
    view = owner >> tile_bits
    block = (((core << xy_bits) | chip) << view_bits) | view
    row = (block << lane_bits) | (local & ((1 << lane_bits) - 1))
    code = (row << 3) | (local >> lane_bits)
    piece_ref[0] = (code & 255).astype(F32)
    piece_ref[1] = ((code >> 8) & 255).astype(F32)
    piece_ref[2] = (code >> 16).astype(F32)
    lhs_ref[...] = jnp.zeros_like(lhs_ref)
    down = lax.broadcasted_iota(jnp.int32, (slots, slots), 0)

    def one_tile(t, _):
        for p in range(3):
            lhs_ref[p : p + 1, :] = piece_ref[p, pl.ds(t, 1), :]
        picked = (down == order_ref[pl.ds(t, 1), :]).astype(F32).astype(BF16)
        ordered = dot_nn(lhs_ref[...].astype(BF16), picked)
        placed = (down == rho_ref[pl.ds(t, 1), :]).astype(F32).astype(BF16)
        out = dot_nt(ordered.astype(BF16), placed)
        code_ref[pl.ds(t, 1), :] = out[0:1] + 256.0 * out[1:2] + 65536.0 * out[2:3]
        return 0

    lax.fori_loop(0, tiles, one_tile, 0)
    codes = code_ref[...].astype(jnp.int32)
    row_ref[...] = codes >> 3
    group_ref[...] = codes & 7


def splat_kernel(
    dims,
    cam_ref,
    row_ref,
    live_ref,
    group_ref,
    live_col_ref,
    mine_ref,
    other_ref,
    target_ref,
    mono_ref,
    image_ref,
    grad_mine_ref,
    grad_other_ref,
    *scratch,
):
    views, tiles_view, slots, pixels, lanes = dims
    table, buf, raw, rec, mom, grad, e_s, c_s, p_s, w_hi, w_lo, g_1, g_2, g_3, row_s, row_2 = scratch[:16]
    accs = scratch[16:]
    tiles = views * tiles_view
    half = mine_ref.shape[0]
    used = FIELDS * GROUPS
    pad = jnp.zeros((lanes - used, lanes), F32)

    for acc in accs:
        acc[...] = jnp.zeros_like(acc)
    for ref in (buf, e_s, c_s, p_s, w_hi, w_lo, g_1, g_2, g_3, row_s, row_2):
        ref[...] = jnp.zeros_like(ref)

    def build(d, _):
        for base, ref in ((0, mine_ref), (half, other_ref)):
            block = jnp.concatenate([ref[d], pad], axis=0)
            start = pl.multiple_of((base + d) * lanes, lanes)
            table[pl.ds(start, lanes), :] = jnp.transpose(block)
        return 0

    lax.fori_loop(0, half, build, 0)

    sub = lax.broadcasted_iota(jnp.int32, (GROUPS, slots), 0)

    def fetch(t, _):
        rows = chunk_rows(live_ref[t])

        def copy(i, _):
            for k in range(GROUPS):
                buf[pl.ds(i * GROUPS + k, 1), :] = table[pl.ds(row_ref[t, i * GROUPS + k], 1), :]
            return 0

        lax.fori_loop(0, rows, copy, 0)
        turned = jnp.transpose(buf[...])
        mine = sub == group_ref[pl.ds(t, 1), :]
        for f in range(FIELDS):
            part = jnp.where(mine, turned[f * GROUPS : (f + 1) * GROUPS], 0.0)
            raw[f, pl.ds(t, 1), :] = jnp.sum(part, axis=0, keepdims=True)
        return 0

    lax.fori_loop(0, tiles, fetch, 0)

    pos = lax.broadcasted_iota(jnp.int32, (tiles_view, slots), 1)

    def project(v):
        block = slice(v * tiles_view, (v + 1) * tiles_view)
        cam = [cam_ref[v * 8 + n] for n in range(8)]
        field = lambda f: raw[f, block, :]
        u = cam[0] * field(0) + cam[1] * field(1) + cam[2] * field(2) + cam[3]
        w = cam[4] * field(0) + cam[5] * field(1) + cam[6] * field(2) + cam[7]
        d0, d1, d2 = jnp.exp(field(3)), jnp.exp(field(5)), jnp.exp(field(8))
        factor = []
        for i in range(2):
            m = cam[4 * i : 4 * i + 3]
            factor.append(
                (
                    m[0] * d0 + m[1] * field(4) + m[2] * field(6),
                    m[1] * d1 + m[2] * field(7),
                    m[2] * d2,
                )
            )
        f0, f1 = factor
        s00 = f0[0] * f0[0] + f0[1] * f0[1] + f0[2] * f0[2] + 0.3
        s01 = f0[0] * f1[0] + f0[1] * f1[1] + f0[2] * f1[2]
        s11 = f1[0] * f1[0] + f1[1] * f1[1] + f1[2] * f1[2] + 0.3
        inverse = 1.0 / (s00 * s11 - s01 * s01)
        conic = (s11 * inverse, -s01 * inverse, s00 * inverse)
        return cam, block, u, w, (d0, d1, d2), f0, f1, conic

    for v in range(views):
        cam, block, u, w, _, _, _, (ka, kb, kc) = project(v)
        live = live_col_ref[block, :]
        rows = jnp.broadcast_to(chunk_rows(live), pos.shape)
        here = (pos >> 3 < rows) & ((pos & 7) * rows + (pos >> 3) < live)
        x_line = ka * u + kb * w
        y_line = kb * u + kc * w
        log_opacity = math.log(0.95) - jnp.log(1.0 + jnp.exp(-raw[9, block, :]))
        level = log_opacity - 0.5 * (u * x_line + w * y_line)
        terms = (-0.5 * ka, -kb, -0.5 * kc, x_line, y_line)
        for n, term in enumerate(terms):
            rec[n, block, :] = jnp.where(here, term, 0.0)
        rec[5, block, :] = jnp.where(here, level, OFF)
        for c in range(3):
            rec[6 + c, block, :] = jnp.where(here, raw[10 + c, block, :], 0.0)

    lane_row = lax.broadcasted_iota(jnp.int32, (GROUPS, pixels), 0)
    zero_rows = jnp.zeros((8, slots), F32)
    zero_pix = jnp.zeros((8, pixels), F32)

    def render(t, _):
        pairs = chunk_rows(live_ref[t]) >> 1
        for n in range(6):
            row_s[n : n + 1, :] = rec[n, pl.ds(t, 1), :]
        for c in range(3):
            row_s[8 + c : 9 + c, :] = rec[6 + c, pl.ds(t, 1), :]
        coef = pieces_of(row_s[0:8, :], 3)
        lhs = jnp.concatenate(coef + [zero_rows], axis=0).astype(BF16)
        e_s[...] = dot_tn(lhs, mono_ref[...])
        colour = pieces_of(row_s[8:16, :], 3)

        def through(i, prod):
            start = pl.multiple_of(i * 16, 16)
            for h in range(2):
                rows = pl.ds(start + 8 * h, 8)
                cover = jnp.exp(e_s[rows, :])
                c_s[rows, :] = cover
                p_s[rows, :] = prod
                prod = prod * (1.0 - cover)
            return prod

        whole = lax.fori_loop(0, pairs, through, jnp.ones((GROUPS, pixels), F32))
        before = whole
        for step in (1, 2, 4):
            before = before * jnp.where(lane_row >= step, pltpu.roll(before, step, 0), 1.0)
        before = jnp.where(lane_row >= 1, pltpu.roll(before, 1, 0), 1.0)

        def weigh(i, _):
            start = pl.multiple_of(i * 16, 16)
            both = pl.ds(start, 16)
            lead = jnp.concatenate([before, before], axis=0)
            weight = p_s[both, :] * lead * c_s[both, :]
            p_s[both, :] = weight
            high = weight.astype(BF16)
            w_hi[both, :] = high
            w_lo[both, :] = (weight - high.astype(F32)).astype(BF16)
            return 0

        lax.fori_loop(0, pairs, weigh, 0)
        col_lhs = jnp.concatenate(colour + [zero_rows], axis=0).astype(BF16)
        image = dot_nn(col_lhs, w_hi[...]) + dot_nn(col_lhs, w_lo[...])
        image = image[0:8] + image[8:16] + image[16:24]
        image_ref[t] = image[0:3]
        row_2[0:3, :] = image[0:3] - target_ref[t]
        miss = pieces_of(row_2[0:8, :], 3)
        lhs = jnp.concatenate(
            [colour[0], colour[0], colour[1], colour[0], colour[1], colour[2]] + [zero_rows] * 2, axis=0
        ).astype(BF16)
        rhs = jnp.concatenate(
            [miss[0], miss[1], miss[0], miss[2], miss[1], miss[0]] + [zero_pix] * 2, axis=0
        ).astype(BF16)
        e_s[...] = dot_tn(lhs, rhs)

        def pull(i, total):
            start = pl.multiple_of(i * 16, 16)
            for h in range(2):
                rows = pl.ds(start + 8 * h, 8)
                part = p_s[rows, :] * e_s[rows, :]
                total = total + part
                cover = c_s[rows, :]
                ratio = cover / (1.0 - cover)
                c_s[rows, :] = ratio
                e_s[rows, :] = part + ratio * total
            return total

        whole = lax.fori_loop(0, pairs, pull, jnp.zeros((GROUPS, pixels), F32))
        after = whole
        for step in (1, 2, 4):
            after = after + jnp.where(lane_row < GROUPS - step, pltpu.roll(after, GROUPS - step, 0), 0.0)

        def settle(i, _):
            start = pl.multiple_of(i * 16, 16)
            both = pl.ds(start, 16)
            tail = jnp.concatenate([after, after], axis=0)
            slope = e_s[both, :] - c_s[both, :] * tail
            high = slope.astype(BF16)
            rest = slope - high.astype(F32)
            middle = rest.astype(BF16)
            g_1[both, :] = high
            g_2[both, :] = middle
            g_3[both, :] = (rest - middle.astype(F32)).astype(BF16)
            return 0

        lax.fori_loop(0, pairs, settle, 0)
        mono = mono_ref[0:16, :]
        moments = dot_nt(mono, g_1[...]) + dot_nt(mono, g_2[...]) + dot_nt(mono, g_3[...])
        miss_lhs = jnp.concatenate(miss + [zero_pix], axis=0).astype(BF16)
        tint = dot_nt(miss_lhs, w_hi[...]) + dot_nt(miss_lhs, w_lo[...])
        row_s[0:8, :] = moments[0:8]
        row_s[8:16, :] = tint[0:8] + tint[8:16] + tint[16:24]
        for n in range(6):
            mom[n, pl.ds(t, 1), :] = row_s[n : n + 1, :]
        for c in range(3):
            mom[6 + c, pl.ds(t, 1), :] = row_s[8 + c : 9 + c, :]
        return 0

    lax.fori_loop(0, tiles, render, 0)

    for v in range(views):
        cam, block, u, w, (d0, d1, d2), f0, f1, (ka, kb, kc) = project(v)
        live = live_col_ref[block, :]
        rows = jnp.broadcast_to(chunk_rows(live), pos.shape)
        here = (pos >> 3 < rows) & ((pos & 7) * rows + (pos >> 3) < live)
        mxx, mxy, myy, mx, my, m1 = [jnp.where(here, mom[n, block, :], 0.0) for n in range(6)]
        dx = mx - u * m1
        dy = my - w * m1
        dxx = mxx - 2.0 * u * mx + u * u * m1
        dxy = mxy - u * my - w * mx + u * w * m1
        dyy = myy - 2.0 * w * my + w * w * m1
        gu = ka * dx + kb * dy
        gw = kb * dx + kc * dy
        ax, ay = ka * dxx + kb * dxy, ka * dxy + kb * dyy
        bx, by = kb * dxx + kc * dxy, kb * dxy + kc * dyy
        h00 = ax * ka + ay * kb
        h01 = ax * kb + ay * kc
        h11 = bx * kb + by * kc
        g0 = [h00 * f0[j] + h01 * f1[j] for j in range(3)]
        g1 = [h01 * f0[j] + h11 * f1[j] for j in range(3)]
        for k in range(3):
            grad[k, block, :] = cam[k] * gu + cam[4 + k] * gw
        grad[3, block, :] = (cam[0] * g0[0] + cam[4] * g1[0]) * d0
        grad[4, block, :] = cam[1] * g0[0] + cam[5] * g1[0]
        grad[5, block, :] = (cam[1] * g0[1] + cam[5] * g1[1]) * d1
        grad[6, block, :] = cam[2] * g0[0] + cam[6] * g1[0]
        grad[7, block, :] = cam[2] * g0[1] + cam[6] * g1[1]
        grad[8, block, :] = (cam[2] * g0[2] + cam[6] * g1[2]) * d2
        grad[9, block, :] = m1 - m1 / (1.0 + jnp.exp(-raw[9, block, :]))
        for c in range(3):
            grad[10 + c, block, :] = jnp.where(here, mom[6 + c, block, :], 0.0)

    def give(t, _):
        mine = sub == group_ref[pl.ds(t, 1), :]
        spread = [
            jnp.where(mine, jnp.broadcast_to(grad[f, pl.ds(t, 1), :], (GROUPS, slots)), 0.0)
            for f in range(FIELDS)
        ]
        spread.append(jnp.zeros((lanes - used, slots), F32))
        buf[...] = jnp.transpose(jnp.concatenate(spread, axis=0))
        rows = chunk_rows(live_ref[t])

        def add(i, _):
            for k in range(0, GROUPS, len(accs)):
                where = [row_ref[t, i * GROUPS + k + n] for n in range(len(accs))]
                olds = [accs[n][pl.ds(where[n], 1), :] for n in range(len(accs))]
                news = [buf[pl.ds(i * GROUPS + k + n, 1), :] for n in range(len(accs))]
                for n in range(len(accs)):
                    accs[n][pl.ds(where[n], 1), :] = olds[n] + news[n]
            return 0

        lax.fori_loop(0, rows, add, 0)
        return 0

    lax.fori_loop(0, tiles, give, 0)

    def finish(d, _):
        for base, ref in ((0, grad_mine_ref), (half, grad_other_ref)):
            start = pl.multiple_of((base + d) * lanes, lanes)
            total = accs[0][pl.ds(start, lanes), :]
            for acc in accs[1:]:
                total = total + acc[pl.ds(start, lanes), :]
            ref[d] = jnp.transpose(total)[0:used]
        return 0

    lax.fori_loop(0, half, finish, 0)


def monomials(pixels):
    side = math.isqrt(pixels)
    index = np.arange(pixels)
    x = (index % side) - (side - 1) / 2.0
    y = (index // side) - (side - 1) / 2.0
    one = np.ones_like(x)
    zero = np.zeros_like(x)
    group = np.stack([x * x, x * y, y * y, x, y, one, zero, zero])
    return jnp.asarray(np.concatenate([group, group, group, np.zeros_like(group)]), BF16)


def swap(array, axis, mask):
    size = lax.axis_size(axis)
    return lax.ppermute(array, axis, [(i, i ^ mask) for i in range(size)])


def shards(centres, shape_raw, opacity_logit, colours, camera, target, intersection_ids, depth_order, live_count):
    view_group = lax.axis_size("view")
    tile_group = lax.axis_size("tile")
    devices = view_group * tile_group
    chips = tile_group // 2
    own_count = centres.shape[1]
    lanes = own_count // GROUPS
    views, tiles_view, slots = intersection_ids.shape
    tiles = views * tiles_view
    pixels = target.shape[3]
    view_index = lax.axis_index("view")
    tile_index = lax.axis_index("tile")
    me = (view_index * tile_group + tile_index).astype(jnp.int32)

    totals = jnp.sum(live_count, axis=1)
    within = jnp.cumsum(live_count, axis=1) - live_count
    before = jnp.zeros_like(totals)
    whole = totals
    for mask in range(1, tile_group):
        theirs = swap(totals, "tile", mask)
        whole = whole + theirs
        before = before + jnp.where((tile_index ^ mask) < tile_index, theirs, 0)
    next_owner = (before[:, None] + within) * tile_group // whole[:, None]

    fields = jnp.concatenate([centres, shape_raw, opacity_logit[None], colours], axis=0)
    block = fields.reshape(FIELDS * GROUPS, lanes)
    column = jnp.stack([block] + [swap(block, "view", m) for m in range(1, view_group)])
    mine = jnp.stack([column] + [swap(column, "tile", 2 * m) for m in range(1, chips)])
    mine = mine.reshape(chips * view_group, FIELDS * GROUPS, lanes)
    other = swap(mine, "tile", 1)

    flat_live = live_count.reshape(tiles)
    prep = pl.pallas_call(
        partial(
            prep_kernel,
            (log2_of(own_count), log2_of(lanes), log2_of(view_group), log2_of(tile_group)),
        ),
        out_shape=[jax.ShapeDtypeStruct((tiles, slots), jnp.int32)] * 2,
        in_specs=[pl.BlockSpec(memory_space=pltpu.SMEM)] + [pl.BlockSpec(memory_space=pltpu.VMEM)] * 3,
        out_specs=[pl.BlockSpec(memory_space=pltpu.VMEM)] * 2,
        scratch_shapes=[
            pltpu.VMEM((3, tiles, slots), F32),
            pltpu.VMEM((tiles, slots), jnp.int32),
            pltpu.VMEM((tiles, slots), F32),
            pltpu.VMEM((16, slots), F32),
        ],
        cost_estimate=pl.CostEstimate(flops=20_000_000_000, bytes_accessed=4 * tiles * slots * 4, transcendentals=0),
        name="prep",
    )
    rows, group = prep(
        me[None],
        intersection_ids.reshape(tiles, slots),
        depth_order.reshape(tiles, slots),
        flat_live[:, None],
    )

    cam = lax.dynamic_slice_in_dim(camera, view_index * views, views, 0).reshape(views * 8)
    smem = pl.BlockSpec(memory_space=pltpu.SMEM)
    vmem = pl.BlockSpec(memory_space=pltpu.VMEM)
    table_rows = devices * lanes
    square = (slots, pixels)
    splat = pl.pallas_call(
        partial(splat_kernel, (views, tiles_view, slots, pixels, lanes)),
        out_shape=[
            jax.ShapeDtypeStruct((tiles, 3, pixels), F32),
            jax.ShapeDtypeStruct(mine.shape, F32),
            jax.ShapeDtypeStruct(mine.shape, F32),
        ],
        in_specs=[smem] * 3 + [vmem] * 6,
        out_specs=[vmem] * 3,
        scratch_shapes=[
            pltpu.VMEM((table_rows, lanes), F32),
            pltpu.VMEM((slots, lanes), F32),
            pltpu.VMEM((FIELDS, tiles, slots), F32),
            pltpu.VMEM((9, tiles, slots), F32),
            pltpu.VMEM((9, tiles, slots), F32),
            pltpu.VMEM((FIELDS, tiles, slots), F32),
            pltpu.VMEM(square, F32),
            pltpu.VMEM(square, F32),
            pltpu.VMEM(square, F32),
        ]
        + [pltpu.VMEM(square, BF16)] * 5
        + [pltpu.VMEM((16, slots), F32), pltpu.VMEM((8, pixels), F32)]
        + [pltpu.VMEM((table_rows, lanes), F32)] * (ACCS if devices <= 32 else 2),
        compiler_params=pltpu.CompilerParams(vmem_limit_bytes=60 * 1024 * 1024),
        name="splat",
    )
    rendered, grad_mine, grad_other = splat(
        cam,
        rows,
        flat_live,
        group,
        flat_live[:, None],
        mine,
        other,
        target.reshape(tiles, 3, pixels),
        monomials(pixels),
    )

    joined = grad_mine + swap(grad_other, "tile", 1)
    joined = joined.reshape(chips, view_group, FIELDS * GROUPS, lanes)
    part = joined[0]
    for m in range(1, chips):
        part = part + swap(joined[m], "tile", 2 * m)
    summed = part[0]
    for m in range(1, view_group):
        summed = summed + swap(part[m], "view", m)
    summed = summed.reshape(FIELDS, own_count)
    return (
        rendered.reshape(views, tiles_view, 3, pixels),
        summed[0:3],
        summed[3:9],
        summed[9],
        summed[10:13],
        next_owner,
    )


def solution(mesh):
    in_specs = (
        P(None, ("view", "tile")),
        P(None, ("view", "tile")),
        P(("view", "tile")),
        P(None, ("view", "tile")),
        P(),
        P("view", "tile", None, None),
        P("view", "tile", None),
        P("view", "tile", None),
        P("view", "tile"),
    )
    out_specs = (
        P("view", "tile", None, None),
        P(None, ("view", "tile")),
        P(None, ("view", "tile")),
        P(("view", "tile")),
        P(None, ("view", "tile")),
        P("view", "tile"),
    )
    return jax.shard_map(shards, mesh=mesh, in_specs=in_specs, out_specs=out_specs, check_vma=False)
```

```python
from functools import partial
import math

import jax
import jax.numpy as jnp
import numpy as np
from jax import lax
from jax.experimental import pallas as pl
from jax.experimental.pallas import tpu as pltpu
from jax.sharding import PartitionSpec as P

F32 = jnp.float32
BF16 = jnp.bfloat16
FIELDS = 13
GROUPS = 8
ACCS = 4
UNROLL = 4
BATCH = 2
LOG2E = math.log2(math.e)
OFF = -1e4


def log2_of(n):
    bits = n.bit_length() - 1
    assert n == 1 << bits
    return bits


def pieces_of(value, count):
    out = []
    rest = value
    for _ in range(count - 1):
        piece = rest.astype(BF16).astype(F32)
        out.append(piece)
        rest = rest - piece
    out.append(rest)
    return out


def dot_nn(a, b):
    return lax.dot_general(a, b, (((1,), (0,)), ((), ())), preferred_element_type=F32)


def dot_nt(a, b):
    return lax.dot_general(a, b, (((1,), (1,)), ((), ())), preferred_element_type=F32)


def dot_tn(a, b):
    return lax.dot_general(a, b, (((0,), (0,)), ((), ())), preferred_element_type=F32)


def chunk_rows(live):
    return (live + 7) >> 3


def repeat(count, step, body):
    many = lax.div(count, step)

    def trip(i, _):
        for u in range(step):
            body(i * step + u)
        return 0

    def single(i, _):
        body(i)
        return 0

    lax.fori_loop(0, many, trip, 0)
    lax.fori_loop(many * step, count, single, 0)


def prep_kernel(
    dims,
    me_ref,
    live_ref,
    camera_ref,
    ids_ref,
    order_ref,
    row_ref,
    group_ref,
    cam_ref,
    piece_ref,
    rho_ref,
    code_ref,
    lhs_ref,
    live_full,
    order_b,
):
    own_bits, lane_bits, view_bits, tile_bits, tiles_view = dims
    tiles, slots = ids_ref.shape
    me = me_ref[0]
    views = tiles // tiles_view
    first = (me >> tile_bits) * views
    for v in range(views):
        for i in range(2):
            for j in range(4):
                cam_ref[v * 8 + i * 4 + j] = camera_ref[first + v, i, j]
    for t in range(tiles):
        live_full[t : t + 1, :] = jnp.full((1, slots), live_ref[t // tiles_view, t % tiles_view], jnp.int32)
    live = live_full[...]
    order = order_ref[...]
    active = order < live
    upper = (
        lax.broadcasted_iota(jnp.int32, (slots, slots), 0)
        < lax.broadcasted_iota(jnp.int32, (slots, slots), 1)
    ).astype(F32).astype(BF16)
    place = dot_nn(active.astype(F32).astype(BF16), upper).astype(jnp.int32)
    rows = chunk_rows(live)
    chunk = jnp.zeros((tiles, slots), jnp.int32)
    for m in range(1, GROUPS):
        chunk = chunk + (place >= m * rows).astype(jnp.int32)
    rho_ref[...] = jnp.where(active, (place - chunk * rows) * GROUPS + chunk, -1).astype(F32)
    order_b[...] = order.astype(F32)
    ids = ids_ref[...]
    owner = (ids >> own_bits) ^ me
    local = ids & ((1 << own_bits) - 1)
    xy_bits = tile_bits - 1
    core = owner & 1
    chip = (owner >> 1) & ((1 << xy_bits) - 1)
    view = owner >> tile_bits
    block = (((core << xy_bits) | chip) << view_bits) | view
    row = (block << lane_bits) | (local & ((1 << lane_bits) - 1))
    code = (row << 3) | (local >> lane_bits)
    piece_ref[0] = (code & 255).astype(F32)
    piece_ref[1] = ((code >> 8) & 255).astype(F32)
    piece_ref[2] = (code >> 16).astype(F32)
    lhs_ref[...] = jnp.zeros_like(lhs_ref)
    down = lax.broadcasted_iota(jnp.int32, (slots, slots), 0).astype(F32).astype(BF16)
    one = jnp.ones((slots, slots), BF16)
    nil = jnp.zeros((slots, slots), BF16)

    def some_tiles(s, _):
        for u in range(UNROLL):
            t = s * UNROLL + u
            for p in range(3):
                lhs_ref[u, p : p + 1, :] = piece_ref[p, pl.ds(t, 1), :]
            picked = jnp.where(down == order_b[pl.ds(t, 1), :].astype(BF16), one, nil)
            ordered = dot_nn(lhs_ref[u].astype(BF16), picked)
            placed = jnp.where(down == rho_ref[pl.ds(t, 1), :].astype(BF16), one, nil)
            out = dot_nt(ordered.astype(BF16), placed)
            code_ref[pl.ds(t, 1), :] = out[0:1] + 256.0 * out[1:2] + 65536.0 * out[2:3]
        return 0

    lax.fori_loop(0, tiles // UNROLL, some_tiles, 0)
    codes = code_ref[...].astype(jnp.int32)
    row_ref[...] = codes >> 3
    pos = lax.broadcasted_iota(jnp.int32, (tiles, slots), 1)
    here = (pos >> 3 < rows) & ((pos & 7) * rows + (pos >> 3) < live)
    group_ref[...] = jnp.where(here, codes & 7, GROUPS)


def splat_kernel(
    dims,
    cam_ref,
    row_ref,
    live_ref,
    group_ref,
    mine_ref,
    other_ref,
    target_ref,
    mono_ref,
    image_ref,
    grad_mine_ref,
    grad_other_ref,
    *scratch,
):
    views, tiles_view, slots, pixels, lanes, column = dims
    table, buf, raw, rec, mom, grad, c_s, h_s, w_hi, w_lo, g_1, g_2, g_3, row_s, row_2 = scratch[:15]
    accs = scratch[15:]
    tiles = views * tiles_view
    chips = mine_ref.shape[0]
    half = chips * column
    used = FIELDS * GROUPS
    pad = jnp.zeros((lanes - used, lanes), F32)

    for acc in accs:
        acc[...] = jnp.zeros_like(acc)
    for ref in (buf, w_hi, w_lo, g_1, g_2, g_3, row_s, row_2):
        ref[...] = jnp.zeros_like(ref)

    def build(q, _):
        for base, ref in ((0, mine_ref), (half, other_ref)):
            for d in range(column):
                block = jnp.concatenate([ref[q, d * used : (d + 1) * used, :], pad], axis=0)
                start = pl.multiple_of((base + q * column + d) * lanes, lanes)
                table[pl.ds(start, lanes), :] = jnp.transpose(block)
        return 0

    lax.fori_loop(0, chips, build, 0)

    def live_of(t):
        return live_ref[lax.div(t, tiles_view), lax.rem(t, tiles_view)]

    sub = lax.broadcasted_iota(jnp.int32, (GROUPS, slots), 0)

    def fetch(t, _):
        def copy(i):
            for k in range(GROUPS):
                buf[pl.ds(i * GROUPS + k, 1), :] = table[pl.ds(row_ref[t * slots + i * GROUPS + k], 1), :]

        repeat(chunk_rows(live_of(t)), 4, copy)
        turned = jnp.transpose(buf[...])
        mine = sub == group_ref[pl.ds(t, 1), :]
        for f in range(FIELDS):
            part = jnp.where(mine, turned[f * GROUPS : (f + 1) * GROUPS], 0.0)
            raw[f, pl.ds(t, 1), :] = jnp.sum(part, axis=0, keepdims=True)
        return 0

    lax.fori_loop(0, tiles, fetch, 0)

    def project(v):
        block = slice(v * tiles_view, (v + 1) * tiles_view)
        cam = [cam_ref[v * 8 + n] for n in range(8)]
        field = lambda f: raw[f, block, :]
        u = cam[0] * field(0) + cam[1] * field(1) + cam[2] * field(2) + cam[3]
        w = cam[4] * field(0) + cam[5] * field(1) + cam[6] * field(2) + cam[7]
        d0, d1, d2 = jnp.exp(field(3)), jnp.exp(field(5)), jnp.exp(field(8))
        factor = []
        for i in range(2):
            m = cam[4 * i : 4 * i + 3]
            factor.append(
                (
                    m[0] * d0 + m[1] * field(4) + m[2] * field(6),
                    m[1] * d1 + m[2] * field(7),
                    m[2] * d2,
                )
            )
        f0, f1 = factor
        s00 = f0[0] * f0[0] + f0[1] * f0[1] + f0[2] * f0[2] + 0.3
        s01 = f0[0] * f1[0] + f0[1] * f1[1] + f0[2] * f1[2]
        s11 = f1[0] * f1[0] + f1[1] * f1[1] + f1[2] * f1[2] + 0.3
        inverse = 1.0 / (s00 * s11 - s01 * s01)
        conic = (s11 * inverse, -s01 * inverse, s00 * inverse)
        here = group_ref[block, :] < GROUPS
        return here, cam, block, u, w, (d0, d1, d2), f0, f1, conic

    for v in range(views):
        here, cam, block, u, w, _, _, _, (ka, kb, kc) = project(v)
        x_line = ka * u + kb * w
        y_line = kb * u + kc * w
        log_opacity = math.log(0.95) - jnp.log(1.0 + jnp.exp(-raw[9, block, :]))
        level = log_opacity - 0.5 * (u * x_line + w * y_line)
        terms = (-0.5 * ka, -kb, -0.5 * kc, x_line, y_line)
        for n, term in enumerate(terms):
            rec[n, block, :] = jnp.where(here, term * LOG2E, 0.0)
        rec[5, block, :] = jnp.where(here, level * LOG2E, OFF)
        for c in range(3):
            rec[6 + c, block, :] = raw[10 + c, block, :]

    lane_row = lax.broadcasted_iota(jnp.int32, (GROUPS, pixels), 0)
    own_chunk = (lax.broadcasted_iota(jnp.int32, (GROUPS, slots), 1) & 7) == sub
    zero_rows = jnp.zeros((8, slots), F32)
    zero_pix = jnp.zeros((8, pixels), F32)

    def paired(a, b):
        return a + pltpu.roll(b, 3, 0)

    def render(s, _):
        tile = [s * BATCH + g for g in range(BATCH)]
        blocks = [(chunk_rows(live_of(t)) + 3) >> 2 for t in tile]
        for g, t in enumerate(tile):
            for n in range(6):
                row_s[g, n : n + 1, :] = rec[n, pl.ds(t, 1), :]
            for c in range(3):
                row_s[g, 8 + c : 9 + c, :] = rec[6 + c, pl.ds(t, 1), :]
        for g in range(BATCH):
            lhs = jnp.concatenate(pieces_of(row_s[g, 0:8, :], 3) + [zero_rows], axis=0).astype(BF16)
            c_s[g] = dot_tn(lhs, mono_ref[...])
        colour = [pieces_of(row_s[g, 8:16, :], 3) for g in range(BATCH)]

        lead = []
        for g in range(BATCH):

            def through(i, prod, g=g):
                rows = pl.ds(pl.multiple_of(i * 32, 32), 32)
                cover = jnp.exp2(c_s[g, rows, :])
                c_s[g, rows, :] = cover
                keep = 1.0 - cover
                return prod * ((keep[0:8] * keep[8:16]) * (keep[16:24] * keep[24:32]))

            lead.append(lax.fori_loop(0, blocks[g], through, jnp.ones((GROUPS, pixels), F32)))
        for g in range(BATCH):
            scan = lead[g]
            for step in (1, 2, 4):
                scan = scan * jnp.where(lane_row >= step, pltpu.roll(scan, step, 0), 1.0)
            lead[g] = jnp.where(lane_row >= 1, pltpu.roll(scan, 1, 0), 1.0)

        def weights(cover, prod):
            out = []
            for h in range(4):
                weight = prod * cover[8 * h : 8 * h + 8]
                prod = prod - weight
                out.append(weight)
            return out, prod

        for g in range(BATCH):

            def weigh(i, prod, g=g):
                rows = pl.ds(pl.multiple_of(i * 32, 32), 32)
                parts, prod = weights(c_s[g, rows, :], prod)
                weight = jnp.concatenate(parts, axis=0)
                high = weight.astype(BF16)
                w_hi[g, rows, :] = high
                w_lo[g, rows, :] = (weight - high.astype(F32)).astype(BF16)
                return prod

            lax.fori_loop(0, blocks[g], weigh, lead[g])

        after = []
        for g, t in enumerate(tile):
            v, tl = lax.div(t, tiles_view), lax.rem(t, tiles_view)
            spread = [
                jnp.where(own_chunk, jnp.broadcast_to(piece[c : c + 1], (GROUPS, slots)), 0.0)
                for c in range(3)
                for piece in colour[g]
            ]
            lhs = jnp.concatenate(spread + [zero_rows], axis=0).astype(BF16)
            image = dot_nn(lhs, w_hi[g]) + dot_nn(lhs, w_lo[g])
            rest = jnp.zeros((GROUPS, pixels), F32)
            for c in range(3):
                part = image[24 * c : 24 * c + 8] + image[24 * c + 8 : 24 * c + 16] + image[24 * c + 16 : 24 * c + 24]
                whole = jnp.sum(part, axis=0, keepdims=True)
                image_ref[v, c, pl.ds(tl, 1), :] = whole
                miss = whole - target_ref[v, c, pl.ds(tl, 1), :]
                row_2[g, c : c + 1, :] = miss
                rest = rest + part * miss
            for step in (1, 2, 4):
                rest = rest + jnp.where(lane_row < GROUPS - step, pltpu.roll(rest, GROUPS - step, 0), 0.0)
            after.append(rest)
        missed = [pieces_of(row_2[g], 3) for g in range(BATCH)]
        for g in range(BATCH):
            c1, c2, c3 = colour[g]
            m1, m2, m3 = missed[g]
            lhs = jnp.concatenate([paired(c1, c1), paired(c2, c1), paired(c2, c3), zero_rows], axis=0)
            rhs = jnp.concatenate([paired(m1, m2), paired(m1, m3), paired(m2, m1), zero_pix], axis=0)
            h_s[g] = dot_tn(lhs.astype(BF16), rhs.astype(BF16))

        for g in range(BATCH):

            def settle(i, carry, g=g):
                prod, tail = carry
                rows = pl.ds(pl.multiple_of(i * 32, 32), 32)
                cover = c_s[g, rows, :]
                pull = h_s[g, rows, :]
                parts, prod = weights(cover, prod)
                ratio = cover / (1.0 - cover)
                slopes = []
                for h in range(4):
                    cut = slice(8 * h, 8 * h + 8)
                    part = parts[h] * pull[cut]
                    tail = tail - part
                    slopes.append(part - ratio[cut] * tail)
                slope = jnp.concatenate(slopes, axis=0)
                high = slope.astype(BF16)
                rest = slope - high.astype(F32)
                middle = rest.astype(BF16)
                g_1[g, rows, :] = high
                g_2[g, rows, :] = middle
                g_3[g, rows, :] = (rest - middle.astype(F32)).astype(BF16)
                return prod, tail

            lax.fori_loop(0, blocks[g], settle, (lead[g], after[g]))
        mono = mono_ref[0:16, :]
        for g in range(BATCH):
            moments = dot_nt(mono, g_1[g]) + dot_nt(mono, g_2[g]) + dot_nt(mono, g_3[g])
            miss_lhs = jnp.concatenate(missed[g] + [zero_pix], axis=0).astype(BF16)
            tint = dot_nt(miss_lhs, w_hi[g]) + dot_nt(miss_lhs, w_lo[g])
            row_s[g, 0:8, :] = moments[0:8]
            row_s[g, 8:16, :] = tint[0:8] + tint[8:16] + tint[16:24]
        for g, t in enumerate(tile):
            for n in range(6):
                mom[n, pl.ds(t, 1), :] = row_s[g, n : n + 1, :]
            for c in range(3):
                mom[6 + c, pl.ds(t, 1), :] = row_s[g, 8 + c : 9 + c, :]
        return 0

    lax.fori_loop(0, tiles // BATCH, render, 0)

    for v in range(views):
        here, cam, block, u, w, (d0, d1, d2), f0, f1, (ka, kb, kc) = project(v)
        mxx, mxy, myy, mx, my, m1 = [jnp.where(here, mom[n, block, :], 0.0) for n in range(6)]
        dx = mx - u * m1
        dy = my - w * m1
        dxx = mxx - 2.0 * u * mx + u * u * m1
        dxy = mxy - u * my - w * mx + u * w * m1
        dyy = myy - 2.0 * w * my + w * w * m1
        gu = ka * dx + kb * dy
        gw = kb * dx + kc * dy
        ax, ay = ka * dxx + kb * dxy, ka * dxy + kb * dyy
        bx, by = kb * dxx + kc * dxy, kb * dxy + kc * dyy
        h00 = ax * ka + ay * kb
        h01 = ax * kb + ay * kc
        h11 = bx * kb + by * kc
        g0 = [h00 * f0[j] + h01 * f1[j] for j in range(3)]
        g1 = [h01 * f0[j] + h11 * f1[j] for j in range(3)]
        for k in range(3):
            grad[k, block, :] = cam[k] * gu + cam[4 + k] * gw
        grad[3, block, :] = (cam[0] * g0[0] + cam[4] * g1[0]) * d0
        grad[4, block, :] = cam[1] * g0[0] + cam[5] * g1[0]
        grad[5, block, :] = (cam[1] * g0[1] + cam[5] * g1[1]) * d1
        grad[6, block, :] = cam[2] * g0[0] + cam[6] * g1[0]
        grad[7, block, :] = cam[2] * g0[1] + cam[6] * g1[1]
        grad[8, block, :] = (cam[2] * g0[2] + cam[6] * g1[2]) * d2
        grad[9, block, :] = m1 - m1 / (1.0 + jnp.exp(-raw[9, block, :]))
        for c in range(3):
            grad[10 + c, block, :] = mom[6 + c, block, :]

    def give(t, _):
        mine = sub == group_ref[pl.ds(t, 1), :]
        spread = [
            jnp.where(mine, jnp.broadcast_to(grad[f, pl.ds(t, 1), :], (GROUPS, slots)), 0.0)
            for f in range(FIELDS)
        ]
        spread.append(jnp.zeros((lanes - used, slots), F32))
        buf[...] = jnp.transpose(jnp.concatenate(spread, axis=0))

        def add(i):
            for k in range(0, GROUPS, len(accs)):
                where = [row_ref[t * slots + i * GROUPS + k + n] for n in range(len(accs))]
                olds = [accs[n][pl.ds(where[n], 1), :] for n in range(len(accs))]
                news = [buf[pl.ds(i * GROUPS + k + n, 1), :] for n in range(len(accs))]
                for n in range(len(accs)):
                    accs[n][pl.ds(where[n], 1), :] = olds[n] + news[n]

        repeat(chunk_rows(live_of(t)), 4, add)
        return 0

    lax.fori_loop(0, tiles, give, 0)

    def finish(d, _):
        for base, ref in ((0, grad_mine_ref), (half, grad_other_ref)):
            start = pl.multiple_of((base + d) * lanes, lanes)
            total = accs[0][pl.ds(start, lanes), :]
            for acc in accs[1:]:
                total = total + acc[pl.ds(start, lanes), :]
            ref[d] = jnp.transpose(total)[0:used]
        return 0

    lax.fori_loop(0, half, finish, 0)


def monomials(pixels):
    side = math.isqrt(pixels)
    index = np.arange(pixels)
    x = (index % side) - (side - 1) / 2.0
    y = (index // side) - (side - 1) / 2.0
    one = np.ones_like(x)
    zero = np.zeros_like(x)
    group = np.stack([x * x, x * y, y * y, x, y, one, zero, zero])
    return jnp.asarray(np.concatenate([group, group, group, np.zeros_like(group)]), BF16)


def swap(array, axis, mask):
    size = lax.axis_size(axis)
    return lax.ppermute(array, axis, [(i, i ^ mask) for i in range(size)])


def shards(centres, shape_raw, opacity_logit, colours, camera, target, intersection_ids, depth_order, live_count):
    view_group = lax.axis_size("view")
    tile_group = lax.axis_size("tile")
    devices = view_group * tile_group
    chips = tile_group // 2
    own_count = centres.shape[1]
    lanes = own_count // GROUPS
    views, tiles_view, slots = intersection_ids.shape
    tiles = views * tiles_view
    pixels = target.shape[3]
    view_index = lax.axis_index("view")
    tile_index = lax.axis_index("tile")
    me = (view_index * tile_group + tile_index).astype(jnp.int32)

    totals = jnp.sum(live_count, axis=1)
    within = jnp.cumsum(live_count, axis=1) - live_count

    smem = pl.BlockSpec(memory_space=pltpu.SMEM)
    vmem = pl.BlockSpec(memory_space=pltpu.VMEM)
    prep = pl.pallas_call(
        partial(
            prep_kernel,
            (log2_of(own_count), log2_of(lanes), log2_of(view_group), log2_of(tile_group), tiles_view),
        ),
        out_shape=[
            jax.ShapeDtypeStruct((tiles, slots), jnp.int32),
            jax.ShapeDtypeStruct((tiles, slots), jnp.int32),
            jax.ShapeDtypeStruct((views * 8,), F32),
        ],
        in_specs=[smem] * 3 + [vmem] * 2,
        out_specs=[vmem, vmem, smem],
        scratch_shapes=[
            pltpu.VMEM((3, tiles, slots), F32),
            pltpu.VMEM((tiles, slots), F32),
            pltpu.VMEM((tiles, slots), F32),
            pltpu.VMEM((UNROLL, 16, slots), F32),
            pltpu.VMEM((tiles, slots), jnp.int32),
            pltpu.VMEM((tiles, slots), F32),
        ],
        cost_estimate=pl.CostEstimate(flops=8_000_000_000, bytes_accessed=4 * tiles * slots * 4, transcendentals=0),
        name="prep",
    )

    fields = jnp.concatenate([centres, shape_raw, opacity_logit[None], colours], axis=0)
    block = fields.reshape(FIELDS * GROUPS, lanes)
    note = jnp.pad(totals.astype(F32)[None], ((0, 7), (0, lanes - views)))
    column = jnp.concatenate([block] + [swap(block, "view", m) for m in range(1, view_group)] + [note])
    mine = jnp.stack([column] + [swap(column, "tile", 2 * m) for m in range(1, chips)])
    rows, group, cam = prep(
        me[None],
        live_count,
        camera,
        intersection_ids.reshape(tiles, slots),
        depth_order.reshape(tiles, slots),
    )
    mine, rows, group, cam = lax.optimization_barrier((mine, rows.reshape(-1), group, cam))
    other = swap(mine, "tile", 1)

    table_rows = devices * lanes
    square = (BATCH, slots, pixels)
    half = (chips * view_group, FIELDS * GROUPS, lanes)
    splat = pl.pallas_call(
        partial(splat_kernel, (views, tiles_view, slots, pixels, lanes, view_group)),
        out_shape=[
            jax.ShapeDtypeStruct((views, 3, tiles_view, pixels), F32),
            jax.ShapeDtypeStruct(half, F32),
            jax.ShapeDtypeStruct(half, F32),
        ],
        in_specs=[smem] * 3 + [vmem] * 5,
        out_specs=[vmem] * 3,
        scratch_shapes=[
            pltpu.VMEM((table_rows, lanes), F32),
            pltpu.VMEM((slots, lanes), F32),
            pltpu.VMEM((FIELDS, tiles, slots), F32),
            pltpu.VMEM((9, tiles, slots), F32),
            pltpu.VMEM((9, tiles, slots), F32),
            pltpu.VMEM((FIELDS, tiles, slots), F32),
            pltpu.VMEM(square, F32),
            pltpu.VMEM(square, F32),
        ]
        + [pltpu.VMEM(square, BF16)] * 5
        + [pltpu.VMEM((BATCH, 16, slots), F32), pltpu.VMEM((BATCH, 8, pixels), F32)]
        + [pltpu.VMEM((table_rows, lanes), F32)] * (ACCS if devices <= 32 else 2),
        compiler_params=pltpu.CompilerParams(vmem_limit_bytes=60 * 1024 * 1024),
        name="splat",
    )
    rendered, grad_mine, grad_other = splat(
        cam,
        rows,
        live_count,
        group,
        mine,
        other,
        target.transpose(0, 2, 1, 3),
        monomials(pixels),
    )

    whole = totals
    before = jnp.zeros_like(totals)
    for core, held in enumerate((mine, other)):
        for m in range(chips):
            mask = 2 * m + core
            if mask:
                theirs = held[m, view_group * FIELDS * GROUPS, 0:views].astype(jnp.int32)
                whole = whole + theirs
                before = before + jnp.where((tile_index ^ mask) < tile_index, theirs, 0)
    next_owner = (before[:, None] + within) * tile_group // whole[:, None]

    joined = grad_mine + swap(grad_other, "tile", 1)
    joined = joined.reshape(chips, view_group, FIELDS * GROUPS, lanes)
    part = joined[0]
    for m in range(1, chips):
        part = part + swap(joined[m], "tile", 2 * m)
    summed = part[0]
    for m in range(1, view_group):
        summed = summed + swap(part[m], "view", m)
    summed = summed.reshape(FIELDS, own_count)
    return (
        rendered.transpose(0, 2, 1, 3),
        summed[0:3],
        summed[3:9],
        summed[9],
        summed[10:13],
        next_owner,
    )


def solution(mesh):
    in_specs = (
        P(None, ("view", "tile")),
        P(None, ("view", "tile")),
        P(("view", "tile")),
        P(None, ("view", "tile")),
        P(),
        P("view", "tile", None, None),
        P("view", "tile", None),
        P("view", "tile", None),
        P("view", "tile"),
    )
    out_specs = (
        P("view", "tile", None, None),
        P(None, ("view", "tile")),
        P(None, ("view", "tile")),
        P(("view", "tile")),
        P(None, ("view", "tile")),
        P("view", "tile"),
    )
    return jax.shard_map(shards, mesh=mesh, in_specs=in_specs, out_specs=out_specs, check_vma=False)
```

```python
import functools
from functools import partial
import math

import jax
import jax.numpy as jnp
import numpy as np
from jax import lax
from jax.experimental import pallas as pl
from jax.experimental.pallas import tpu as pltpu
from jax.sharding import PartitionSpec as P

F32 = jnp.float32
BF16 = jnp.bfloat16
FIELDS = 13
GROUPS = 8
ACCS = 4
UNROLL = 4
BATCH = 4
LOG2E = math.log2(math.e)
OFF = -1e4


def log2_of(n):
    bits = n.bit_length() - 1
    assert n == 1 << bits
    return bits


def pieces_of(value, count):
    out = []
    rest = value
    for _ in range(count - 1):
        piece = rest.astype(BF16).astype(F32)
        out.append(piece)
        rest = rest - piece
    out.append(rest)
    return out


def dot_nn(a, b):
    return lax.dot_general(a, b, (((1,), (0,)), ((), ())), preferred_element_type=F32)


def dot_nt(a, b):
    return lax.dot_general(a, b, (((1,), (1,)), ((), ())), preferred_element_type=F32)


def dot_tn(a, b):
    return lax.dot_general(a, b, (((0,), (0,)), ((), ())), preferred_element_type=F32)


def chunk_rows(live):
    return (live + 7) >> 3


def repeat(count, step, body):
    many = lax.div(count, step)

    def trip(i, _):
        for u in range(step):
            body(i * step + u)
        return 0

    def single(i, _):
        body(i)
        return 0

    lax.fori_loop(0, many, trip, 0)
    lax.fori_loop(many * step, count, single, 0)


def prep_kernel(
    dims,
    me_ref,
    live_ref,
    camera_ref,
    ids_ref,
    order_ref,
    row_ref,
    group_ref,
    cam_ref,
    piece_ref,
    rho_ref,
    code_ref,
    lhs_ref,
    live_full,
    order_b,
):
    own_bits, lane_bits, view_bits, tile_bits, tiles_view = dims
    tiles, slots = ids_ref.shape
    me = me_ref[0]
    views = tiles // tiles_view
    first = (me >> tile_bits) * views
    for v in range(views):
        for i in range(2):
            for j in range(4):
                cam_ref[v * 8 + i * 4 + j] = camera_ref[first + v, i, j]
    for t in range(tiles):
        live_full[t : t + 1, :] = jnp.full((1, slots), live_ref[t // tiles_view, t % tiles_view], jnp.int32)
    live = live_full[...]
    order = order_ref[...]
    active = order < live
    upper = (
        lax.broadcasted_iota(jnp.int32, (slots, slots), 0)
        < lax.broadcasted_iota(jnp.int32, (slots, slots), 1)
    ).astype(F32).astype(BF16)
    place = dot_nn(active.astype(F32).astype(BF16), upper).astype(jnp.int32)
    rows = chunk_rows(live)
    chunk = jnp.zeros((tiles, slots), jnp.int32)
    for m in range(1, GROUPS):
        chunk = chunk + (place >= m * rows).astype(jnp.int32)
    rho_ref[...] = jnp.where(active, (place - chunk * rows) * GROUPS + chunk, -1).astype(F32)
    order_b[...] = order.astype(F32)
    ids = ids_ref[...]
    owner = (ids >> own_bits) ^ me
    local = ids & ((1 << own_bits) - 1)
    xy_bits = tile_bits - 1
    core = owner & 1
    chip = (owner >> 1) & ((1 << xy_bits) - 1)
    view = owner >> tile_bits
    block = (((core << xy_bits) | chip) << view_bits) | view
    row = (block << lane_bits) | (local & ((1 << lane_bits) - 1))
    code = (row << 3) | (local >> lane_bits)
    piece_ref[0] = (code & 255).astype(F32)
    piece_ref[1] = ((code >> 8) & 255).astype(F32)
    piece_ref[2] = (code >> 16).astype(F32)
    lhs_ref[...] = jnp.zeros_like(lhs_ref)
    down = lax.broadcasted_iota(jnp.int32, (slots, slots), 0).astype(F32).astype(BF16)
    one = jnp.ones((slots, slots), BF16)
    nil = jnp.zeros((slots, slots), BF16)

    def some_tiles(s, _):
        for u in range(UNROLL):
            t = s * UNROLL + u
            for p in range(3):
                lhs_ref[u, p : p + 1, :] = piece_ref[p, pl.ds(t, 1), :]
            picked = jnp.where(down == order_b[pl.ds(t, 1), :].astype(BF16), one, nil)
            ordered = dot_nn(lhs_ref[u].astype(BF16), picked)
            placed = jnp.where(down == rho_ref[pl.ds(t, 1), :].astype(BF16), one, nil)
            out = dot_nt(ordered.astype(BF16), placed)
            code_ref[pl.ds(t, 1), :] = out[0:1] + 256.0 * out[1:2] + 65536.0 * out[2:3]
        return 0

    lax.fori_loop(0, tiles // UNROLL, some_tiles, 0)
    codes = code_ref[...].astype(jnp.int32)
    row_ref[0:tiles, :] = codes >> 3
    lane = lax.broadcasted_iota(jnp.int32, (tiles, slots), 1)
    above = lax.broadcasted_iota(jnp.int32, (tiles, slots), 0)
    across = jnp.full((tiles, slots), -1, jnp.int32)
    for t in range(tiles):
        across = jnp.where(lane == t, live_ref[t // tiles_view, t % tiles_view], across)
    ahead = (across > live) | ((across == live) & (lane < above))
    rank = jnp.sum(ahead.astype(jnp.int32), axis=1, keepdims=True)
    ranked = jnp.sum(jnp.where(rank == lane, above, 0), axis=0, keepdims=True)
    large = jnp.sum((across > slots // 2).astype(jnp.int32), axis=1, keepdims=True)[0:1]
    row_ref[tiles : tiles + 1, :] = jnp.where(lane[0:1] == tiles, large, ranked)
    pos = lax.broadcasted_iota(jnp.int32, (tiles, slots), 1)
    here = (pos >> 3 < rows) & ((pos & 7) * rows + (pos >> 3) < live)
    group_ref[...] = jnp.where(here, codes & 7, GROUPS)


def splat_kernel(
    dims,
    cam_ref,
    row_ref,
    live_ref,
    group_ref,
    mine_ref,
    other_ref,
    target_ref,
    mono_ref,
    image_ref,
    grad_mine_ref,
    grad_other_ref,
    *scratch,
):
    views, tiles_view, slots, pixels, lanes, column = dims
    table, buf, raw, rec, mom, grad, c_s, h_s, w_hi, w_lo, g_1, g_2, g_3, row_s, row_2 = scratch[:15]
    accs = scratch[15:]
    tiles = views * tiles_view
    chips = mine_ref.shape[0]
    half = chips * column
    used = FIELDS * GROUPS
    pad = jnp.zeros((lanes - used, lanes), F32)

    for acc in accs:
        acc[...] = jnp.zeros_like(acc)
    for ref in (buf, w_hi, w_lo, g_1, g_2, g_3, row_s, row_2):
        ref[...] = jnp.zeros_like(ref)

    def build(q, _):
        for base, ref in ((0, mine_ref), (half, other_ref)):
            for d in range(column):
                block = jnp.concatenate([ref[q, d * used : (d + 1) * used, :], pad], axis=0)
                start = pl.multiple_of((base + q * column + d) * lanes, lanes)
                table[pl.ds(start, lanes), :] = jnp.transpose(block)
        return 0

    lax.fori_loop(0, chips, build, 0)

    def live_of(t):
        return live_ref[lax.div(t, tiles_view), lax.rem(t, tiles_view)]

    def in_turn(body):
        def trip(s, _, positions):
            body([row_ref[tiles * slots + s * BATCH + g] for g in range(BATCH)], positions)
            return 0

        large = lax.div(row_ref[tiles * slots + tiles] + (BATCH - 1), BATCH)
        lax.fori_loop(0, large, partial(trip, positions=slots), 0)
        lax.fori_loop(large, tiles // BATCH, partial(trip, positions=slots // 2), 0)

    sub = lax.broadcasted_iota(jnp.int32, (GROUPS, slots), 0)

    def widen(row):
        spare = slots - row.shape[1]
        return jnp.concatenate([row, jnp.zeros((1, spare), F32)], axis=1) if spare else row

    def fetch(tile, positions):
        for g, t in enumerate(tile):

            def copy(i, t=t, g=g):
                for k in range(GROUPS):
                    buf[g, pl.ds(i * GROUPS + k, 1), :] = table[pl.ds(row_ref[t * slots + i * GROUPS + k], 1), :]

            repeat(chunk_rows(live_of(t)), 4, copy)
        for g, t in enumerate(tile):
            turned = jnp.transpose(buf[g, 0:positions, :])
            mine = sub[:, 0:positions] == group_ref[pl.ds(t, 1), :][:, 0:positions]
            for f in range(FIELDS):
                part = jnp.where(mine, turned[f * GROUPS : (f + 1) * GROUPS], 0.0)
                raw[f, pl.ds(t, 1), :] = widen(jnp.sum(part, axis=0, keepdims=True))

    in_turn(fetch)

    def project(v):
        block = slice(v * tiles_view, (v + 1) * tiles_view)
        cam = [cam_ref[v * 8 + n] for n in range(8)]
        field = lambda f: raw[f, block, :]
        u = cam[0] * field(0) + cam[1] * field(1) + cam[2] * field(2) + cam[3]
        w = cam[4] * field(0) + cam[5] * field(1) + cam[6] * field(2) + cam[7]
        d0, d1, d2 = jnp.exp(field(3)), jnp.exp(field(5)), jnp.exp(field(8))
        factor = []
        for i in range(2):
            m = cam[4 * i : 4 * i + 3]
            factor.append(
                (
                    m[0] * d0 + m[1] * field(4) + m[2] * field(6),
                    m[1] * d1 + m[2] * field(7),
                    m[2] * d2,
                )
            )
        f0, f1 = factor
        s00 = f0[0] * f0[0] + f0[1] * f0[1] + f0[2] * f0[2] + 0.3
        s01 = f0[0] * f1[0] + f0[1] * f1[1] + f0[2] * f1[2]
        s11 = f1[0] * f1[0] + f1[1] * f1[1] + f1[2] * f1[2] + 0.3
        inverse = 1.0 / (s00 * s11 - s01 * s01)
        conic = (s11 * inverse, -s01 * inverse, s00 * inverse)
        here = group_ref[block, :] < GROUPS
        return here, cam, block, u, w, (d0, d1, d2), f0, f1, conic

    for v in range(views):
        here, cam, block, u, w, _, _, _, (ka, kb, kc) = project(v)
        x_line = ka * u + kb * w
        y_line = kb * u + kc * w
        log_opacity = math.log(0.95) - jnp.log(1.0 + jnp.exp(-raw[9, block, :]))
        level = log_opacity - 0.5 * (u * x_line + w * y_line)
        terms = (-0.5 * ka, -kb, -0.5 * kc, x_line, y_line)
        for n, term in enumerate(terms):
            rec[n, block, :] = jnp.where(here, term * LOG2E, 0.0)
        rec[5, block, :] = jnp.where(here, level * LOG2E, OFF)
        for c in range(3):
            rec[6 + c, block, :] = raw[10 + c, block, :]

    lane_row = lax.broadcasted_iota(jnp.int32, (GROUPS, pixels), 0)
    own_chunk = (lax.broadcasted_iota(jnp.int32, (GROUPS, slots), 1) & 7) == sub
    zero_pix = jnp.zeros((8, pixels), F32)

    def paired(a, b):
        return a + pltpu.roll(b, 3, 0)

    def render(tile, positions):
        zero_rows = jnp.zeros((8, positions), F32)
        used = slice(0, positions)
        blocks = (chunk_rows(functools.reduce(jnp.maximum, [live_of(t) for t in tile])) + 3) >> 2
        for g, t in enumerate(tile):
            for n in range(6):
                row_s[g, n : n + 1, :] = rec[n, pl.ds(t, 1), :]
            for c in range(3):
                row_s[g, 8 + c : 9 + c, :] = rec[6 + c, pl.ds(t, 1), :]
        for g in range(BATCH):
            lhs = jnp.concatenate(pieces_of(row_s[g, 0:8, used], 3) + [zero_rows], axis=0).astype(BF16)
            c_s[g, used, :] = dot_tn(lhs, mono_ref[...])
        colour = [pieces_of(row_s[g, 8:16, used], 3) for g in range(BATCH)]

        def through(i, prods):
            rows = pl.ds(pl.multiple_of(i * 32, 32), 32)
            out = []
            for g in range(BATCH):
                cover = jnp.exp2(c_s[g, rows, :])
                c_s[g, rows, :] = cover
                keep = 1.0 - cover
                out.append(prods[g] * ((keep[0:8] * keep[8:16]) * (keep[16:24] * keep[24:32])))
            return tuple(out)

        ones = jnp.ones((GROUPS, pixels), F32)
        lead = list(lax.fori_loop(0, blocks, through, (ones,) * BATCH))
        for g in range(BATCH):
            scan = lead[g]
            for step in (1, 2, 4):
                scan = scan * jnp.where(lane_row >= step, pltpu.roll(scan, step, 0), 1.0)
            lead[g] = jnp.where(lane_row >= 1, pltpu.roll(scan, 1, 0), 1.0)

        def weights(cover, prod):
            out = []
            for h in range(4):
                weight = prod * cover[8 * h : 8 * h + 8]
                prod = prod - weight
                out.append(weight)
            return out, prod

        def weigh(i, prods):
            rows = pl.ds(pl.multiple_of(i * 32, 32), 32)
            out = []
            for g in range(BATCH):
                parts, prod = weights(c_s[g, rows, :], prods[g])
                weight = jnp.concatenate(parts, axis=0)
                high = weight.astype(BF16)
                w_hi[g, rows, :] = high
                w_lo[g, rows, :] = (weight - high.astype(F32)).astype(BF16)
                out.append(prod)
            return tuple(out)

        lax.fori_loop(0, blocks, weigh, tuple(lead))

        after = []
        for g, t in enumerate(tile):
            v, tl = lax.div(t, tiles_view), lax.rem(t, tiles_view)
            spread = [
                jnp.where(own_chunk[:, used], jnp.broadcast_to(piece[c : c + 1], (GROUPS, positions)), 0.0)
                for c in range(3)
                for piece in colour[g]
            ]
            lhs = jnp.concatenate(spread + [zero_rows], axis=0).astype(BF16)
            image = dot_nn(lhs, w_hi[g, used, :]) + dot_nn(lhs, w_lo[g, used, :])
            rest = jnp.zeros((GROUPS, pixels), F32)
            for c in range(3):
                part = image[24 * c : 24 * c + 8] + image[24 * c + 8 : 24 * c + 16] + image[24 * c + 16 : 24 * c + 24]
                whole = jnp.sum(part, axis=0, keepdims=True)
                image_ref[v, c, pl.ds(tl, 1), :] = whole
                miss = whole - target_ref[v, c, pl.ds(tl, 1), :]
                row_2[g, c : c + 1, :] = miss
                rest = rest + part * miss
            for step in (1, 2, 4):
                rest = rest + jnp.where(lane_row < GROUPS - step, pltpu.roll(rest, GROUPS - step, 0), 0.0)
            after.append(rest)
        missed = [pieces_of(row_2[g], 3) for g in range(BATCH)]
        for g in range(BATCH):
            c1, c2, c3 = colour[g]
            m1, m2, m3 = missed[g]
            lhs = jnp.concatenate([paired(c1, c1), paired(c2, c1), paired(c2, c3), zero_rows], axis=0)
            rhs = jnp.concatenate([paired(m1, m2), paired(m1, m3), paired(m2, m1), zero_pix], axis=0)
            h_s[g, used, :] = dot_tn(lhs.astype(BF16), rhs.astype(BF16))

        def settle(i, carry):
            rows = pl.ds(pl.multiple_of(i * 32, 32), 32)
            out = []
            for g in range(BATCH):
                prod, tail = carry[g]
                cover = c_s[g, rows, :]
                pull = h_s[g, rows, :]
                parts, prod = weights(cover, prod)
                ratio = cover / (1.0 - cover)
                slopes = []
                for h in range(4):
                    cut = slice(8 * h, 8 * h + 8)
                    part = parts[h] * pull[cut]
                    tail = tail - part
                    slopes.append(part - ratio[cut] * tail)
                slope = jnp.concatenate(slopes, axis=0)
                high = slope.astype(BF16)
                rest = slope - high.astype(F32)
                middle = rest.astype(BF16)
                g_1[g, rows, :] = high
                g_2[g, rows, :] = middle
                g_3[g, rows, :] = (rest - middle.astype(F32)).astype(BF16)
                out.append((prod, tail))
            return tuple(out)

        lax.fori_loop(0, blocks, settle, tuple(zip(lead, after)))
        mono = mono_ref[0:16, :]
        for g in range(BATCH):
            moments = dot_nt(mono, g_1[g, used, :]) + dot_nt(mono, g_2[g, used, :]) + dot_nt(mono, g_3[g, used, :])
            miss_lhs = jnp.concatenate(missed[g] + [zero_pix], axis=0).astype(BF16)
            tint = dot_nt(miss_lhs, w_hi[g, used, :]) + dot_nt(miss_lhs, w_lo[g, used, :])
            row_s[g, 0:8, used] = moments[0:8]
            row_s[g, 8:16, used] = tint[0:8] + tint[8:16] + tint[16:24]
        for g, t in enumerate(tile):
            for n in range(6):
                mom[n, pl.ds(t, 1), :] = row_s[g, n : n + 1, :]
            for c in range(3):
                mom[6 + c, pl.ds(t, 1), :] = row_s[g, 8 + c : 9 + c, :]

    in_turn(render)

    for v in range(views):
        here, cam, block, u, w, (d0, d1, d2), f0, f1, (ka, kb, kc) = project(v)
        mxx, mxy, myy, mx, my, m1 = [jnp.where(here, mom[n, block, :], 0.0) for n in range(6)]
        dx = mx - u * m1
        dy = my - w * m1
        dxx = mxx - 2.0 * u * mx + u * u * m1
        dxy = mxy - u * my - w * mx + u * w * m1
        dyy = myy - 2.0 * w * my + w * w * m1
        gu = ka * dx + kb * dy
        gw = kb * dx + kc * dy
        ax, ay = ka * dxx + kb * dxy, ka * dxy + kb * dyy
        bx, by = kb * dxx + kc * dxy, kb * dxy + kc * dyy
        h00 = ax * ka + ay * kb
        h01 = ax * kb + ay * kc
        h11 = bx * kb + by * kc
        g0 = [h00 * f0[j] + h01 * f1[j] for j in range(3)]
        g1 = [h01 * f0[j] + h11 * f1[j] for j in range(3)]
        for k in range(3):
            grad[k, block, :] = cam[k] * gu + cam[4 + k] * gw
        grad[3, block, :] = (cam[0] * g0[0] + cam[4] * g1[0]) * d0
        grad[4, block, :] = cam[1] * g0[0] + cam[5] * g1[0]
        grad[5, block, :] = (cam[1] * g0[1] + cam[5] * g1[1]) * d1
        grad[6, block, :] = cam[2] * g0[0] + cam[6] * g1[0]
        grad[7, block, :] = cam[2] * g0[1] + cam[6] * g1[1]
        grad[8, block, :] = (cam[2] * g0[2] + cam[6] * g1[2]) * d2
        grad[9, block, :] = m1 - m1 / (1.0 + jnp.exp(-raw[9, block, :]))
        for c in range(3):
            grad[10 + c, block, :] = mom[6 + c, block, :]

    def give(tile, positions):
        for g, t in enumerate(tile):
            mine = sub[:, 0:positions] == group_ref[pl.ds(t, 1), :][:, 0:positions]
            spread = [
                jnp.where(mine, jnp.broadcast_to(grad[f, pl.ds(t, 1), :][:, 0:positions], (GROUPS, positions)), 0.0)
                for f in range(FIELDS)
            ]
            spread.append(jnp.zeros((lanes - used, positions), F32))
            buf[g, 0:positions, :] = jnp.transpose(jnp.concatenate(spread, axis=0))
        for g, t in enumerate(tile):

            def add(i, t=t, g=g):
                for k in range(0, GROUPS, len(accs)):
                    where = [row_ref[t * slots + i * GROUPS + k + n] for n in range(len(accs))]
                    olds = [accs[n][pl.ds(where[n], 1), :] for n in range(len(accs))]
                    news = [buf[g, pl.ds(i * GROUPS + k + n, 1), :] for n in range(len(accs))]
                    for n in range(len(accs)):
                        accs[n][pl.ds(where[n], 1), :] = olds[n] + news[n]

            repeat(chunk_rows(live_of(t)), 4, add)

    in_turn(give)

    def finish(d, _):
        for base, ref in ((0, grad_mine_ref), (half, grad_other_ref)):
            start = pl.multiple_of((base + d) * lanes, lanes)
            total = accs[0][pl.ds(start, lanes), :]
            for acc in accs[1:]:
                total = total + acc[pl.ds(start, lanes), :]
            ref[d] = jnp.transpose(total)[0:used]
        return 0

    lax.fori_loop(0, half, finish, 0)


def monomials(pixels):
    side = math.isqrt(pixels)
    index = np.arange(pixels)
    x = (index % side) - (side - 1) / 2.0
    y = (index // side) - (side - 1) / 2.0
    one = np.ones_like(x)
    zero = np.zeros_like(x)
    group = np.stack([x * x, x * y, y * y, x, y, one, zero, zero])
    return jnp.asarray(np.concatenate([group, group, group, np.zeros_like(group)]), BF16)


def swap(array, axis, mask):
    size = lax.axis_size(axis)
    return lax.ppermute(array, axis, [(i, i ^ mask) for i in range(size)])


def shards(centres, shape_raw, opacity_logit, colours, camera, target, intersection_ids, depth_order, live_count):
    view_group = lax.axis_size("view")
    tile_group = lax.axis_size("tile")
    devices = view_group * tile_group
    chips = tile_group // 2
    own_count = centres.shape[1]
    lanes = own_count // GROUPS
    views, tiles_view, slots = intersection_ids.shape
    tiles = views * tiles_view
    pixels = target.shape[3]
    view_index = lax.axis_index("view")
    tile_index = lax.axis_index("tile")
    me = (view_index * tile_group + tile_index).astype(jnp.int32)

    totals = jnp.sum(live_count, axis=1)
    within = jnp.cumsum(live_count, axis=1) - live_count

    smem = pl.BlockSpec(memory_space=pltpu.SMEM)
    vmem = pl.BlockSpec(memory_space=pltpu.VMEM)
    prep = pl.pallas_call(
        partial(
            prep_kernel,
            (log2_of(own_count), log2_of(lanes), log2_of(view_group), log2_of(tile_group), tiles_view),
        ),
        out_shape=[
            jax.ShapeDtypeStruct((tiles + 8, slots), jnp.int32),
            jax.ShapeDtypeStruct((tiles, slots), jnp.int32),
            jax.ShapeDtypeStruct((views * 8,), F32),
        ],
        in_specs=[smem] * 3 + [vmem] * 2,
        out_specs=[vmem, vmem, smem],
        scratch_shapes=[
            pltpu.VMEM((3, tiles, slots), F32),
            pltpu.VMEM((tiles, slots), F32),
            pltpu.VMEM((tiles, slots), F32),
            pltpu.VMEM((UNROLL, 16, slots), F32),
            pltpu.VMEM((tiles, slots), jnp.int32),
            pltpu.VMEM((tiles, slots), F32),
        ],
        cost_estimate=pl.CostEstimate(flops=8_000_000_000, bytes_accessed=4 * tiles * slots * 4, transcendentals=0),
        name="prep",
    )

    fields = jnp.concatenate([centres, shape_raw, opacity_logit[None], colours], axis=0)
    block = fields.reshape(FIELDS * GROUPS, lanes)
    note = jnp.pad(totals.astype(F32)[None], ((0, 7), (0, lanes - views)))
    column = jnp.concatenate([block] + [swap(block, "view", m) for m in range(1, view_group)] + [note])
    mine = jnp.stack([column] + [swap(column, "tile", 2 * m) for m in range(1, chips)])
    rows, group, cam = prep(
        me[None],
        live_count,
        camera,
        intersection_ids.reshape(tiles, slots),
        depth_order.reshape(tiles, slots),
    )
    mine, rows, group, cam = lax.optimization_barrier((mine, rows.reshape(-1), group, cam))
    other = swap(mine, "tile", 1)

    table_rows = devices * lanes
    square = (BATCH, slots, pixels)
    half = (chips * view_group, FIELDS * GROUPS, lanes)
    accs = ACCS if devices <= 32 else 2
    room = 4 * table_rows * lanes * (accs + 2) + 16 * 1024 * 1024
    splat = pl.pallas_call(
        partial(splat_kernel, (views, tiles_view, slots, pixels, lanes, view_group)),
        out_shape=[
            jax.ShapeDtypeStruct((views, 3, tiles_view, pixels), F32),
            jax.ShapeDtypeStruct(half, F32),
            jax.ShapeDtypeStruct(half, F32),
        ],
        in_specs=[smem] * 3 + [vmem] * 5,
        out_specs=[vmem] * 3,
        scratch_shapes=[
            pltpu.VMEM((table_rows, lanes), F32),
            pltpu.VMEM((BATCH, slots, lanes), F32),
            pltpu.VMEM((FIELDS, tiles, slots), F32),
            pltpu.VMEM((9, tiles, slots), F32),
            pltpu.VMEM((9, tiles, slots), F32),
            pltpu.VMEM((FIELDS, tiles, slots), F32),
            pltpu.VMEM(square, F32),
            pltpu.VMEM(square, F32),
        ]
        + [pltpu.VMEM(square, BF16)] * 5
        + [pltpu.VMEM((BATCH, 16, slots), F32), pltpu.VMEM((BATCH, 8, pixels), F32)]
        + [pltpu.VMEM((table_rows, lanes), F32)] * accs,
        compiler_params=pltpu.CompilerParams(vmem_limit_bytes=room),
        name="splat",
    )
    rendered, grad_mine, grad_other = splat(
        cam,
        rows,
        live_count,
        group,
        mine,
        other,
        target.transpose(0, 2, 1, 3),
        monomials(pixels),
    )

    whole = totals
    before = jnp.zeros_like(totals)
    for core, held in enumerate((mine, other)):
        for m in range(chips):
            mask = 2 * m + core
            if mask:
                theirs = held[m, view_group * FIELDS * GROUPS, 0:views].astype(jnp.int32)
                whole = whole + theirs
                before = before + jnp.where((tile_index ^ mask) < tile_index, theirs, 0)
    next_owner = (before[:, None] + within) * tile_group // whole[:, None]

    joined = grad_mine + swap(grad_other, "tile", 1)
    joined = joined.reshape(chips, view_group, FIELDS * GROUPS, lanes)
    part = joined[0]
    for m in range(1, chips):
        part = part + swap(joined[m], "tile", 2 * m)
    summed = part[0]
    for m in range(1, view_group):
        summed = summed + swap(part[m], "view", m)
    summed = summed.reshape(FIELDS, own_count)
    return (
        rendered.transpose(0, 2, 1, 3),
        summed[0:3],
        summed[3:9],
        summed[9],
        summed[10:13],
        next_owner,
    )


def solution(mesh):
    in_specs = (
        P(None, ("view", "tile")),
        P(None, ("view", "tile")),
        P(("view", "tile")),
        P(None, ("view", "tile")),
        P(),
        P("view", "tile", None, None),
        P("view", "tile", None),
        P("view", "tile", None),
        P("view", "tile"),
    )
    out_specs = (
        P("view", "tile", None, None),
        P(None, ("view", "tile")),
        P(None, ("view", "tile")),
        P(("view", "tile")),
        P(None, ("view", "tile")),
        P("view", "tile"),
    )
    return jax.shard_map(shards, mesh=mesh, in_specs=in_specs, out_specs=out_specs, check_vma=False)
```

```python
import functools
from functools import partial
import math

import jax
import jax.numpy as jnp
import numpy as np
from jax import lax
from jax.experimental import pallas as pl
from jax.experimental.pallas import tpu as pltpu
from jax.sharding import PartitionSpec as P

F32 = jnp.float32
BF16 = jnp.bfloat16
FIELDS = 13
GROUPS = 8
ACCS = 4
UNROLL = 4
BATCH = 4
LOG2E = math.log2(math.e)
OFF = -1e4


def log2_of(n):
    bits = n.bit_length() - 1
    assert n == 1 << bits
    return bits


def pieces_of(value, count):
    out = []
    rest = value
    for _ in range(count - 1):
        piece = rest.astype(BF16).astype(F32)
        out.append(piece)
        rest = rest - piece
    out.append(rest)
    return out


def dot_nn(a, b):
    return lax.dot_general(a, b, (((1,), (0,)), ((), ())), preferred_element_type=F32)


def dot_nt(a, b):
    return lax.dot_general(a, b, (((1,), (1,)), ((), ())), preferred_element_type=F32)


def dot_tn(a, b):
    return lax.dot_general(a, b, (((0,), (0,)), ((), ())), preferred_element_type=F32)


def chunk_rows(live):
    return (live + 7) >> 3


def repeat(count, step, body):
    many = lax.div(count, step)

    def trip(i, _):
        for u in range(step):
            body(i * step + u)
        return 0

    def single(i, _):
        body(i)
        return 0

    lax.fori_loop(0, many, trip, 0)
    lax.fori_loop(many * step, count, single, 0)


def prep_kernel(
    dims,
    me_ref,
    live_ref,
    camera_ref,
    ids_ref,
    order_ref,
    theirs_ref,
    row_ref,
    group_ref,
    cam_ref,
    piece_ref,
    rho_ref,
    code_ref,
    lhs_ref,
    live_full,
    order_b,
):
    own_bits, lane_bits, view_bits, tile_bits, tiles_view = dims
    views, _, slots = ids_ref.shape
    tiles = views * tiles_view
    kept = tiles_view // 2
    me = me_ref[0]
    first = (me >> tile_bits) * views
    for v in range(views):
        for i in range(2):
            for j in range(4):
                cam_ref[v * 8 + i * 4 + j] = camera_ref[first + v, i, j]
    for t in range(tiles):
        live_full[t : t + 1, :] = jnp.full((1, slots), live_ref[t // tiles_view, t % tiles_view], jnp.int32)
    live = live_full[...]
    parts = []
    for v in range(views):
        parts += [order_ref[v, 0:kept, :], theirs_ref[v, kept : 2 * kept, :]]
    order = jnp.concatenate(parts, axis=0)
    active = order < live
    upper = (
        lax.broadcasted_iota(jnp.int32, (slots, slots), 0)
        < lax.broadcasted_iota(jnp.int32, (slots, slots), 1)
    ).astype(F32).astype(BF16)
    place = dot_nn(active.astype(F32).astype(BF16), upper).astype(jnp.int32)
    rows = chunk_rows(live)
    chunk = jnp.zeros((tiles, slots), jnp.int32)
    for m in range(1, GROUPS):
        chunk = chunk + (place >= m * rows).astype(jnp.int32)
    rho_ref[...] = jnp.where(active, (place - chunk * rows) * GROUPS + chunk, -1).astype(F32)
    order_b[...] = order.astype(F32)
    parts = []
    for v in range(views):
        parts += [ids_ref[v, 0:kept, :], theirs_ref[v, 0:kept, :]]
    ids = jnp.concatenate(parts, axis=0)
    owner = (ids >> own_bits) ^ me
    local = ids & ((1 << own_bits) - 1)
    xy_bits = tile_bits - 1
    core = owner & 1
    chip = (owner >> 1) & ((1 << xy_bits) - 1)
    view = owner >> tile_bits
    block = (((core << xy_bits) | chip) << view_bits) | view
    row = (block << lane_bits) | (local & ((1 << lane_bits) - 1))
    code = (row << 3) | (local >> lane_bits)
    piece_ref[0] = (code & 255).astype(F32)
    piece_ref[1] = ((code >> 8) & 255).astype(F32)
    piece_ref[2] = (code >> 16).astype(F32)
    lhs_ref[...] = jnp.zeros_like(lhs_ref)
    down = lax.broadcasted_iota(jnp.int32, (slots, slots), 0).astype(F32).astype(BF16)
    one = jnp.ones((slots, slots), BF16)
    nil = jnp.zeros((slots, slots), BF16)

    def some_tiles(s, _):
        for u in range(UNROLL):
            t = s * UNROLL + u
            for p in range(3):
                lhs_ref[u, p : p + 1, :] = piece_ref[p, pl.ds(t, 1), :]
            picked = jnp.where(down == order_b[pl.ds(t, 1), :].astype(BF16), one, nil)
            ordered = dot_nn(lhs_ref[u].astype(BF16), picked)
            placed = jnp.where(down == rho_ref[pl.ds(t, 1), :].astype(BF16), one, nil)
            out = dot_nt(ordered.astype(BF16), placed)
            code_ref[pl.ds(t, 1), :] = out[0:1] + 256.0 * out[1:2] + 65536.0 * out[2:3]
        return 0

    lax.fori_loop(0, tiles // UNROLL, some_tiles, 0)
    codes = code_ref[...].astype(jnp.int32)
    row_ref[0:tiles, :] = codes >> 3
    lane = lax.broadcasted_iota(jnp.int32, (tiles, slots), 1)
    above = lax.broadcasted_iota(jnp.int32, (tiles, slots), 0)
    across = jnp.full((tiles, slots), -1, jnp.int32)
    for t in range(tiles):
        across = jnp.where(lane == t, live_ref[t // tiles_view, t % tiles_view], across)
    ahead = (across > live) | ((across == live) & (lane < above))
    rank = jnp.sum(ahead.astype(jnp.int32), axis=1, keepdims=True)
    ranked = jnp.sum(jnp.where(rank == lane, above, 0), axis=0, keepdims=True)
    large = jnp.sum((across > slots // 2).astype(jnp.int32), axis=1, keepdims=True)[0:1]
    row_ref[tiles : tiles + 1, :] = jnp.where(lane[0:1] == tiles, large, ranked)
    pos = lax.broadcasted_iota(jnp.int32, (tiles, slots), 1)
    here = (pos >> 3 < rows) & ((pos & 7) * rows + (pos >> 3) < live)
    group_ref[...] = jnp.where(here, codes & 7, GROUPS)


def splat_kernel(
    dims,
    cam_ref,
    row_ref,
    live_ref,
    group_ref,
    mine_ref,
    other_ref,
    target_ref,
    their_target_ref,
    mono_ref,
    image_ref,
    their_image_ref,
    grad_mine_ref,
    grad_other_ref,
    *scratch,
):
    views, tiles_view, slots, pixels, lanes, column = dims
    table, buf, raw, rec, mom, grad, c_s, h_s, w_hi, w_lo, g_1, g_2, g_3, row_s, row_2, want, got = scratch[:17]
    accs = scratch[17:]
    tiles = views * tiles_view
    chips = mine_ref.shape[0]
    half = chips * column
    used = FIELDS * GROUPS
    pad = jnp.zeros((lanes - used, lanes), F32)

    for acc in accs:
        acc[...] = jnp.zeros_like(acc)
    for ref in (buf, w_hi, w_lo, g_1, g_2, g_3, row_s, row_2):
        ref[...] = jnp.zeros_like(ref)

    kept = tiles_view // 2
    want[:, :, 0:kept, :] = target_ref[:, :, 0:kept, :]
    want[:, :, kept:, :] = their_target_ref[...]

    def build(q, _):
        for base, ref in ((0, mine_ref), (half, other_ref)):
            for d in range(column):
                block = jnp.concatenate([ref[q, d * used : (d + 1) * used, :], pad], axis=0)
                start = pl.multiple_of((base + q * column + d) * lanes, lanes)
                table[pl.ds(start, lanes), :] = jnp.transpose(block)
        return 0

    lax.fori_loop(0, chips, build, 0)

    def live_of(t):
        return live_ref[lax.div(t, tiles_view), lax.rem(t, tiles_view)]

    def in_turn(body):
        def trip(s, _, positions):
            body([row_ref[tiles * slots + s * BATCH + g] for g in range(BATCH)], positions)
            return 0

        large = lax.div(row_ref[tiles * slots + tiles] + (BATCH - 1), BATCH)
        lax.fori_loop(0, large, partial(trip, positions=slots), 0)
        lax.fori_loop(large, tiles // BATCH, partial(trip, positions=slots // 2), 0)

    sub = lax.broadcasted_iota(jnp.int32, (GROUPS, slots), 0)

    def widen(row):
        spare = slots - row.shape[1]
        return jnp.concatenate([row, jnp.zeros((1, spare), F32)], axis=1) if spare else row

    def fetch(tile, positions):
        for g, t in enumerate(tile):

            def copy(i, t=t, g=g):
                for k in range(GROUPS):
                    buf[g, pl.ds(i * GROUPS + k, 1), :] = table[pl.ds(row_ref[t * slots + i * GROUPS + k], 1), :]

            repeat(chunk_rows(live_of(t)), 4, copy)
        for g, t in enumerate(tile):
            turned = jnp.transpose(buf[g, 0:positions, :])
            mine = sub[:, 0:positions] == group_ref[pl.ds(t, 1), :][:, 0:positions]
            for f in range(FIELDS):
                part = jnp.where(mine, turned[f * GROUPS : (f + 1) * GROUPS], 0.0)
                raw[f, pl.ds(t, 1), :] = widen(jnp.sum(part, axis=0, keepdims=True))

    in_turn(fetch)

    def project(v):
        block = slice(v * tiles_view, (v + 1) * tiles_view)
        cam = [cam_ref[v * 8 + n] for n in range(8)]
        field = lambda f: raw[f, block, :]
        u = cam[0] * field(0) + cam[1] * field(1) + cam[2] * field(2) + cam[3]
        w = cam[4] * field(0) + cam[5] * field(1) + cam[6] * field(2) + cam[7]
        d0, d1, d2 = jnp.exp(field(3)), jnp.exp(field(5)), jnp.exp(field(8))
        factor = []
        for i in range(2):
            m = cam[4 * i : 4 * i + 3]
            factor.append(
                (
                    m[0] * d0 + m[1] * field(4) + m[2] * field(6),
                    m[1] * d1 + m[2] * field(7),
                    m[2] * d2,
                )
            )
        f0, f1 = factor
        s00 = f0[0] * f0[0] + f0[1] * f0[1] + f0[2] * f0[2] + 0.3
        s01 = f0[0] * f1[0] + f0[1] * f1[1] + f0[2] * f1[2]
        s11 = f1[0] * f1[0] + f1[1] * f1[1] + f1[2] * f1[2] + 0.3
        inverse = 1.0 / (s00 * s11 - s01 * s01)
        conic = (s11 * inverse, -s01 * inverse, s00 * inverse)
        here = group_ref[block, :] < GROUPS
        return here, cam, block, u, w, (d0, d1, d2), f0, f1, conic

    for v in range(views):
        here, cam, block, u, w, _, _, _, (ka, kb, kc) = project(v)
        x_line = ka * u + kb * w
        y_line = kb * u + kc * w
        log_opacity = math.log(0.95) - jnp.log(1.0 + jnp.exp(-raw[9, block, :]))
        level = log_opacity - 0.5 * (u * x_line + w * y_line)
        terms = (-0.5 * ka, -kb, -0.5 * kc, x_line, y_line)
        for n, term in enumerate(terms):
            rec[n, block, :] = jnp.where(here, term * LOG2E, 0.0)
        rec[5, block, :] = jnp.where(here, level * LOG2E, OFF)
        for c in range(3):
            rec[6 + c, block, :] = raw[10 + c, block, :]

    lane_row = lax.broadcasted_iota(jnp.int32, (GROUPS, pixels), 0)
    own_chunk = (lax.broadcasted_iota(jnp.int32, (GROUPS, slots), 1) & 7) == sub
    zero_pix = jnp.zeros((8, pixels), F32)

    def paired(a, b):
        return a + pltpu.roll(b, 3, 0)

    def render(tile, positions):
        zero_rows = jnp.zeros((8, positions), F32)
        used = slice(0, positions)
        blocks = (chunk_rows(functools.reduce(jnp.maximum, [live_of(t) for t in tile])) + 3) >> 2
        for g, t in enumerate(tile):
            for n in range(6):
                row_s[g, n : n + 1, :] = rec[n, pl.ds(t, 1), :]
            for c in range(3):
                row_s[g, 8 + c : 9 + c, :] = rec[6 + c, pl.ds(t, 1), :]
        for g in range(BATCH):
            lhs = jnp.concatenate(pieces_of(row_s[g, 0:8, used], 3) + [zero_rows], axis=0).astype(BF16)
            c_s[g, used, :] = dot_tn(lhs, mono_ref[...])
        colour = [pieces_of(row_s[g, 8:16, used], 3) for g in range(BATCH)]

        def through(i, prods):
            rows = pl.ds(pl.multiple_of(i * 32, 32), 32)
            out = []
            for g in range(BATCH):
                cover = jnp.exp2(c_s[g, rows, :])
                c_s[g, rows, :] = cover
                keep = 1.0 - cover
                out.append(prods[g] * ((keep[0:8] * keep[8:16]) * (keep[16:24] * keep[24:32])))
            return tuple(out)

        ones = jnp.ones((GROUPS, pixels), F32)
        lead = list(lax.fori_loop(0, blocks, through, (ones,) * BATCH))
        for g in range(BATCH):
            scan = lead[g]
            for step in (1, 2, 4):
                scan = scan * jnp.where(lane_row >= step, pltpu.roll(scan, step, 0), 1.0)
            lead[g] = jnp.where(lane_row >= 1, pltpu.roll(scan, 1, 0), 1.0)

        def weights(cover, prod):
            out = []
            for h in range(4):
                weight = prod * cover[8 * h : 8 * h + 8]
                prod = prod - weight
                out.append(weight)
            return out, prod

        def weigh(i, prods):
            rows = pl.ds(pl.multiple_of(i * 32, 32), 32)
            out = []
            for g in range(BATCH):
                parts, prod = weights(c_s[g, rows, :], prods[g])
                weight = jnp.concatenate(parts, axis=0)
                high = weight.astype(BF16)
                w_hi[g, rows, :] = high
                w_lo[g, rows, :] = (weight - high.astype(F32)).astype(BF16)
                out.append(prod)
            return tuple(out)

        lax.fori_loop(0, blocks, weigh, tuple(lead))

        after = []
        for g, t in enumerate(tile):
            v, tl = lax.div(t, tiles_view), lax.rem(t, tiles_view)
            spread = [
                jnp.where(own_chunk[:, used], jnp.broadcast_to(piece[c : c + 1], (GROUPS, positions)), 0.0)
                for c in range(3)
                for piece in colour[g]
            ]
            lhs = jnp.concatenate(spread + [zero_rows], axis=0).astype(BF16)
            image = dot_nn(lhs, w_hi[g, used, :]) + dot_nn(lhs, w_lo[g, used, :])
            rest = jnp.zeros((GROUPS, pixels), F32)
            for c in range(3):
                part = image[24 * c : 24 * c + 8] + image[24 * c + 8 : 24 * c + 16] + image[24 * c + 16 : 24 * c + 24]
                whole = jnp.sum(part, axis=0, keepdims=True)
                got[v, c, pl.ds(tl, 1), :] = whole
                miss = whole - want[v, c, pl.ds(tl, 1), :]
                row_2[g, c : c + 1, :] = miss
                rest = rest + part * miss
            for step in (1, 2, 4):
                rest = rest + jnp.where(lane_row < GROUPS - step, pltpu.roll(rest, GROUPS - step, 0), 0.0)
            after.append(rest)
        missed = [pieces_of(row_2[g], 3) for g in range(BATCH)]
        for g in range(BATCH):
            c1, c2, c3 = colour[g]
            m1, m2, m3 = missed[g]
            lhs = jnp.concatenate([paired(c1, c1), paired(c2, c1), paired(c2, c3), zero_rows], axis=0)
            rhs = jnp.concatenate([paired(m1, m2), paired(m1, m3), paired(m2, m1), zero_pix], axis=0)
            h_s[g, used, :] = dot_tn(lhs.astype(BF16), rhs.astype(BF16))

        def settle(i, carry):
            rows = pl.ds(pl.multiple_of(i * 32, 32), 32)
            out = []
            for g in range(BATCH):
                prod, tail = carry[g]
                cover = c_s[g, rows, :]
                pull = h_s[g, rows, :]
                parts, prod = weights(cover, prod)
                ratio = cover / (1.0 - cover)
                slopes = []
                for h in range(4):
                    cut = slice(8 * h, 8 * h + 8)
                    part = parts[h] * pull[cut]
                    tail = tail - part
                    slopes.append(part - ratio[cut] * tail)
                slope = jnp.concatenate(slopes, axis=0)
                high = slope.astype(BF16)
                rest = slope - high.astype(F32)
                middle = rest.astype(BF16)
                g_1[g, rows, :] = high
                g_2[g, rows, :] = middle
                g_3[g, rows, :] = (rest - middle.astype(F32)).astype(BF16)
                out.append((prod, tail))
            return tuple(out)

        lax.fori_loop(0, blocks, settle, tuple(zip(lead, after)))
        mono = mono_ref[0:16, :]
        for g in range(BATCH):
            moments = dot_nt(mono, g_1[g, used, :]) + dot_nt(mono, g_2[g, used, :]) + dot_nt(mono, g_3[g, used, :])
            miss_lhs = jnp.concatenate(missed[g] + [zero_pix], axis=0).astype(BF16)
            tint = dot_nt(miss_lhs, w_hi[g, used, :]) + dot_nt(miss_lhs, w_lo[g, used, :])
            row_s[g, 0:8, used] = moments[0:8]
            row_s[g, 8:16, used] = tint[0:8] + tint[8:16] + tint[16:24]
        for g, t in enumerate(tile):
            for n in range(6):
                mom[n, pl.ds(t, 1), :] = row_s[g, n : n + 1, :]
            for c in range(3):
                mom[6 + c, pl.ds(t, 1), :] = row_s[g, 8 + c : 9 + c, :]

    in_turn(render)
    image_ref[...] = got[:, :, 0:kept, :]
    their_image_ref[...] = got[:, :, kept:, :]

    for v in range(views):
        here, cam, block, u, w, (d0, d1, d2), f0, f1, (ka, kb, kc) = project(v)
        mxx, mxy, myy, mx, my, m1 = [jnp.where(here, mom[n, block, :], 0.0) for n in range(6)]
        dx = mx - u * m1
        dy = my - w * m1
        dxx = mxx - 2.0 * u * mx + u * u * m1
        dxy = mxy - u * my - w * mx + u * w * m1
        dyy = myy - 2.0 * w * my + w * w * m1
        gu = ka * dx + kb * dy
        gw = kb * dx + kc * dy
        ax, ay = ka * dxx + kb * dxy, ka * dxy + kb * dyy
        bx, by = kb * dxx + kc * dxy, kb * dxy + kc * dyy
        h00 = ax * ka + ay * kb
        h01 = ax * kb + ay * kc
        h11 = bx * kb + by * kc
        g0 = [h00 * f0[j] + h01 * f1[j] for j in range(3)]
        g1 = [h01 * f0[j] + h11 * f1[j] for j in range(3)]
        for k in range(3):
            grad[k, block, :] = cam[k] * gu + cam[4 + k] * gw
        grad[3, block, :] = (cam[0] * g0[0] + cam[4] * g1[0]) * d0
        grad[4, block, :] = cam[1] * g0[0] + cam[5] * g1[0]
        grad[5, block, :] = (cam[1] * g0[1] + cam[5] * g1[1]) * d1
        grad[6, block, :] = cam[2] * g0[0] + cam[6] * g1[0]
        grad[7, block, :] = cam[2] * g0[1] + cam[6] * g1[1]
        grad[8, block, :] = (cam[2] * g0[2] + cam[6] * g1[2]) * d2
        grad[9, block, :] = m1 - m1 / (1.0 + jnp.exp(-raw[9, block, :]))
        for c in range(3):
            grad[10 + c, block, :] = mom[6 + c, block, :]

    def give(tile, positions):
        for g, t in enumerate(tile):
            mine = sub[:, 0:positions] == group_ref[pl.ds(t, 1), :][:, 0:positions]
            spread = [
                jnp.where(mine, jnp.broadcast_to(grad[f, pl.ds(t, 1), :][:, 0:positions], (GROUPS, positions)), 0.0)
                for f in range(FIELDS)
            ]
            spread.append(jnp.zeros((lanes - used, positions), F32))
            buf[g, 0:positions, :] = jnp.transpose(jnp.concatenate(spread, axis=0))
        for g, t in enumerate(tile):

            def add(i, t=t, g=g):
                for k in range(0, GROUPS, len(accs)):
                    where = [row_ref[t * slots + i * GROUPS + k + n] for n in range(len(accs))]
                    olds = [accs[n][pl.ds(where[n], 1), :] for n in range(len(accs))]
                    news = [buf[g, pl.ds(i * GROUPS + k + n, 1), :] for n in range(len(accs))]
                    for n in range(len(accs)):
                        accs[n][pl.ds(where[n], 1), :] = olds[n] + news[n]

            repeat(chunk_rows(live_of(t)), 4, add)

    in_turn(give)

    def finish(d, _):
        for base, ref in ((0, grad_mine_ref), (half, grad_other_ref)):
            start = pl.multiple_of((base + d) * lanes, lanes)
            total = accs[0][pl.ds(start, lanes), :]
            for acc in accs[1:]:
                total = total + acc[pl.ds(start, lanes), :]
            ref[d] = jnp.transpose(total)[0:used]
        return 0

    lax.fori_loop(0, half, finish, 0)


def tail_kernel(*refs):
    parts, (centres_ref, shape_ref, opacity_ref, colours_ref), total = refs[:-5], refs[-5:-1], refs[-1]
    lanes = total.shape[1]
    value = parts[0][...]
    for part in parts[1:]:
        value = value + part[...]
    total[...] = value
    field = 0
    for ref in (centres_ref, shape_ref, opacity_ref, colours_ref):
        for row in range(ref.shape[0]):
            for k in range(GROUPS):
                at = field * GROUPS + k
                ref[row : row + 1, k * lanes : (k + 1) * lanes] = total[at : at + 1, :]
            field += 1


def monomials(pixels):
    side = math.isqrt(pixels)
    index = np.arange(pixels)
    x = (index % side) - (side - 1) / 2.0
    y = (index // side) - (side - 1) / 2.0
    one = np.ones_like(x)
    zero = np.zeros_like(x)
    group = np.stack([x * x, x * y, y * y, x, y, one, zero, zero])
    return jnp.asarray(np.concatenate([group, group, group, np.zeros_like(group)]), BF16)


def swap(array, axis, mask):
    size = lax.axis_size(axis)
    return lax.ppermute(array, axis, [(i, i ^ mask) for i in range(size)])


def shards(centres, shape_raw, opacity_logit, colours, camera, target, intersection_ids, depth_order, live_count):
    view_group = lax.axis_size("view")
    tile_group = lax.axis_size("tile")
    devices = view_group * tile_group
    chips = tile_group // 2
    own_count = centres.shape[1]
    lanes = own_count // GROUPS
    views, tiles_view, slots = intersection_ids.shape
    tiles = views * tiles_view
    pixels = target.shape[3]
    view_index = lax.axis_index("view")
    tile_index = lax.axis_index("tile")
    me = (view_index * tile_group + tile_index).astype(jnp.int32)

    totals = jnp.sum(live_count, axis=1)
    within = jnp.cumsum(live_count, axis=1) - live_count

    smem = pl.BlockSpec(memory_space=pltpu.SMEM)
    vmem = pl.BlockSpec(memory_space=pltpu.VMEM)
    prep = pl.pallas_call(
        partial(
            prep_kernel,
            (log2_of(own_count), log2_of(lanes), log2_of(view_group), log2_of(tile_group), tiles_view),
        ),
        out_shape=[
            jax.ShapeDtypeStruct((tiles + 8, slots), jnp.int32),
            jax.ShapeDtypeStruct((tiles, slots), jnp.int32),
            jax.ShapeDtypeStruct((views * 8,), F32),
        ],
        in_specs=[smem] * 3 + [vmem] * 3,
        out_specs=[vmem, vmem, smem],
        scratch_shapes=[
            pltpu.VMEM((3, tiles, slots), F32),
            pltpu.VMEM((tiles, slots), F32),
            pltpu.VMEM((tiles, slots), F32),
            pltpu.VMEM((UNROLL, 16, slots), F32),
            pltpu.VMEM((tiles, slots), jnp.int32),
            pltpu.VMEM((tiles, slots), F32),
        ],
        cost_estimate=pl.CostEstimate(flops=8_000_000_000, bytes_accessed=4 * tiles * slots * 4, transcendentals=0),
        name="prep",
    )

    kept = tiles_view // 2
    mirror = tile_group - 1
    live_row = jnp.pad(live_count[:, None, kept:], ((0, 0), (0, 7), (0, slots - kept)))
    theirs = jnp.concatenate([intersection_ids[:, kept:], depth_order[:, kept:], live_row], axis=1)

    fields = jnp.concatenate([centres, shape_raw, opacity_logit[None], colours], axis=0)
    block = fields.reshape(FIELDS * GROUPS, lanes)
    note = jnp.pad(totals.astype(F32)[None], ((0, 7), (0, lanes - views)))
    beyond = [swap(block, "view", m) for m in range(1, view_group)]
    level = [swap(block, "tile", 2 * m) for m in range(1, chips)]
    theirs = swap(theirs, "tile", mirror)
    beyond = jnp.concatenate(beyond + [note])
    beyond, theirs, *level = lax.optimization_barrier((beyond, theirs, *level))
    far = [swap(beyond, "tile", 2 * m) for m in range(1, chips)]
    mine = jnp.stack([jnp.concatenate([near, rest]) for near, rest in zip([block] + level, [beyond] + far)])
    live_now = jnp.concatenate([live_count[:, :kept], theirs[:, 2 * kept, :kept]], axis=1)
    rows, group, cam = prep(me[None], live_now, camera, intersection_ids, depth_order, theirs)
    mine, rows, group, cam = lax.optimization_barrier((mine, rows.reshape(-1), group, cam))
    target = target.transpose(0, 2, 1, 3)
    their_target = swap(target[:, :, kept:], "tile", mirror)
    other = swap(mine, "tile", 1)

    table_rows = devices * lanes
    square = (BATCH, slots, pixels)
    half = (chips * view_group, FIELDS * GROUPS, lanes)
    accs = ACCS if devices <= 32 else 2
    room = 4 * table_rows * lanes * (accs + 2) + 16 * 1024 * 1024
    splat = pl.pallas_call(
        partial(splat_kernel, (views, tiles_view, slots, pixels, lanes, view_group)),
        out_shape=[
            jax.ShapeDtypeStruct((views, 3, kept, pixels), F32),
            jax.ShapeDtypeStruct((views, 3, tiles_view - kept, pixels), F32),
            jax.ShapeDtypeStruct(half, F32),
            jax.ShapeDtypeStruct(half, F32),
        ],
        in_specs=[smem] * 3 + [vmem] * 6,
        out_specs=[vmem] * 4,
        scratch_shapes=[
            pltpu.VMEM((table_rows, lanes), F32),
            pltpu.VMEM((BATCH, slots, lanes), F32),
            pltpu.VMEM((FIELDS, tiles, slots), F32),
            pltpu.VMEM((9, tiles, slots), F32),
            pltpu.VMEM((9, tiles, slots), F32),
            pltpu.VMEM((FIELDS, tiles, slots), F32),
            pltpu.VMEM(square, F32),
            pltpu.VMEM(square, F32),
        ]
        + [pltpu.VMEM(square, BF16)] * 5
        + [pltpu.VMEM((BATCH, 16, slots), F32), pltpu.VMEM((BATCH, 8, pixels), F32)]
        + [pltpu.VMEM((views, 3, tiles_view, pixels), F32)] * 2
        + [pltpu.VMEM((table_rows, lanes), F32)] * accs,
        compiler_params=pltpu.CompilerParams(vmem_limit_bytes=room),
        name="splat",
    )
    image, their_image, grad_mine, grad_other = splat(
        cam,
        rows,
        live_now,
        group,
        mine,
        other,
        target,
        their_target,
        monomials(pixels),
    )

    whole = totals
    before = jnp.zeros_like(totals)
    for core, held in enumerate((mine, other)):
        for m in range(chips):
            mask = 2 * m + core
            if mask:
                theirs = held[m, view_group * FIELDS * GROUPS, 0:views].astype(jnp.int32)
                whole = whole + theirs
                before = before + jnp.where((tile_index ^ mask) < tile_index, theirs, 0)
    next_owner = (before[:, None] + within) * tile_group // whole[:, None]

    grad_other = swap(grad_other, "tile", 1)
    rendered = jnp.concatenate([image, swap(their_image, "tile", mirror)], axis=2)
    joined = (grad_mine + grad_other).reshape(chips, view_group, FIELDS * GROUPS, lanes)
    far = [swap(joined[m, 1:], "tile", 2 * m) for m in range(1, chips)]
    near = joined[:, 0]
    near, *far = lax.optimization_barrier((near, *far))
    beyond = joined[0, 1:]
    for part in far:
        beyond = beyond + part
    parts = [near[0]]
    parts += [swap(beyond[m - 1], "view", m) for m in range(1, view_group)]
    parts += [swap(near[m], "tile", 2 * m) for m in range(1, chips)]
    tail = pl.pallas_call(
        tail_kernel,
        out_shape=[jax.ShapeDtypeStruct((count, own_count), F32) for count in (3, 6, 1, 3)],
        in_specs=[vmem] * len(parts),
        out_specs=[vmem] * 4,
        scratch_shapes=[pltpu.VMEM((FIELDS * GROUPS, lanes), F32)],
        compiler_params=pltpu.CompilerParams(vmem_limit_bytes=8 * 1024 * 1024),
        name="tail",
    )
    grad_centres, grad_shape, grad_opacity, grad_colours = tail(*parts)
    return (
        rendered.transpose(0, 2, 1, 3),
        grad_centres,
        grad_shape,
        grad_opacity[0],
        grad_colours,
        next_owner,
    )


def solution(mesh):
    in_specs = (
        P(None, ("view", "tile")),
        P(None, ("view", "tile")),
        P(("view", "tile")),
        P(None, ("view", "tile")),
        P(),
        P("view", "tile", None, None),
        P("view", "tile", None),
        P("view", "tile", None),
        P("view", "tile"),
    )
    out_specs = (
        P("view", "tile", None, None),
        P(None, ("view", "tile")),
        P(None, ("view", "tile")),
        P(("view", "tile")),
        P(None, ("view", "tile")),
        P("view", "tile"),
    )
    return jax.shard_map(shards, mesh=mesh, in_specs=in_specs, out_specs=out_specs, check_vma=False)
```

```python
import functools
from functools import partial
import math

import jax
import jax.numpy as jnp
import numpy as np
from jax import lax
from jax.experimental import pallas as pl
from jax.experimental.pallas import tpu as pltpu
from jax.sharding import PartitionSpec as P

F32 = jnp.float32
BF16 = jnp.bfloat16
FIELDS = 13
GROUPS = 8
ACCS = 4
UNROLL = 4
BATCH = 4
LOG2E = math.log2(math.e)
OFF = -1e4


def log2_of(n):
    bits = n.bit_length() - 1
    assert n == 1 << bits
    return bits


def pieces_of(value, count):
    out = []
    rest = value
    for _ in range(count - 1):
        piece = rest.astype(BF16).astype(F32)
        out.append(piece)
        rest = rest - piece
    out.append(rest)
    return out


def dot_nn(a, b):
    return lax.dot_general(a, b, (((1,), (0,)), ((), ())), preferred_element_type=F32)


def dot_nt(a, b):
    return lax.dot_general(a, b, (((1,), (1,)), ((), ())), preferred_element_type=F32)


def dot_tn(a, b):
    return lax.dot_general(a, b, (((0,), (0,)), ((), ())), preferred_element_type=F32)


def chunk_rows(live):
    return (live + 7) >> 3


def repeat(count, step, body):
    many = lax.div(count, step)

    def trip(i, _):
        for u in range(step):
            body(i * step + u)
        return 0

    def single(i, _):
        body(i)
        return 0

    lax.fori_loop(0, many, trip, 0)
    lax.fori_loop(many * step, count, single, 0)


def place_slots(dims, me, live_at, ids, order, scratch):
    own_bits, lane_bits, view_bits, tile_bits = dims
    piece_ref, rho_ref, code_ref, lhs_ref, live_full, order_b = scratch
    tiles, slots = ids.shape
    for t in range(tiles):
        live_full[t : t + 1, :] = jnp.full((1, slots), live_at(t), jnp.int32)
    live = live_full[...]
    active = order < live
    upper = (
        lax.broadcasted_iota(jnp.int32, (slots, slots), 0)
        < lax.broadcasted_iota(jnp.int32, (slots, slots), 1)
    ).astype(F32).astype(BF16)
    place = dot_nn(active.astype(F32).astype(BF16), upper).astype(jnp.int32)
    rows = chunk_rows(live)
    chunk = jnp.zeros((tiles, slots), jnp.int32)
    for m in range(1, GROUPS):
        chunk = chunk + (place >= m * rows).astype(jnp.int32)
    rho_ref[...] = jnp.where(active, (place - chunk * rows) * GROUPS + chunk, -1).astype(F32)
    order_b[...] = order.astype(F32)
    owner = (ids >> own_bits) ^ me
    local = ids & ((1 << own_bits) - 1)
    xy_bits = tile_bits - 1
    core = owner & 1
    chip = (owner >> 1) & ((1 << xy_bits) - 1)
    view = owner >> tile_bits
    block = (((core << xy_bits) | chip) << view_bits) | view
    row = (block << lane_bits) | (local & ((1 << lane_bits) - 1))
    code = (row << 3) | (local >> lane_bits)
    piece_ref[0] = (code & 255).astype(F32)
    piece_ref[1] = ((code >> 8) & 255).astype(F32)
    piece_ref[2] = (code >> 16).astype(F32)
    lhs_ref[...] = jnp.zeros_like(lhs_ref)
    down = lax.broadcasted_iota(jnp.int32, (slots, slots), 0).astype(F32).astype(BF16)
    one = jnp.ones((slots, slots), BF16)
    nil = jnp.zeros((slots, slots), BF16)

    def some_tiles(s, _):
        for u in range(UNROLL):
            t = s * UNROLL + u
            for p in range(3):
                lhs_ref[u, p : p + 1, :] = piece_ref[p, pl.ds(t, 1), :]
            picked = jnp.where(down == order_b[pl.ds(t, 1), :].astype(BF16), one, nil)
            ordered = dot_nn(lhs_ref[u].astype(BF16), picked)
            placed = jnp.where(down == rho_ref[pl.ds(t, 1), :].astype(BF16), one, nil)
            out = dot_nt(ordered.astype(BF16), placed)
            code_ref[pl.ds(t, 1), :] = out[0:1] + 256.0 * out[1:2] + 65536.0 * out[2:3]
        return 0

    lax.fori_loop(0, tiles // UNROLL, some_tiles, 0)
    codes = code_ref[...].astype(jnp.int32)
    pos = lax.broadcasted_iota(jnp.int32, (tiles, slots), 1)
    here = (pos >> 3 < rows) & ((pos & 7) * rows + (pos >> 3) < live)
    return codes >> 3, jnp.where(here, codes & 7, GROUPS)


def prep_own_kernel(dims, me_ref, live_ref, camera_ref, ids_ref, order_ref, row_ref, group_ref, cam_ref, *scratch):
    views, tiles_view, _ = ids_ref.shape
    kept = tiles_view // 2
    me = me_ref[0]
    first = (me >> dims[3]) * views
    for v in range(views):
        for i in range(2):
            for j in range(4):
                cam_ref[v * 8 + i * 4 + j] = camera_ref[first + v, i, j]
    ids = jnp.concatenate([ids_ref[v, 0:kept, :] for v in range(views)], axis=0)
    order = jnp.concatenate([order_ref[v, 0:kept, :] for v in range(views)], axis=0)
    live_at = lambda t: live_ref[t // kept, t % kept]
    row_ref[...], group_ref[...] = place_slots(dims, me, live_at, ids, order, scratch)


def prep_their_kernel(dims, me_ref, live_ref, message_ref, row_ref, group_ref, *scratch):
    tiles, slots = group_ref.shape
    total = live_ref.shape[0]
    ids = message_ref[0:tiles, :].astype(jnp.int32)
    order = message_ref[tiles : 2 * tiles, :].astype(jnp.int32)
    live_at = lambda t: live_ref[total - tiles + t]
    row_ref[0:tiles, :], group_ref[...] = place_slots(dims, me_ref[0], live_at, ids, order, scratch)
    lane = lax.broadcasted_iota(jnp.int32, (total, slots), 1)
    above = lax.broadcasted_iota(jnp.int32, (total, slots), 0)
    across = jnp.full((total, slots), -1, jnp.int32)
    down = jnp.zeros((total, slots), jnp.int32)
    for t in range(total):
        across = jnp.where(lane == t, live_ref[t], across)
        down = jnp.where(above == t, live_ref[t], down)
    ahead = (across > down) | ((across == down) & (lane < above))
    rank = jnp.sum(ahead.astype(jnp.int32), axis=1, keepdims=True)
    ranked = jnp.sum(jnp.where(rank == lane, above, 0), axis=0, keepdims=True)
    large = jnp.sum((across > slots // 2).astype(jnp.int32), axis=1, keepdims=True)[0:1]
    row_ref[tiles : tiles + 1, :] = jnp.where(lane[0:1] == total, large, ranked)


def splat_kernel(
    dims,
    cam_ref,
    row_ref,
    live_ref,
    own_group_ref,
    their_group_ref,
    mine_ref,
    other_ref,
    target_ref,
    message_ref,
    mono_ref,
    image_ref,
    their_image_ref,
    grad_mine_ref,
    grad_other_ref,
    *scratch,
):
    views, tiles_view, slots, pixels, lanes, column = dims
    table, buf, raw, rec, mom, grad, c_s, h_s, w_hi, w_lo, g_1, g_2, g_3, row_s, row_2, want, got, group_ref = scratch[:18]
    accs = scratch[18:]
    tiles = views * tiles_view
    chips = mine_ref.shape[0]
    half = chips * column
    used = FIELDS * GROUPS
    pad = jnp.zeros((lanes - used, lanes), F32)

    for acc in accs:
        acc[...] = jnp.zeros_like(acc)
    for ref in (buf, w_hi, w_lo, g_1, g_2, g_3, row_s, row_2):
        ref[...] = jnp.zeros_like(ref)

    kept = tiles_view // 2
    part_tiles = views * kept
    for v in range(views):
        for c in range(3):
            want[v, c, :, :] = target_ref[v, c, 0:kept, :]
            start = 2 * part_tiles + (v * 3 + c) * kept
            want[views + v, c, :, :] = message_ref[start : start + kept, :]
    group_ref[0:part_tiles, :] = own_group_ref[...]
    group_ref[part_tiles:, :] = their_group_ref[...]

    def build(q, _):
        for base, ref in ((0, mine_ref), (half, other_ref)):
            for d in range(column):
                block = jnp.concatenate([ref[q, d * used : (d + 1) * used, :], pad], axis=0)
                start = pl.multiple_of((base + q * column + d) * lanes, lanes)
                table[pl.ds(start, lanes), :] = jnp.transpose(block)
        return 0

    lax.fori_loop(0, chips, build, 0)

    def live_of(t):
        return live_ref[t]

    def in_turn(body):
        def trip(s, _, positions):
            body([row_ref[tiles * slots + s * BATCH + g] for g in range(BATCH)], positions)
            return 0

        large = lax.div(row_ref[tiles * slots + tiles] + (BATCH - 1), BATCH)
        lax.fori_loop(0, large, partial(trip, positions=slots), 0)
        lax.fori_loop(large, tiles // BATCH, partial(trip, positions=slots // 2), 0)

    sub = lax.broadcasted_iota(jnp.int32, (GROUPS, slots), 0)

    def widen(row):
        spare = slots - row.shape[1]
        return jnp.concatenate([row, jnp.zeros((1, spare), F32)], axis=1) if spare else row

    def fetch(tile, positions):
        for g, t in enumerate(tile):

            def copy(i, t=t, g=g):
                for k in range(GROUPS):
                    buf[g, pl.ds(i * GROUPS + k, 1), :] = table[pl.ds(row_ref[t * slots + i * GROUPS + k], 1), :]

            repeat(chunk_rows(live_of(t)), 4, copy)
        for g, t in enumerate(tile):
            turned = jnp.transpose(buf[g, 0:positions, :])
            mine = sub[:, 0:positions] == group_ref[pl.ds(t, 1), :][:, 0:positions]
            for f in range(FIELDS):
                part = jnp.where(mine, turned[f * GROUPS : (f + 1) * GROUPS], 0.0)
                raw[f, pl.ds(t, 1), :] = widen(jnp.sum(part, axis=0, keepdims=True))

    in_turn(fetch)

    def project(v):
        block = slice(v * kept, (v + 1) * kept)
        cam = [cam_ref[v % views * 8 + n] for n in range(8)]
        field = lambda f: raw[f, block, :]
        u = cam[0] * field(0) + cam[1] * field(1) + cam[2] * field(2) + cam[3]
        w = cam[4] * field(0) + cam[5] * field(1) + cam[6] * field(2) + cam[7]
        d0, d1, d2 = jnp.exp(field(3)), jnp.exp(field(5)), jnp.exp(field(8))
        factor = []
        for i in range(2):
            m = cam[4 * i : 4 * i + 3]
            factor.append(
                (
                    m[0] * d0 + m[1] * field(4) + m[2] * field(6),
                    m[1] * d1 + m[2] * field(7),
                    m[2] * d2,
                )
            )
        f0, f1 = factor
        s00 = f0[0] * f0[0] + f0[1] * f0[1] + f0[2] * f0[2] + 0.3
        s01 = f0[0] * f1[0] + f0[1] * f1[1] + f0[2] * f1[2]
        s11 = f1[0] * f1[0] + f1[1] * f1[1] + f1[2] * f1[2] + 0.3
        inverse = 1.0 / (s00 * s11 - s01 * s01)
        conic = (s11 * inverse, -s01 * inverse, s00 * inverse)
        here = group_ref[block, :] < GROUPS
        return here, cam, block, u, w, (d0, d1, d2), f0, f1, conic

    for v in range(2 * views):
        here, cam, block, u, w, _, _, _, (ka, kb, kc) = project(v)
        x_line = ka * u + kb * w
        y_line = kb * u + kc * w
        log_opacity = math.log(0.95) - jnp.log(1.0 + jnp.exp(-raw[9, block, :]))
        level = log_opacity - 0.5 * (u * x_line + w * y_line)
        terms = (-0.5 * ka, -kb, -0.5 * kc, x_line, y_line)
        for n, term in enumerate(terms):
            rec[n, block, :] = jnp.where(here, term * LOG2E, 0.0)
        rec[5, block, :] = jnp.where(here, level * LOG2E, OFF)
        for c in range(3):
            rec[6 + c, block, :] = raw[10 + c, block, :]

    lane_row = lax.broadcasted_iota(jnp.int32, (GROUPS, pixels), 0)
    own_chunk = (lax.broadcasted_iota(jnp.int32, (GROUPS, slots), 1) & 7) == sub
    zero_pix = jnp.zeros((8, pixels), F32)

    def paired(a, b):
        return a + pltpu.roll(b, 3, 0)

    def render(tile, positions):
        zero_rows = jnp.zeros((8, positions), F32)
        used = slice(0, positions)
        blocks = (chunk_rows(functools.reduce(jnp.maximum, [live_of(t) for t in tile])) + 3) >> 2
        for g, t in enumerate(tile):
            for n in range(6):
                row_s[g, n : n + 1, :] = rec[n, pl.ds(t, 1), :]
            for c in range(3):
                row_s[g, 8 + c : 9 + c, :] = rec[6 + c, pl.ds(t, 1), :]
        for g in range(BATCH):
            lhs = jnp.concatenate(pieces_of(row_s[g, 0:8, used], 3) + [zero_rows], axis=0).astype(BF16)
            c_s[g, used, :] = dot_tn(lhs, mono_ref[...])
        colour = [pieces_of(row_s[g, 8:16, used], 3) for g in range(BATCH)]

        def through(i, prods):
            rows = pl.ds(pl.multiple_of(i * 32, 32), 32)
            out = []
            for g in range(BATCH):
                cover = jnp.exp2(c_s[g, rows, :])
                c_s[g, rows, :] = cover
                keep = 1.0 - cover
                out.append(prods[g] * ((keep[0:8] * keep[8:16]) * (keep[16:24] * keep[24:32])))
            return tuple(out)

        ones = jnp.ones((GROUPS, pixels), F32)
        lead = list(lax.fori_loop(0, blocks, through, (ones,) * BATCH))
        for g in range(BATCH):
            scan = lead[g]
            for step in (1, 2, 4):
                scan = scan * jnp.where(lane_row >= step, pltpu.roll(scan, step, 0), 1.0)
            lead[g] = jnp.where(lane_row >= 1, pltpu.roll(scan, 1, 0), 1.0)

        def weights(cover, prod):
            out = []
            for h in range(4):
                weight = prod * cover[8 * h : 8 * h + 8]
                prod = prod - weight
                out.append(weight)
            return out, prod

        def weigh(i, prods):
            rows = pl.ds(pl.multiple_of(i * 32, 32), 32)
            out = []
            for g in range(BATCH):
                parts, prod = weights(c_s[g, rows, :], prods[g])
                weight = jnp.concatenate(parts, axis=0)
                high = weight.astype(BF16)
                w_hi[g, rows, :] = high
                w_lo[g, rows, :] = (weight - high.astype(F32)).astype(BF16)
                out.append(prod)
            return tuple(out)

        lax.fori_loop(0, blocks, weigh, tuple(lead))

        after = []
        for g, t in enumerate(tile):
            v, tl = lax.div(t, kept), lax.rem(t, kept)
            spread = [
                jnp.where(own_chunk[:, used], jnp.broadcast_to(piece[c : c + 1], (GROUPS, positions)), 0.0)
                for c in range(3)
                for piece in colour[g]
            ]
            lhs = jnp.concatenate(spread + [zero_rows], axis=0).astype(BF16)
            image = dot_nn(lhs, w_hi[g, used, :]) + dot_nn(lhs, w_lo[g, used, :])
            rest = jnp.zeros((GROUPS, pixels), F32)
            for c in range(3):
                part = image[24 * c : 24 * c + 8] + image[24 * c + 8 : 24 * c + 16] + image[24 * c + 16 : 24 * c + 24]
                whole = jnp.sum(part, axis=0, keepdims=True)
                got[v, c, pl.ds(tl, 1), :] = whole
                miss = whole - want[v, c, pl.ds(tl, 1), :]
                row_2[g, c : c + 1, :] = miss
                rest = rest + part * miss
            for step in (1, 2, 4):
                rest = rest + jnp.where(lane_row < GROUPS - step, pltpu.roll(rest, GROUPS - step, 0), 0.0)
            after.append(rest)
        missed = [pieces_of(row_2[g], 3) for g in range(BATCH)]
        for g in range(BATCH):
            c1, c2, c3 = colour[g]
            m1, m2, m3 = missed[g]
            lhs = jnp.concatenate([paired(c1, c1), paired(c2, c1), paired(c2, c3), zero_rows], axis=0)
            rhs = jnp.concatenate([paired(m1, m2), paired(m1, m3), paired(m2, m1), zero_pix], axis=0)
            h_s[g, used, :] = dot_tn(lhs.astype(BF16), rhs.astype(BF16))

        def settle(i, carry):
            rows = pl.ds(pl.multiple_of(i * 32, 32), 32)
            out = []
            for g in range(BATCH):
                prod, tail = carry[g]
                cover = c_s[g, rows, :]
                pull = h_s[g, rows, :]
                parts, prod = weights(cover, prod)
                ratio = cover / (1.0 - cover)
                slopes = []
                for h in range(4):
                    cut = slice(8 * h, 8 * h + 8)
                    part = parts[h] * pull[cut]
                    tail = tail - part
                    slopes.append(part - ratio[cut] * tail)
                slope = jnp.concatenate(slopes, axis=0)
                high = slope.astype(BF16)
                rest = slope - high.astype(F32)
                middle = rest.astype(BF16)
                g_1[g, rows, :] = high
                g_2[g, rows, :] = middle
                g_3[g, rows, :] = (rest - middle.astype(F32)).astype(BF16)
                out.append((prod, tail))
            return tuple(out)

        lax.fori_loop(0, blocks, settle, tuple(zip(lead, after)))
        mono = mono_ref[0:16, :]
        for g in range(BATCH):
            moments = dot_nt(mono, g_1[g, used, :]) + dot_nt(mono, g_2[g, used, :]) + dot_nt(mono, g_3[g, used, :])
            miss_lhs = jnp.concatenate(missed[g] + [zero_pix], axis=0).astype(BF16)
            tint = dot_nt(miss_lhs, w_hi[g, used, :]) + dot_nt(miss_lhs, w_lo[g, used, :])
            row_s[g, 0:8, used] = moments[0:8]
            row_s[g, 8:16, used] = tint[0:8] + tint[8:16] + tint[16:24]
        for g, t in enumerate(tile):
            for n in range(6):
                mom[n, pl.ds(t, 1), :] = row_s[g, n : n + 1, :]
            for c in range(3):
                mom[6 + c, pl.ds(t, 1), :] = row_s[g, 8 + c : 9 + c, :]

    in_turn(render)
    image_ref[...] = got[0:views]
    their_image_ref[...] = got[views:]

    for v in range(2 * views):
        here, cam, block, u, w, (d0, d1, d2), f0, f1, (ka, kb, kc) = project(v)
        mxx, mxy, myy, mx, my, m1 = [jnp.where(here, mom[n, block, :], 0.0) for n in range(6)]
        dx = mx - u * m1
        dy = my - w * m1
        dxx = mxx - 2.0 * u * mx + u * u * m1
        dxy = mxy - u * my - w * mx + u * w * m1
        dyy = myy - 2.0 * w * my + w * w * m1
        gu = ka * dx + kb * dy
        gw = kb * dx + kc * dy
        ax, ay = ka * dxx + kb * dxy, ka * dxy + kb * dyy
        bx, by = kb * dxx + kc * dxy, kb * dxy + kc * dyy
        h00 = ax * ka + ay * kb
        h01 = ax * kb + ay * kc
        h11 = bx * kb + by * kc
        g0 = [h00 * f0[j] + h01 * f1[j] for j in range(3)]
        g1 = [h01 * f0[j] + h11 * f1[j] for j in range(3)]
        for k in range(3):
            grad[k, block, :] = cam[k] * gu + cam[4 + k] * gw
        grad[3, block, :] = (cam[0] * g0[0] + cam[4] * g1[0]) * d0
        grad[4, block, :] = cam[1] * g0[0] + cam[5] * g1[0]
        grad[5, block, :] = (cam[1] * g0[1] + cam[5] * g1[1]) * d1
        grad[6, block, :] = cam[2] * g0[0] + cam[6] * g1[0]
        grad[7, block, :] = cam[2] * g0[1] + cam[6] * g1[1]
        grad[8, block, :] = (cam[2] * g0[2] + cam[6] * g1[2]) * d2
        grad[9, block, :] = m1 - m1 / (1.0 + jnp.exp(-raw[9, block, :]))
        for c in range(3):
            grad[10 + c, block, :] = mom[6 + c, block, :]

    def give(tile, positions):
        for g, t in enumerate(tile):
            mine = sub[:, 0:positions] == group_ref[pl.ds(t, 1), :][:, 0:positions]
            spread = [
                jnp.where(mine, jnp.broadcast_to(grad[f, pl.ds(t, 1), :][:, 0:positions], (GROUPS, positions)), 0.0)
                for f in range(FIELDS)
            ]
            spread.append(jnp.zeros((lanes - used, positions), F32))
            buf[g, 0:positions, :] = jnp.transpose(jnp.concatenate(spread, axis=0))
        for g, t in enumerate(tile):

            def add(i, t=t, g=g):
                for k in range(0, GROUPS, len(accs)):
                    where = [row_ref[t * slots + i * GROUPS + k + n] for n in range(len(accs))]
                    olds = [accs[n][pl.ds(where[n], 1), :] for n in range(len(accs))]
                    news = [buf[g, pl.ds(i * GROUPS + k + n, 1), :] for n in range(len(accs))]
                    for n in range(len(accs)):
                        accs[n][pl.ds(where[n], 1), :] = olds[n] + news[n]

            repeat(chunk_rows(live_of(t)), 4, add)

    in_turn(give)

    def finish(d, _):
        for base, ref in ((0, grad_mine_ref), (half, grad_other_ref)):
            start = pl.multiple_of((base + d) * lanes, lanes)
            total = accs[0][pl.ds(start, lanes), :]
            for acc in accs[1:]:
                total = total + acc[pl.ds(start, lanes), :]
            ref[d] = jnp.transpose(total)[0:used]
        return 0

    lax.fori_loop(0, half, finish, 0)


def tail_kernel(*refs):
    parts, (centres_ref, shape_ref, opacity_ref, colours_ref), total = refs[:-5], refs[-5:-1], refs[-1]
    lanes = total.shape[1]
    value = parts[0][...]
    for part in parts[1:]:
        value = value + part[...]
    total[...] = value
    field = 0
    for ref in (centres_ref, shape_ref, opacity_ref, colours_ref):
        for row in range(ref.shape[0]):
            for k in range(GROUPS):
                at = field * GROUPS + k
                ref[row : row + 1, k * lanes : (k + 1) * lanes] = total[at : at + 1, :]
            field += 1


def monomials(pixels):
    side = math.isqrt(pixels)
    index = np.arange(pixels)
    x = (index % side) - (side - 1) / 2.0
    y = (index // side) - (side - 1) / 2.0
    one = np.ones_like(x)
    zero = np.zeros_like(x)
    group = np.stack([x * x, x * y, y * y, x, y, one, zero, zero])
    return jnp.asarray(np.concatenate([group, group, group, np.zeros_like(group)]), BF16)


def swap(array, axis, mask):
    size = lax.axis_size(axis)
    return lax.ppermute(array, axis, [(i, i ^ mask) for i in range(size)])


def shards(centres, shape_raw, opacity_logit, colours, camera, target, intersection_ids, depth_order, live_count):
    view_group = lax.axis_size("view")
    tile_group = lax.axis_size("tile")
    devices = view_group * tile_group
    chips = tile_group // 2
    own_count = centres.shape[1]
    lanes = own_count // GROUPS
    views, tiles_view, slots = intersection_ids.shape
    tiles = views * tiles_view
    pixels = target.shape[3]
    view_index = lax.axis_index("view")
    tile_index = lax.axis_index("tile")
    me = (view_index * tile_group + tile_index).astype(jnp.int32)

    totals = jnp.sum(live_count, axis=1)
    within = jnp.cumsum(live_count, axis=1) - live_count

    smem = pl.BlockSpec(memory_space=pltpu.SMEM)
    vmem = pl.BlockSpec(memory_space=pltpu.VMEM)
    kept = tiles_view // 2
    part_tiles = views * kept
    dims = (log2_of(own_count), log2_of(lanes), log2_of(view_group), log2_of(tile_group))
    prep_options = dict(
        scratch_shapes=[
            pltpu.VMEM((3, part_tiles, slots), F32),
            pltpu.VMEM((part_tiles, slots), F32),
            pltpu.VMEM((part_tiles, slots), F32),
            pltpu.VMEM((UNROLL, 16, slots), F32),
            pltpu.VMEM((part_tiles, slots), jnp.int32),
            pltpu.VMEM((part_tiles, slots), F32),
        ],
        compiler_params=pltpu.CompilerParams(vmem_limit_bytes=8 * 1024 * 1024),
        cost_estimate=pl.CostEstimate(flops=4_000_000_000, bytes_accessed=8 * tiles * slots, transcendentals=0),
    )
    prep_own = pl.pallas_call(
        partial(prep_own_kernel, dims),
        out_shape=[
            jax.ShapeDtypeStruct((part_tiles, slots), jnp.int32),
            jax.ShapeDtypeStruct((part_tiles, slots), jnp.int32),
            jax.ShapeDtypeStruct((views * 8,), F32),
        ],
        in_specs=[smem] * 3 + [vmem] * 2,
        out_specs=[vmem, vmem, smem],
        name="prep_own",
        **prep_options,
    )
    prep_their = pl.pallas_call(
        partial(prep_their_kernel, dims),
        out_shape=[
            jax.ShapeDtypeStruct((part_tiles + 8, slots), jnp.int32),
            jax.ShapeDtypeStruct((part_tiles, slots), jnp.int32),
        ],
        in_specs=[smem] * 2 + [vmem],
        out_specs=[vmem] * 2,
        name="prep_their",
        **prep_options,
    )

    mirror = tile_group - 1
    target = target.transpose(0, 2, 1, 3)
    message = jnp.concatenate(
        [
            intersection_ids[:, kept:].reshape(part_tiles, slots).astype(F32),
            depth_order[:, kept:].reshape(part_tiles, slots).astype(F32),
            target[:, :, kept:].reshape(3 * part_tiles, pixels),
            jnp.pad(live_count[:, kept:].astype(F32), ((0, 8 - views), (0, slots - kept))),
        ]
    )
    fields = jnp.concatenate([centres, shape_raw, opacity_logit[None], colours], axis=0)
    block = fields.reshape(FIELDS * GROUPS, lanes)
    note = jnp.pad(totals.astype(F32)[None], ((0, 7), (0, lanes - views)))
    column = jnp.concatenate([block] + [swap(block, "view", m) for m in range(1, view_group)] + [note])
    message = swap(message, "tile", mirror)
    own_rows, own_group, cam = prep_own(me[None], live_count, camera, intersection_ids, depth_order)
    column, own_rows, own_group, cam = lax.optimization_barrier((column, own_rows, own_group, cam))
    mine = jnp.stack([column] + [swap(column, "tile", 2 * m) for m in range(1, chips)])
    their_live = message[5 * part_tiles : 5 * part_tiles + views, :kept].astype(jnp.int32)
    live_now = jnp.concatenate([live_count[:, :kept].reshape(-1), their_live.reshape(-1)])
    their_rows, their_group = prep_their(me[None], live_now, message)
    rows = jnp.concatenate([own_rows, their_rows]).reshape(-1)
    mine, rows, their_group = lax.optimization_barrier((mine, rows, their_group))
    other = swap(mine, "tile", 1)

    table_rows = devices * lanes
    square = (BATCH, slots, pixels)
    half = (chips * view_group, FIELDS * GROUPS, lanes)
    accs = ACCS if devices <= 32 else 2
    room = 4 * table_rows * lanes * (accs + 2) + 16 * 1024 * 1024
    splat = pl.pallas_call(
        partial(splat_kernel, (views, tiles_view, slots, pixels, lanes, view_group)),
        out_shape=[
            jax.ShapeDtypeStruct((views, 3, kept, pixels), F32),
            jax.ShapeDtypeStruct((views, 3, tiles_view - kept, pixels), F32),
            jax.ShapeDtypeStruct(half, F32),
            jax.ShapeDtypeStruct(half, F32),
        ],
        in_specs=[smem] * 3 + [vmem] * 7,
        out_specs=[vmem] * 4,
        scratch_shapes=[
            pltpu.VMEM((table_rows, lanes), F32),
            pltpu.VMEM((BATCH, slots, lanes), F32),
            pltpu.VMEM((FIELDS, tiles, slots), F32),
            pltpu.VMEM((9, tiles, slots), F32),
            pltpu.VMEM((9, tiles, slots), F32),
            pltpu.VMEM((FIELDS, tiles, slots), F32),
            pltpu.VMEM(square, F32),
            pltpu.VMEM(square, F32),
        ]
        + [pltpu.VMEM(square, BF16)] * 5
        + [pltpu.VMEM((BATCH, 16, slots), F32), pltpu.VMEM((BATCH, 8, pixels), F32)]
        + [pltpu.VMEM((2 * views, 3, kept, pixels), F32)] * 2
        + [pltpu.VMEM((tiles, slots), jnp.int32)]
        + [pltpu.VMEM((table_rows, lanes), F32)] * accs,
        compiler_params=pltpu.CompilerParams(vmem_limit_bytes=room),
        name="splat",
    )
    image, their_image, grad_mine, grad_other = splat(
        cam,
        rows,
        live_now,
        own_group,
        their_group,
        mine,
        other,
        target,
        message,
        monomials(pixels),
    )

    whole = totals
    before = jnp.zeros_like(totals)
    for core, held in enumerate((mine, other)):
        for m in range(chips):
            mask = 2 * m + core
            if mask:
                theirs = held[m, view_group * FIELDS * GROUPS, 0:views].astype(jnp.int32)
                whole = whole + theirs
                before = before + jnp.where((tile_index ^ mask) < tile_index, theirs, 0)
    next_owner = (before[:, None] + within) * tile_group // whole[:, None]

    grad_other = swap(grad_other, "tile", 1)
    rendered = jnp.concatenate([image, swap(their_image, "tile", mirror)], axis=2)
    joined = (grad_mine + grad_other).reshape(chips, view_group, FIELDS * GROUPS, lanes)
    part = joined[0]
    for m in range(1, chips):
        part = part + swap(joined[m], "tile", 2 * m)
    parts = [part[0]] + [swap(part[m], "view", m) for m in range(1, view_group)]
    tail = pl.pallas_call(
        tail_kernel,
        out_shape=[jax.ShapeDtypeStruct((count, own_count), F32) for count in (3, 6, 1, 3)],
        in_specs=[vmem] * len(parts),
        out_specs=[vmem] * 4,
        scratch_shapes=[pltpu.VMEM((FIELDS * GROUPS, lanes), F32)],
        compiler_params=pltpu.CompilerParams(vmem_limit_bytes=8 * 1024 * 1024),
        name="tail",
    )
    grad_centres, grad_shape, grad_opacity, grad_colours = tail(*parts)
    return (
        rendered.transpose(0, 2, 1, 3),
        grad_centres,
        grad_shape,
        grad_opacity[0],
        grad_colours,
        next_owner,
    )


def solution(mesh):
    in_specs = (
        P(None, ("view", "tile")),
        P(None, ("view", "tile")),
        P(("view", "tile")),
        P(None, ("view", "tile")),
        P(),
        P("view", "tile", None, None),
        P("view", "tile", None),
        P("view", "tile", None),
        P("view", "tile"),
    )
    out_specs = (
        P("view", "tile", None, None),
        P(None, ("view", "tile")),
        P(None, ("view", "tile")),
        P(("view", "tile")),
        P(None, ("view", "tile")),
        P("view", "tile"),
    )
    return jax.shard_map(shards, mesh=mesh, in_specs=in_specs, out_specs=out_specs, check_vma=False)
```

```python
import functools
from functools import partial
import math

import jax
import jax.numpy as jnp
import numpy as np
from jax import lax
from jax.experimental import pallas as pl
from jax.experimental.pallas import tpu as pltpu
from jax.sharding import PartitionSpec as P

F32 = jnp.float32
BF16 = jnp.bfloat16
FIELDS = 13
GROUPS = 8
ACCS = 4
UNROLL = 8
SIZES = 3
BATCH = 8
LOG2E = math.log2(math.e)
OFF = -1e4


def log2_of(n):
    bits = n.bit_length() - 1
    assert n == 1 << bits
    return bits


def pieces_of(value, count):
    out = []
    rest = value
    for _ in range(count - 1):
        piece = rest.astype(BF16).astype(F32)
        out.append(piece)
        rest = rest - piece
    out.append(rest)
    return out


def dot_nn(a, b):
    return lax.dot_general(a, b, (((1,), (0,)), ((), ())), preferred_element_type=F32)


def dot_nt(a, b):
    return lax.dot_general(a, b, (((1,), (1,)), ((), ())), preferred_element_type=F32)


def dot_tn(a, b):
    return lax.dot_general(a, b, (((0,), (0,)), ((), ())), preferred_element_type=F32)


def chunk_rows(live):
    return (live + 7) >> 3


def repeat(count, step, body):
    many = lax.div(count, step)

    def trip(i, _):
        for u in range(step):
            body(i * step + u)
        return 0

    def single(i, _):
        body(i)
        return 0

    lax.fori_loop(0, many, trip, 0)
    lax.fori_loop(many * step, count, single, 0)


def place_slots(dims, me, live_at, ids, order, scratch):
    own_bits, lane_bits, view_bits, tile_bits = dims
    piece_ref, rho_ref, code_ref, lhs_ref, live_full, order_b = scratch
    tiles, slots = ids.shape
    for t in range(tiles):
        live_full[t : t + 1, :] = jnp.full((1, slots), live_at(t), jnp.int32)
    live = live_full[...]
    active = order < live
    upper = (
        lax.broadcasted_iota(jnp.int32, (slots, slots), 0)
        < lax.broadcasted_iota(jnp.int32, (slots, slots), 1)
    ).astype(F32).astype(BF16)
    place = dot_nn(active.astype(F32).astype(BF16), upper).astype(jnp.int32)
    rows = chunk_rows(live)
    chunk = jnp.zeros((tiles, slots), jnp.int32)
    for m in range(1, GROUPS):
        chunk = chunk + (place >= m * rows).astype(jnp.int32)
    rho_ref[...] = jnp.where(active, (place - chunk * rows) * GROUPS + chunk, -1).astype(F32)
    order_b[...] = order.astype(F32)
    owner = (ids >> own_bits) ^ me
    local = ids & ((1 << own_bits) - 1)
    xy_bits = tile_bits - 1
    core = owner & 1
    chip = (owner >> 1) & ((1 << xy_bits) - 1)
    view = owner >> tile_bits
    block = (((core << xy_bits) | chip) << view_bits) | view
    row = (block << lane_bits) | (local & ((1 << lane_bits) - 1))
    code = (row << 3) | (local >> lane_bits)
    piece_ref[0] = (code & 255).astype(F32)
    piece_ref[1] = ((code >> 8) & 255).astype(F32)
    piece_ref[2] = (code >> 16).astype(F32)
    lhs_ref[...] = jnp.zeros_like(lhs_ref)
    down = lax.broadcasted_iota(jnp.int32, (slots, slots), 0).astype(F32).astype(BF16)
    one = jnp.ones((slots, slots), BF16)
    nil = jnp.zeros((slots, slots), BF16)

    def some_tiles(s, _):
        for u in range(UNROLL):
            t = s * UNROLL + u
            for p in range(3):
                lhs_ref[u, p : p + 1, :] = piece_ref[p, pl.ds(t, 1), :]
            picked = jnp.where(down == order_b[pl.ds(t, 1), :].astype(BF16), one, nil)
            ordered = dot_nn(lhs_ref[u].astype(BF16), picked)
            placed = jnp.where(down == rho_ref[pl.ds(t, 1), :].astype(BF16), one, nil)
            out = dot_nt(ordered.astype(BF16), placed)
            code_ref[pl.ds(t, 1), :] = out[0:1] + 256.0 * out[1:2] + 65536.0 * out[2:3]
        return 0

    lax.fori_loop(0, tiles // UNROLL, some_tiles, 0)
    codes = code_ref[...].astype(jnp.int32)
    pos = lax.broadcasted_iota(jnp.int32, (tiles, slots), 1)
    here = (pos >> 3 < rows) & ((pos & 7) * rows + (pos >> 3) < live)
    return codes >> 3, jnp.where(here, codes & 7, GROUPS)


def prep_own_kernel(dims, me_ref, live_ref, camera_ref, ids_ref, order_ref, row_ref, group_ref, cam_ref, *scratch):
    views, tiles_view, _ = ids_ref.shape
    kept = tiles_view // 2
    me = me_ref[0]
    first = (me >> dims[3]) * views
    for v in range(views):
        for i in range(2):
            for j in range(4):
                cam_ref[v * 8 + i * 4 + j] = camera_ref[first + v, i, j]
    ids = jnp.concatenate([ids_ref[v, 0:kept, :] for v in range(views)], axis=0)
    order = jnp.concatenate([order_ref[v, 0:kept, :] for v in range(views)], axis=0)
    live_at = lambda t: live_ref[t // kept, t % kept]
    row_ref[...], group_ref[...] = place_slots(dims, me, live_at, ids, order, scratch)


def prep_their_kernel(dims, me_ref, live_ref, message_ref, row_ref, group_ref, *scratch):
    tiles, slots = group_ref.shape
    total = live_ref.shape[0]
    ids = message_ref[0:tiles, :].astype(jnp.int32)
    order = message_ref[tiles : 2 * tiles, :].astype(jnp.int32)
    live_at = lambda t: live_ref[total - tiles + t]
    row_ref[0:tiles, :], group_ref[...] = place_slots(dims, me_ref[0], live_at, ids, order, scratch)
    lane = lax.broadcasted_iota(jnp.int32, (total, slots), 1)
    above = lax.broadcasted_iota(jnp.int32, (total, slots), 0)
    across = jnp.full((total, slots), -1, jnp.int32)
    down = jnp.zeros((total, slots), jnp.int32)
    for t in range(total):
        across = jnp.where(lane == t, live_ref[t], across)
        down = jnp.where(above == t, live_ref[t], down)
    ahead = (across > down) | ((across == down) & (lane < above))
    rank = jnp.sum(ahead.astype(jnp.int32), axis=1, keepdims=True)
    ranked = jnp.sum(jnp.where(rank == lane, above, 0), axis=0, keepdims=True)
    for n in range(1, SIZES):
        over = jnp.sum((across > slots >> n).astype(jnp.int32), axis=1, keepdims=True)[0:1]
        ranked = jnp.where(lane[0:1] == total + n - 1, over, ranked)
    row_ref[tiles : tiles + 1, :] = ranked


def splat_kernel(
    dims,
    cam_ref,
    row_ref,
    live_ref,
    own_group_ref,
    their_group_ref,
    mine_ref,
    other_ref,
    target_ref,
    message_ref,
    mono_ref,
    image_ref,
    their_image_ref,
    grad_mine_ref,
    grad_other_ref,
    *scratch,
):
    views, tiles_view, slots, pixels, lanes, column = dims
    table, buf, raw, rec, mom, grad, c_s, h_s, w_hi, w_lo, g_1, g_2, g_3, row_s, row_2, want, got, group_ref = scratch[:18]
    accs = scratch[18:]
    tiles = views * tiles_view
    chips = mine_ref.shape[0]
    half = chips * column
    used = FIELDS * GROUPS
    pad = jnp.zeros((lanes - used, lanes), F32)

    for acc in accs:
        acc[...] = jnp.zeros_like(acc)
    for ref in (buf, w_hi, w_lo, g_1, g_2, g_3, row_s, row_2):
        ref[...] = jnp.zeros_like(ref)

    kept = tiles_view // 2
    part_tiles = views * kept
    for v in range(views):
        for c in range(3):
            want[v, c, :, :] = target_ref[v, c, 0:kept, :]
            start = 2 * part_tiles + (v * 3 + c) * kept
            want[views + v, c, :, :] = message_ref[start : start + kept, :]
    group_ref[0:part_tiles, :] = own_group_ref[...]
    group_ref[part_tiles:, :] = their_group_ref[...]

    def build(q, _):
        for base, ref in ((0, mine_ref), (half, other_ref)):
            for d in range(column):
                block = jnp.concatenate([ref[q, d * used : (d + 1) * used, :], pad], axis=0)
                start = pl.multiple_of((base + q * column + d) * lanes, lanes)
                table[pl.ds(start, lanes), :] = jnp.transpose(block)
        return 0

    lax.fori_loop(0, chips, build, 0)

    def live_of(t):
        return live_ref[t]

    sizes = [slots >> n for n in range(SIZES)]

    def in_turn(body):
        def trip(s, _, positions):
            body([row_ref[tiles * slots + s * BATCH + g] for g in range(BATCH)], positions)
            return 0

        start = 0
        for n, positions in enumerate(sizes):
            over = row_ref[tiles * slots + tiles + n] if n + 1 < len(sizes) else tiles
            end = lax.div(over + (BATCH - 1), BATCH)
            lax.fori_loop(start, end, partial(trip, positions=positions), 0)
            start = end

    sub = lax.broadcasted_iota(jnp.int32, (GROUPS, slots), 0)

    def widen(row):
        spare = slots - row.shape[1]
        return jnp.concatenate([row, jnp.zeros((1, spare), F32)], axis=1) if spare else row

    def fetch(tile, positions):
        for g, t in enumerate(tile):

            def copy(i, t=t, g=g):
                for k in range(GROUPS):
                    buf[g, pl.ds(i * GROUPS + k, 1), :] = table[pl.ds(row_ref[t * slots + i * GROUPS + k], 1), :]

            repeat(chunk_rows(live_of(t)), 4, copy)
        for g, t in enumerate(tile):
            turned = jnp.transpose(buf[g, 0:positions, :])
            mine = sub[:, 0:positions] == group_ref[pl.ds(t, 1), :][:, 0:positions]
            for f in range(FIELDS):
                part = jnp.where(mine, turned[f * GROUPS : (f + 1) * GROUPS], 0.0)
                raw[f, pl.ds(t, 1), :] = widen(jnp.sum(part, axis=0, keepdims=True))

    in_turn(fetch)

    def project(v):
        block = slice(v * kept, (v + 1) * kept)
        cam = [cam_ref[v % views * 8 + n] for n in range(8)]
        field = lambda f: raw[f, block, :]
        u = cam[0] * field(0) + cam[1] * field(1) + cam[2] * field(2) + cam[3]
        w = cam[4] * field(0) + cam[5] * field(1) + cam[6] * field(2) + cam[7]
        d0, d1, d2 = jnp.exp(field(3)), jnp.exp(field(5)), jnp.exp(field(8))
        factor = []
        for i in range(2):
            m = cam[4 * i : 4 * i + 3]
            factor.append(
                (
                    m[0] * d0 + m[1] * field(4) + m[2] * field(6),
                    m[1] * d1 + m[2] * field(7),
                    m[2] * d2,
                )
            )
        f0, f1 = factor
        s00 = f0[0] * f0[0] + f0[1] * f0[1] + f0[2] * f0[2] + 0.3
        s01 = f0[0] * f1[0] + f0[1] * f1[1] + f0[2] * f1[2]
        s11 = f1[0] * f1[0] + f1[1] * f1[1] + f1[2] * f1[2] + 0.3
        inverse = 1.0 / (s00 * s11 - s01 * s01)
        conic = (s11 * inverse, -s01 * inverse, s00 * inverse)
        here = group_ref[block, :] < GROUPS
        return here, cam, block, u, w, (d0, d1, d2), f0, f1, conic

    for v in range(2 * views):
        here, cam, block, u, w, _, _, _, (ka, kb, kc) = project(v)
        x_line = ka * u + kb * w
        y_line = kb * u + kc * w
        log_opacity = math.log(0.95) - jnp.log(1.0 + jnp.exp(-raw[9, block, :]))
        level = log_opacity - 0.5 * (u * x_line + w * y_line)
        terms = (-0.5 * ka, -kb, -0.5 * kc, x_line, y_line)
        for n, term in enumerate(terms):
            rec[n, block, :] = jnp.where(here, term * LOG2E, 0.0)
        rec[5, block, :] = jnp.where(here, level * LOG2E, OFF)
        for c in range(3):
            rec[6 + c, block, :] = raw[10 + c, block, :]

    lane_row = lax.broadcasted_iota(jnp.int32, (GROUPS, pixels), 0)
    own_chunk = (lax.broadcasted_iota(jnp.int32, (GROUPS, slots), 1) & 7) == sub
    zero_pix = jnp.zeros((8, pixels), F32)

    def paired(a, b):
        return a + pltpu.roll(b, 3, 0)

    def render(tile, positions):
        zero_rows = jnp.zeros((8, positions), F32)
        used = slice(0, positions)
        blocks = (chunk_rows(functools.reduce(jnp.maximum, [live_of(t) for t in tile])) + 3) >> 2
        for g, t in enumerate(tile):
            for n in range(6):
                row_s[g, n : n + 1, :] = rec[n, pl.ds(t, 1), :]
            for c in range(3):
                row_s[g, 8 + c : 9 + c, :] = rec[6 + c, pl.ds(t, 1), :]
        for g in range(BATCH):
            lhs = jnp.concatenate(pieces_of(row_s[g, 0:8, used], 3) + [zero_rows], axis=0).astype(BF16)
            c_s[g, used, :] = dot_tn(lhs, mono_ref[...])
        colour = [pieces_of(row_s[g, 8:16, used], 3) for g in range(BATCH)]

        def through(i, prods):
            rows = pl.ds(pl.multiple_of(i * 32, 32), 32)
            out = []
            for g in range(BATCH):
                cover = jnp.exp2(c_s[g, rows, :])
                c_s[g, rows, :] = cover
                keep = 1.0 - cover
                out.append(prods[g] * ((keep[0:8] * keep[8:16]) * (keep[16:24] * keep[24:32])))
            return tuple(out)

        ones = jnp.ones((GROUPS, pixels), F32)
        lead = list(lax.fori_loop(0, blocks, through, (ones,) * BATCH))
        for g in range(BATCH):
            scan = lead[g]
            for step in (1, 2, 4):
                scan = scan * jnp.where(lane_row >= step, pltpu.roll(scan, step, 0), 1.0)
            lead[g] = jnp.where(lane_row >= 1, pltpu.roll(scan, 1, 0), 1.0)

        def weights(cover, prod):
            out = []
            for h in range(4):
                weight = prod * cover[8 * h : 8 * h + 8]
                prod = prod - weight
                out.append(weight)
            return out, prod

        def weigh(i, prods):
            rows = pl.ds(pl.multiple_of(i * 32, 32), 32)
            out = []
            for g in range(BATCH):
                parts, prod = weights(c_s[g, rows, :], prods[g])
                weight = jnp.concatenate(parts, axis=0)
                high = weight.astype(BF16)
                w_hi[g, rows, :] = high
                w_lo[g, rows, :] = (weight - high.astype(F32)).astype(BF16)
                out.append(prod)
            return tuple(out)

        lax.fori_loop(0, blocks, weigh, tuple(lead))

        after = []
        for g, t in enumerate(tile):
            v, tl = lax.div(t, kept), lax.rem(t, kept)
            spread = [
                jnp.where(own_chunk[:, used], jnp.broadcast_to(piece[c : c + 1], (GROUPS, positions)), 0.0)
                for c in range(3)
                for piece in colour[g]
            ]
            lhs = jnp.concatenate(spread + [zero_rows], axis=0).astype(BF16)
            image = dot_nn(lhs, w_hi[g, used, :]) + dot_nn(lhs, w_lo[g, used, :])
            rest = jnp.zeros((GROUPS, pixels), F32)
            for c in range(3):
                part = image[24 * c : 24 * c + 8] + image[24 * c + 8 : 24 * c + 16] + image[24 * c + 16 : 24 * c + 24]
                whole = jnp.sum(part, axis=0, keepdims=True)
                got[v, c, pl.ds(tl, 1), :] = whole
                miss = whole - want[v, c, pl.ds(tl, 1), :]
                row_2[g, c : c + 1, :] = miss
                rest = rest + part * miss
            for step in (1, 2, 4):
                rest = rest + jnp.where(lane_row < GROUPS - step, pltpu.roll(rest, GROUPS - step, 0), 0.0)
            after.append(rest)
        missed = [pieces_of(row_2[g], 3) for g in range(BATCH)]
        for g in range(BATCH):
            c1, c2, c3 = colour[g]
            m1, m2, m3 = missed[g]
            lhs = jnp.concatenate([paired(c1, c1), paired(c2, c1), paired(c2, c3), zero_rows], axis=0)
            rhs = jnp.concatenate([paired(m1, m2), paired(m1, m3), paired(m2, m1), zero_pix], axis=0)
            h_s[g, used, :] = dot_tn(lhs.astype(BF16), rhs.astype(BF16))

        def settle(i, carry):
            rows = pl.ds(pl.multiple_of(i * 32, 32), 32)
            out = []
            for g in range(BATCH):
                prod, tail = carry[g]
                cover = c_s[g, rows, :]
                pull = h_s[g, rows, :]
                parts, prod = weights(cover, prod)
                ratio = cover / (1.0 - cover)
                slopes = []
                for h in range(4):
                    cut = slice(8 * h, 8 * h + 8)
                    part = parts[h] * pull[cut]
                    tail = tail - part
                    slopes.append(part - ratio[cut] * tail)
                slope = jnp.concatenate(slopes, axis=0)
                high = slope.astype(BF16)
                rest = slope - high.astype(F32)
                middle = rest.astype(BF16)
                g_1[g, rows, :] = high
                g_2[g, rows, :] = middle
                g_3[g, rows, :] = (rest - middle.astype(F32)).astype(BF16)
                out.append((prod, tail))
            return tuple(out)

        lax.fori_loop(0, blocks, settle, tuple(zip(lead, after)))
        mono = mono_ref[0:16, :]
        for g in range(BATCH):
            moments = dot_nt(mono, g_1[g, used, :]) + dot_nt(mono, g_2[g, used, :]) + dot_nt(mono, g_3[g, used, :])
            miss_lhs = jnp.concatenate(missed[g] + [zero_pix], axis=0).astype(BF16)
            tint = dot_nt(miss_lhs, w_hi[g, used, :]) + dot_nt(miss_lhs, w_lo[g, used, :])
            row_s[g, 0:8, used] = moments[0:8]
            row_s[g, 8:16, used] = tint[0:8] + tint[8:16] + tint[16:24]
        for g, t in enumerate(tile):
            for n in range(6):
                mom[n, pl.ds(t, 1), :] = row_s[g, n : n + 1, :]
            for c in range(3):
                mom[6 + c, pl.ds(t, 1), :] = row_s[g, 8 + c : 9 + c, :]

    in_turn(render)
    image_ref[...] = got[0:views]
    their_image_ref[...] = got[views:]

    for v in range(2 * views):
        here, cam, block, u, w, (d0, d1, d2), f0, f1, (ka, kb, kc) = project(v)
        mxx, mxy, myy, mx, my, m1 = [jnp.where(here, mom[n, block, :], 0.0) for n in range(6)]
        dx = mx - u * m1
        dy = my - w * m1
        dxx = mxx - 2.0 * u * mx + u * u * m1
        dxy = mxy - u * my - w * mx + u * w * m1
        dyy = myy - 2.0 * w * my + w * w * m1
        gu = ka * dx + kb * dy
        gw = kb * dx + kc * dy
        ax, ay = ka * dxx + kb * dxy, ka * dxy + kb * dyy
        bx, by = kb * dxx + kc * dxy, kb * dxy + kc * dyy
        h00 = ax * ka + ay * kb
        h01 = ax * kb + ay * kc
        h11 = bx * kb + by * kc
        g0 = [h00 * f0[j] + h01 * f1[j] for j in range(3)]
        g1 = [h01 * f0[j] + h11 * f1[j] for j in range(3)]
        for k in range(3):
            grad[k, block, :] = cam[k] * gu + cam[4 + k] * gw
        grad[3, block, :] = (cam[0] * g0[0] + cam[4] * g1[0]) * d0
        grad[4, block, :] = cam[1] * g0[0] + cam[5] * g1[0]
        grad[5, block, :] = (cam[1] * g0[1] + cam[5] * g1[1]) * d1
        grad[6, block, :] = cam[2] * g0[0] + cam[6] * g1[0]
        grad[7, block, :] = cam[2] * g0[1] + cam[6] * g1[1]
        grad[8, block, :] = (cam[2] * g0[2] + cam[6] * g1[2]) * d2
        grad[9, block, :] = m1 - m1 / (1.0 + jnp.exp(-raw[9, block, :]))
        for c in range(3):
            grad[10 + c, block, :] = mom[6 + c, block, :]

    def give(tile, positions):
        for g, t in enumerate(tile):
            mine = sub[:, 0:positions] == group_ref[pl.ds(t, 1), :][:, 0:positions]
            spread = [
                jnp.where(mine, jnp.broadcast_to(grad[f, pl.ds(t, 1), :][:, 0:positions], (GROUPS, positions)), 0.0)
                for f in range(FIELDS)
            ]
            spread.append(jnp.zeros((lanes - used, positions), F32))
            buf[g, 0:positions, :] = jnp.transpose(jnp.concatenate(spread, axis=0))
        for g, t in enumerate(tile):

            def add(i, t=t, g=g):
                for k in range(0, GROUPS, len(accs)):
                    where = [row_ref[t * slots + i * GROUPS + k + n] for n in range(len(accs))]
                    olds = [accs[n][pl.ds(where[n], 1), :] for n in range(len(accs))]
                    news = [buf[g, pl.ds(i * GROUPS + k + n, 1), :] for n in range(len(accs))]
                    for n in range(len(accs)):
                        accs[n][pl.ds(where[n], 1), :] = olds[n] + news[n]

            repeat(chunk_rows(live_of(t)), 4, add)

    in_turn(give)

    def finish(d, _):
        for base, ref in ((0, grad_mine_ref), (half, grad_other_ref)):
            start = pl.multiple_of((base + d) * lanes, lanes)
            total = accs[0][pl.ds(start, lanes), :]
            for acc in accs[1:]:
                total = total + acc[pl.ds(start, lanes), :]
            ref[d] = jnp.transpose(total)[0:used]
        return 0

    lax.fori_loop(0, half, finish, 0)


def tail_kernel(*refs):
    parts, (centres_ref, shape_ref, opacity_ref, colours_ref), total = refs[:-5], refs[-5:-1], refs[-1]
    lanes = total.shape[1]
    value = parts[0][...]
    for part in parts[1:]:
        value = value + part[...]
    total[...] = value
    field = 0
    for ref in (centres_ref, shape_ref, opacity_ref, colours_ref):
        for row in range(ref.shape[0]):
            for k in range(GROUPS):
                at = field * GROUPS + k
                ref[row : row + 1, k * lanes : (k + 1) * lanes] = total[at : at + 1, :]
            field += 1


def monomials(pixels):
    side = math.isqrt(pixels)
    index = np.arange(pixels)
    x = (index % side) - (side - 1) / 2.0
    y = (index // side) - (side - 1) / 2.0
    one = np.ones_like(x)
    zero = np.zeros_like(x)
    group = np.stack([x * x, x * y, y * y, x, y, one, zero, zero])
    return jnp.asarray(np.concatenate([group, group, group, np.zeros_like(group)]), BF16)


def gather(array, axis, masks):
    got = {mask: swap(array, axis, mask) for mask in sorted(masks, reverse=True)}
    return [got[mask] for mask in masks]


def swap(array, axis, mask):
    size = lax.axis_size(axis)
    return lax.ppermute(array, axis, [(i, i ^ mask) for i in range(size)])


def shards(centres, shape_raw, opacity_logit, colours, camera, target, intersection_ids, depth_order, live_count):
    view_group = lax.axis_size("view")
    tile_group = lax.axis_size("tile")
    devices = view_group * tile_group
    chips = tile_group // 2
    own_count = centres.shape[1]
    lanes = own_count // GROUPS
    views, tiles_view, slots = intersection_ids.shape
    tiles = views * tiles_view
    pixels = target.shape[3]
    view_index = lax.axis_index("view")
    tile_index = lax.axis_index("tile")
    me = (view_index * tile_group + tile_index).astype(jnp.int32)

    totals = jnp.sum(live_count, axis=1)
    within = jnp.cumsum(live_count, axis=1) - live_count

    smem = pl.BlockSpec(memory_space=pltpu.SMEM)
    vmem = pl.BlockSpec(memory_space=pltpu.VMEM)
    kept = tiles_view // 2
    part_tiles = views * kept
    dims = (log2_of(own_count), log2_of(lanes), log2_of(view_group), log2_of(tile_group))
    prep_options = dict(
        scratch_shapes=[
            pltpu.VMEM((3, part_tiles, slots), F32),
            pltpu.VMEM((part_tiles, slots), F32),
            pltpu.VMEM((part_tiles, slots), F32),
            pltpu.VMEM((UNROLL, 16, slots), F32),
            pltpu.VMEM((part_tiles, slots), jnp.int32),
            pltpu.VMEM((part_tiles, slots), F32),
        ],
        compiler_params=pltpu.CompilerParams(vmem_limit_bytes=8 * 1024 * 1024),
        cost_estimate=pl.CostEstimate(flops=4_000_000_000, bytes_accessed=8 * tiles * slots, transcendentals=0),
    )
    prep_own = pl.pallas_call(
        partial(prep_own_kernel, dims),
        out_shape=[
            jax.ShapeDtypeStruct((part_tiles, slots), jnp.int32),
            jax.ShapeDtypeStruct((part_tiles, slots), jnp.int32),
            jax.ShapeDtypeStruct((views * 8,), F32),
        ],
        in_specs=[smem] * 3 + [vmem] * 2,
        out_specs=[vmem, vmem, smem],
        name="prep_own",
        **prep_options,
    )
    prep_their = pl.pallas_call(
        partial(prep_their_kernel, dims),
        out_shape=[
            jax.ShapeDtypeStruct((part_tiles + 8, slots), jnp.int32),
            jax.ShapeDtypeStruct((part_tiles, slots), jnp.int32),
        ],
        in_specs=[smem] * 2 + [vmem],
        out_specs=[vmem] * 2,
        name="prep_their",
        **prep_options,
    )

    mirror = tile_group - 1
    target = target.transpose(0, 2, 1, 3)
    message = jnp.concatenate(
        [
            intersection_ids[:, kept:].reshape(part_tiles, slots).astype(F32),
            depth_order[:, kept:].reshape(part_tiles, slots).astype(F32),
            target[:, :, kept:].reshape(3 * part_tiles, pixels),
            jnp.pad(live_count[:, kept:].astype(F32), ((0, 8 - views), (0, slots - kept))),
        ]
    )
    fields = jnp.concatenate([centres, shape_raw, opacity_logit[None], colours], axis=0)
    block = fields.reshape(FIELDS * GROUPS, lanes)
    note = jnp.pad(totals.astype(F32)[None], ((0, 7), (0, lanes - views)))
    column = jnp.concatenate([block] + gather(block, "view", range(1, view_group)) + [note])
    message = swap(message, "tile", mirror)
    column, me = lax.optimization_barrier((column, me))
    mine = jnp.stack([column] + gather(column, "tile", range(2, tile_group, 2)))
    own_rows, own_group, cam = prep_own(me[None], live_count, camera, intersection_ids, depth_order)
    their_live = message[5 * part_tiles : 5 * part_tiles + views, :kept].astype(jnp.int32)
    live_now = jnp.concatenate([live_count[:, :kept].reshape(-1), their_live.reshape(-1)])
    their_rows, their_group = prep_their(me[None], live_now, message)
    rows = jnp.concatenate([own_rows, their_rows]).reshape(-1)
    mine, rows, own_group, their_group, cam = lax.optimization_barrier((mine, rows, own_group, their_group, cam))
    other = swap(mine, "tile", 1)

    table_rows = devices * lanes
    square = (BATCH, slots, pixels)
    half = (chips * view_group, FIELDS * GROUPS, lanes)
    accs = ACCS if devices <= 32 else 2
    room = 4 * table_rows * lanes * (accs + 2) + 16 * 1024 * 1024
    splat = pl.pallas_call(
        partial(splat_kernel, (views, tiles_view, slots, pixels, lanes, view_group)),
        out_shape=[
            jax.ShapeDtypeStruct((views, 3, kept, pixels), F32),
            jax.ShapeDtypeStruct((views, 3, tiles_view - kept, pixels), F32),
            jax.ShapeDtypeStruct(half, F32),
            jax.ShapeDtypeStruct(half, F32),
        ],
        in_specs=[smem] * 3 + [vmem] * 7,
        out_specs=[vmem] * 4,
        scratch_shapes=[
            pltpu.VMEM((table_rows, lanes), F32),
            pltpu.VMEM((BATCH, slots, lanes), F32),
            pltpu.VMEM((FIELDS, tiles, slots), F32),
            pltpu.VMEM((9, tiles, slots), F32),
            pltpu.VMEM((9, tiles, slots), F32),
            pltpu.VMEM((FIELDS, tiles, slots), F32),
            pltpu.VMEM(square, F32),
            pltpu.VMEM(square, F32),
        ]
        + [pltpu.VMEM(square, BF16)] * 5
        + [pltpu.VMEM((BATCH, 16, slots), F32), pltpu.VMEM((BATCH, 8, pixels), F32)]
        + [pltpu.VMEM((2 * views, 3, kept, pixels), F32)] * 2
        + [pltpu.VMEM((tiles, slots), jnp.int32)]
        + [pltpu.VMEM((table_rows, lanes), F32)] * accs,
        compiler_params=pltpu.CompilerParams(vmem_limit_bytes=room),
        name="splat",
    )
    image, their_image, grad_mine, grad_other = splat(
        cam,
        rows,
        live_now,
        own_group,
        their_group,
        mine,
        other,
        target,
        message,
        monomials(pixels),
    )

    whole = totals
    before = jnp.zeros_like(totals)
    for core, held in enumerate((mine, other)):
        for m in range(chips):
            mask = 2 * m + core
            if mask:
                theirs = held[m, view_group * FIELDS * GROUPS, 0:views].astype(jnp.int32)
                whole = whole + theirs
                before = before + jnp.where((tile_index ^ mask) < tile_index, theirs, 0)
    next_owner = (before[:, None] + within) * tile_group // whole[:, None]

    grad_other = swap(grad_other, "tile", 1)
    rendered = jnp.concatenate([image, swap(their_image, "tile", mirror)], axis=2)
    joined = (grad_mine + grad_other).reshape(chips, view_group, FIELDS * GROUPS, lanes)
    part = joined[0]
    for m in reversed(range(1, chips)):
        part = part + swap(joined[m], "tile", 2 * m)
    parts = [part[0]] + [swap(part[m], "view", m) for m in reversed(range(1, view_group))]
    tail = pl.pallas_call(
        tail_kernel,
        out_shape=[jax.ShapeDtypeStruct((count, own_count), F32) for count in (3, 6, 1, 3)],
        in_specs=[vmem] * len(parts),
        out_specs=[vmem] * 4,
        scratch_shapes=[pltpu.VMEM((FIELDS * GROUPS, lanes), F32)],
        compiler_params=pltpu.CompilerParams(vmem_limit_bytes=8 * 1024 * 1024),
        name="tail",
    )
    grad_centres, grad_shape, grad_opacity, grad_colours = tail(*parts)
    return (
        rendered.transpose(0, 2, 1, 3),
        grad_centres,
        grad_shape,
        grad_opacity[0],
        grad_colours,
        next_owner,
    )


def solution(mesh):
    in_specs = (
        P(None, ("view", "tile")),
        P(None, ("view", "tile")),
        P(("view", "tile")),
        P(None, ("view", "tile")),
        P(),
        P("view", "tile", None, None),
        P("view", "tile", None),
        P("view", "tile", None),
        P("view", "tile"),
    )
    out_specs = (
        P("view", "tile", None, None),
        P(None, ("view", "tile")),
        P(None, ("view", "tile")),
        P(("view", "tile")),
        P(None, ("view", "tile")),
        P("view", "tile"),
    )
    return jax.shard_map(shards, mesh=mesh, in_specs=in_specs, out_specs=out_specs, check_vma=False)
```

```python
import functools
from functools import partial
import math

import jax
import jax.numpy as jnp
import numpy as np
from jax import lax
from jax.experimental import pallas as pl
from jax.experimental.pallas import tpu as pltpu
from jax.sharding import PartitionSpec as P

F32 = jnp.float32
BF16 = jnp.bfloat16
FIELDS = 13
GROUPS = 8
ACCS = 4
UNROLL = 8
SIZES = 3
BATCH = 8
LOG2E = math.log2(math.e)
OFF = -1e4


def log2_of(n):
    bits = n.bit_length() - 1
    assert n == 1 << bits
    return bits


def pieces_of(value, count):
    out = []
    rest = value
    for _ in range(count - 1):
        piece = rest.astype(BF16).astype(F32)
        out.append(piece)
        rest = rest - piece
    out.append(rest)
    return out


def dot_nn(a, b):
    return lax.dot_general(a, b, (((1,), (0,)), ((), ())), preferred_element_type=F32)


def dot_nt(a, b):
    return lax.dot_general(a, b, (((1,), (1,)), ((), ())), preferred_element_type=F32)


def dot_tn(a, b):
    return lax.dot_general(a, b, (((0,), (0,)), ((), ())), preferred_element_type=F32)


def chunk_rows(live):
    return (live + 7) >> 3


def repeat(count, step, body):
    def trip(i, _):
        for u in range(step):
            body(i * step + u)
        return 0

    lax.fori_loop(0, lax.div(count + (step - 1), step), trip, 0)


def place_slots(dims, me, live_at, ids, order, scratch):
    own_bits, lane_bits, view_bits, tile_bits = dims
    piece_ref, rho_ref, code_ref, lhs_ref, live_full, order_b = scratch
    tiles, slots = ids.shape
    for t in range(tiles):
        live_full[t : t + 1, :] = jnp.full((1, slots), live_at(t), jnp.int32)
    live = live_full[...]
    active = order < live
    upper = (
        lax.broadcasted_iota(jnp.int32, (slots, slots), 0)
        < lax.broadcasted_iota(jnp.int32, (slots, slots), 1)
    ).astype(F32).astype(BF16)
    place = dot_nn(active.astype(F32).astype(BF16), upper).astype(jnp.int32)
    rows = chunk_rows(live)
    chunk = jnp.zeros((tiles, slots), jnp.int32)
    for m in range(1, GROUPS):
        chunk = chunk + (place >= m * rows).astype(jnp.int32)
    rho_ref[...] = jnp.where(active, (place - chunk * rows) * GROUPS + chunk, -1).astype(F32)
    order_b[...] = order.astype(F32)
    owner = (ids >> own_bits) ^ me
    local = ids & ((1 << own_bits) - 1)
    xy_bits = tile_bits - 1
    core = owner & 1
    chip = (owner >> 1) & ((1 << xy_bits) - 1)
    view = owner >> tile_bits
    block = (((core << xy_bits) | chip) << view_bits) | view
    row = (block << lane_bits) | (local & ((1 << lane_bits) - 1))
    code = (row << 3) | (local >> lane_bits)
    piece_ref[0] = (code & 255).astype(F32)
    piece_ref[1] = ((code >> 8) & 255).astype(F32)
    piece_ref[2] = (code >> 16).astype(F32)
    lhs_ref[...] = jnp.zeros_like(lhs_ref)
    down = lax.broadcasted_iota(jnp.int32, (slots, slots), 0).astype(F32).astype(BF16)
    one = jnp.ones((slots, slots), BF16)
    nil = jnp.zeros((slots, slots), BF16)

    def some_tiles(s, _):
        for u in range(UNROLL):
            t = s * UNROLL + u
            for p in range(3):
                lhs_ref[u, p : p + 1, :] = piece_ref[p, pl.ds(t, 1), :]
            picked = jnp.where(down == order_b[pl.ds(t, 1), :].astype(BF16), one, nil)
            ordered = dot_nn(lhs_ref[u].astype(BF16), picked)
            placed = jnp.where(down == rho_ref[pl.ds(t, 1), :].astype(BF16), one, nil)
            out = dot_nt(ordered.astype(BF16), placed)
            code_ref[pl.ds(t, 1), :] = out[0:1] + 256.0 * out[1:2] + 65536.0 * out[2:3]
        return 0

    lax.fori_loop(0, tiles // UNROLL, some_tiles, 0)
    codes = code_ref[...].astype(jnp.int32)
    pos = lax.broadcasted_iota(jnp.int32, (tiles, slots), 1)
    here = (pos >> 3 < rows) & ((pos & 7) * rows + (pos >> 3) < live)
    return codes >> 3, jnp.where(here, codes & 7, GROUPS)


def prep_own_kernel(dims, me_ref, live_ref, camera_ref, ids_ref, order_ref, row_ref, group_ref, cam_ref, *scratch):
    views, tiles_view, _ = ids_ref.shape
    kept = tiles_view // 2
    me = me_ref[0]
    first = (me >> dims[3]) * views
    for v in range(views):
        for i in range(2):
            for j in range(4):
                cam_ref[v * 8 + i * 4 + j] = camera_ref[first + v, i, j]
    ids = jnp.concatenate([ids_ref[v, 0:kept, :] for v in range(views)], axis=0)
    order = jnp.concatenate([order_ref[v, 0:kept, :] for v in range(views)], axis=0)
    live_at = lambda t: live_ref[t // kept, t % kept]
    row_ref[...], group_ref[...] = place_slots(dims, me, live_at, ids, order, scratch)


def prep_their_kernel(dims, me_ref, live_ref, message_ref, row_ref, group_ref, *scratch):
    tiles, slots = group_ref.shape
    total = live_ref.shape[0]
    ids = message_ref[0:tiles, :].astype(jnp.int32)
    order = message_ref[tiles : 2 * tiles, :].astype(jnp.int32)
    live_at = lambda t: live_ref[total - tiles + t]
    row_ref[0:tiles, :], group_ref[...] = place_slots(dims, me_ref[0], live_at, ids, order, scratch)
    lane = lax.broadcasted_iota(jnp.int32, (total, slots), 1)
    above = lax.broadcasted_iota(jnp.int32, (total, slots), 0)
    across = jnp.full((total, slots), -1, jnp.int32)
    down = jnp.zeros((total, slots), jnp.int32)
    for t in range(total):
        across = jnp.where(lane == t, live_ref[t], across)
        down = jnp.where(above == t, live_ref[t], down)
    ahead = (across > down) | ((across == down) & (lane < above))
    rank = jnp.sum(ahead.astype(jnp.int32), axis=1, keepdims=True)
    ranked = jnp.sum(jnp.where(rank == lane, above, 0), axis=0, keepdims=True)
    for n in range(1, SIZES):
        over = jnp.sum((across > slots >> n).astype(jnp.int32), axis=1, keepdims=True)[0:1]
        ranked = jnp.where(lane[0:1] == total + n - 1, over, ranked)
    row_ref[tiles : tiles + 1, :] = ranked


def splat_kernel(
    dims,
    cam_ref,
    row_ref,
    live_ref,
    own_group_ref,
    their_group_ref,
    mine_ref,
    other_ref,
    target_ref,
    message_ref,
    mono_ref,
    image_ref,
    their_image_ref,
    grad_mine_ref,
    grad_other_ref,
    *scratch,
):
    views, tiles_view, slots, pixels, lanes, column = dims
    table, buf, raw, rec, mom, grad, c_s, h_s, w_hi, w_lo, g_1, g_2, g_3, row_s, row_2, want, got, group_ref = scratch[:18]
    accs = scratch[18:]
    tiles = views * tiles_view
    chips = mine_ref.shape[0]
    half = chips * column
    used = FIELDS * GROUPS
    pad = jnp.zeros((lanes - used, lanes), F32)

    for acc in accs:
        acc[...] = jnp.zeros_like(acc)
    for ref in (buf, w_hi, w_lo, g_1, g_2, g_3, row_s, row_2):
        ref[...] = jnp.zeros_like(ref)

    kept = tiles_view // 2
    part_tiles = views * kept
    for v in range(views):
        for c in range(3):
            want[v, c, :, :] = target_ref[v, c, 0:kept, :]
            start = 2 * part_tiles + (v * 3 + c) * kept
            want[views + v, c, :, :] = message_ref[start : start + kept, :]
    group_ref[0:part_tiles, :] = own_group_ref[...]
    group_ref[part_tiles:, :] = their_group_ref[...]

    def build(q, _):
        for base, ref in ((0, mine_ref), (half, other_ref)):
            for d in range(column):
                block = jnp.concatenate([ref[q, d * used : (d + 1) * used, :], pad], axis=0)
                start = pl.multiple_of((base + q * column + d) * lanes, lanes)
                table[pl.ds(start, lanes), :] = jnp.transpose(block)
        return 0

    lax.fori_loop(0, chips, build, 0)

    def live_of(t):
        return live_ref[t]

    sizes = [slots >> n for n in range(SIZES)]

    def in_turn(body):
        def trip(s, _, positions):
            body([row_ref[tiles * slots + s * BATCH + g] for g in range(BATCH)], positions)
            return 0

        start = 0
        for n, positions in enumerate(sizes):
            over = row_ref[tiles * slots + tiles + n] if n + 1 < len(sizes) else tiles
            end = lax.div(over + (BATCH - 1), BATCH)
            lax.fori_loop(start, end, partial(trip, positions=positions), 0)
            start = end

    sub = lax.broadcasted_iota(jnp.int32, (GROUPS, slots), 0)

    def widen(row):
        spare = slots - row.shape[1]
        return jnp.concatenate([row, jnp.zeros((1, spare), F32)], axis=1) if spare else row

    def fetch(tile, positions):
        for g, t in enumerate(tile):

            def copy(i, t=t, g=g):
                for k in range(GROUPS):
                    buf[g, pl.ds(i * GROUPS + k, 1), :] = table[pl.ds(row_ref[t * slots + i * GROUPS + k], 1), :]

            repeat(chunk_rows(live_of(t)), 4, copy)
        for g, t in enumerate(tile):
            turned = jnp.transpose(buf[g, 0:positions, :])
            mine = sub[:, 0:positions] == group_ref[pl.ds(t, 1), :][:, 0:positions]
            for f in range(FIELDS):
                part = jnp.where(mine, turned[f * GROUPS : (f + 1) * GROUPS], 0.0)
                raw[f, pl.ds(t, 1), :] = widen(jnp.sum(part, axis=0, keepdims=True))

    in_turn(fetch)

    def project(v):
        block = slice(v * kept, (v + 1) * kept)
        cam = [cam_ref[v % views * 8 + n] for n in range(8)]
        field = lambda f: raw[f, block, :]
        u = cam[0] * field(0) + cam[1] * field(1) + cam[2] * field(2) + cam[3]
        w = cam[4] * field(0) + cam[5] * field(1) + cam[6] * field(2) + cam[7]
        d0, d1, d2 = jnp.exp(field(3)), jnp.exp(field(5)), jnp.exp(field(8))
        factor = []
        for i in range(2):
            m = cam[4 * i : 4 * i + 3]
            factor.append(
                (
                    m[0] * d0 + m[1] * field(4) + m[2] * field(6),
                    m[1] * d1 + m[2] * field(7),
                    m[2] * d2,
                )
            )
        f0, f1 = factor
        s00 = f0[0] * f0[0] + f0[1] * f0[1] + f0[2] * f0[2] + 0.3
        s01 = f0[0] * f1[0] + f0[1] * f1[1] + f0[2] * f1[2]
        s11 = f1[0] * f1[0] + f1[1] * f1[1] + f1[2] * f1[2] + 0.3
        inverse = 1.0 / (s00 * s11 - s01 * s01)
        conic = (s11 * inverse, -s01 * inverse, s00 * inverse)
        here = group_ref[block, :] < GROUPS
        return here, cam, block, u, w, (d0, d1, d2), f0, f1, conic

    for v in range(2 * views):
        here, cam, block, u, w, _, _, _, (ka, kb, kc) = project(v)
        x_line = ka * u + kb * w
        y_line = kb * u + kc * w
        log_opacity = math.log(0.95) - jnp.log(1.0 + jnp.exp(-raw[9, block, :]))
        level = log_opacity - 0.5 * (u * x_line + w * y_line)
        terms = (-0.5 * ka, -kb, -0.5 * kc, x_line, y_line)
        for n, term in enumerate(terms):
            rec[n, block, :] = jnp.where(here, term * LOG2E, 0.0)
        rec[5, block, :] = jnp.where(here, level * LOG2E, OFF)
        for c in range(3):
            rec[6 + c, block, :] = raw[10 + c, block, :]

    lane_row = lax.broadcasted_iota(jnp.int32, (GROUPS, pixels), 0)
    own_chunk = (lax.broadcasted_iota(jnp.int32, (GROUPS, slots), 1) & 7) == sub
    zero_pix = jnp.zeros((8, pixels), F32)

    def paired(a, b):
        return a + pltpu.roll(b, 3, 0)

    def render(tile, positions):
        zero_rows = jnp.zeros((8, positions), F32)
        used = slice(0, positions)
        blocks = (chunk_rows(functools.reduce(jnp.maximum, [live_of(t) for t in tile])) + 3) >> 2
        for g, t in enumerate(tile):
            for n in range(6):
                row_s[g, n : n + 1, :] = rec[n, pl.ds(t, 1), :]
            for c in range(3):
                row_s[g, 8 + c : 9 + c, :] = rec[6 + c, pl.ds(t, 1), :]
        for g in range(BATCH):
            lhs = jnp.concatenate(pieces_of(row_s[g, 0:8, used], 3) + [zero_rows], axis=0).astype(BF16)
            c_s[g, used, :] = dot_tn(lhs, mono_ref[...])
        colour = [pieces_of(row_s[g, 8:16, used], 3) for g in range(BATCH)]

        def through(i, prods):
            rows = pl.ds(pl.multiple_of(i * 32, 32), 32)
            out = []
            for g in range(BATCH):
                cover = jnp.exp2(c_s[g, rows, :])
                c_s[g, rows, :] = cover
                keep = 1.0 - cover
                out.append(prods[g] * ((keep[0:8] * keep[8:16]) * (keep[16:24] * keep[24:32])))
            return tuple(out)

        ones = jnp.ones((GROUPS, pixels), F32)
        lead = list(lax.fori_loop(0, blocks, through, (ones,) * BATCH))
        for g in range(BATCH):
            scan = lead[g]
            for step in (1, 2, 4):
                scan = scan * jnp.where(lane_row >= step, pltpu.roll(scan, step, 0), 1.0)
            lead[g] = jnp.where(lane_row >= 1, pltpu.roll(scan, 1, 0), 1.0)

        def weights(cover, prod):
            out = []
            for h in range(4):
                weight = prod * cover[8 * h : 8 * h + 8]
                prod = prod - weight
                out.append(weight)
            return out, prod

        def weigh(i, prods):
            rows = pl.ds(pl.multiple_of(i * 32, 32), 32)
            out = []
            for g in range(BATCH):
                parts, prod = weights(c_s[g, rows, :], prods[g])
                weight = jnp.concatenate(parts, axis=0)
                high = weight.astype(BF16)
                w_hi[g, rows, :] = high
                w_lo[g, rows, :] = (weight - high.astype(F32)).astype(BF16)
                out.append(prod)
            return tuple(out)

        lax.fori_loop(0, blocks, weigh, tuple(lead))

        after = []
        for g, t in enumerate(tile):
            v, tl = lax.div(t, kept), lax.rem(t, kept)
            spread = [
                jnp.where(own_chunk[:, used], jnp.broadcast_to(piece[c : c + 1], (GROUPS, positions)), 0.0)
                for c in range(3)
                for piece in colour[g]
            ]
            lhs = jnp.concatenate(spread + [zero_rows], axis=0).astype(BF16)
            image = dot_nn(lhs, w_hi[g, used, :]) + dot_nn(lhs, w_lo[g, used, :])
            rest = jnp.zeros((GROUPS, pixels), F32)
            for c in range(3):
                part = image[24 * c : 24 * c + 8] + image[24 * c + 8 : 24 * c + 16] + image[24 * c + 16 : 24 * c + 24]
                whole = jnp.sum(part, axis=0, keepdims=True)
                got[v, c, pl.ds(tl, 1), :] = whole
                miss = whole - want[v, c, pl.ds(tl, 1), :]
                row_2[g, c : c + 1, :] = miss
                rest = rest + part * miss
            for step in (1, 2, 4):
                rest = rest + jnp.where(lane_row < GROUPS - step, pltpu.roll(rest, GROUPS - step, 0), 0.0)
            after.append(rest)
        missed = [pieces_of(row_2[g], 3) for g in range(BATCH)]
        for g in range(BATCH):
            c1, c2, c3 = colour[g]
            m1, m2, m3 = missed[g]
            lhs = jnp.concatenate([paired(c1, c1), paired(c2, c1), paired(c2, c3), zero_rows], axis=0)
            rhs = jnp.concatenate([paired(m1, m2), paired(m1, m3), paired(m2, m1), zero_pix], axis=0)
            h_s[g, used, :] = dot_tn(lhs.astype(BF16), rhs.astype(BF16))

        def settle(i, carry):
            rows = pl.ds(pl.multiple_of(i * 32, 32), 32)
            out = []
            for g in range(BATCH):
                prod, tail = carry[g]
                cover = c_s[g, rows, :]
                pull = h_s[g, rows, :]
                parts, prod = weights(cover, prod)
                ratio = cover / (1.0 - cover)
                slopes = []
                for h in range(4):
                    cut = slice(8 * h, 8 * h + 8)
                    part = parts[h] * pull[cut]
                    tail = tail - part
                    slopes.append(part - ratio[cut] * tail)
                slope = jnp.concatenate(slopes, axis=0)
                high = slope.astype(BF16)
                rest = slope - high.astype(F32)
                middle = rest.astype(BF16)
                g_1[g, rows, :] = high
                g_2[g, rows, :] = middle
                g_3[g, rows, :] = (rest - middle.astype(F32)).astype(BF16)
                out.append((prod, tail))
            return tuple(out)

        lax.fori_loop(0, blocks, settle, tuple(zip(lead, after)))
        mono = mono_ref[0:16, :]
        for g in range(BATCH):
            moments = dot_nt(mono, g_1[g, used, :]) + dot_nt(mono, g_2[g, used, :]) + dot_nt(mono, g_3[g, used, :])
            miss_lhs = jnp.concatenate(missed[g] + [zero_pix], axis=0).astype(BF16)
            tint = dot_nt(miss_lhs, w_hi[g, used, :]) + dot_nt(miss_lhs, w_lo[g, used, :])
            row_s[g, 0:8, used] = moments[0:8]
            row_s[g, 8:16, used] = tint[0:8] + tint[8:16] + tint[16:24]
        for g, t in enumerate(tile):
            for n in range(6):
                mom[n, pl.ds(t, 1), :] = row_s[g, n : n + 1, :]
            for c in range(3):
                mom[6 + c, pl.ds(t, 1), :] = row_s[g, 8 + c : 9 + c, :]

    in_turn(render)
    image_ref[...] = got[0:views]
    their_image_ref[...] = got[views:]

    for v in range(2 * views):
        here, cam, block, u, w, (d0, d1, d2), f0, f1, (ka, kb, kc) = project(v)
        mxx, mxy, myy, mx, my, m1 = [jnp.where(here, mom[n, block, :], 0.0) for n in range(6)]
        dx = mx - u * m1
        dy = my - w * m1
        dxx = mxx - 2.0 * u * mx + u * u * m1
        dxy = mxy - u * my - w * mx + u * w * m1
        dyy = myy - 2.0 * w * my + w * w * m1
        gu = ka * dx + kb * dy
        gw = kb * dx + kc * dy
        ax, ay = ka * dxx + kb * dxy, ka * dxy + kb * dyy
        bx, by = kb * dxx + kc * dxy, kb * dxy + kc * dyy
        h00 = ax * ka + ay * kb
        h01 = ax * kb + ay * kc
        h11 = bx * kb + by * kc
        g0 = [h00 * f0[j] + h01 * f1[j] for j in range(3)]
        g1 = [h01 * f0[j] + h11 * f1[j] for j in range(3)]
        for k in range(3):
            grad[k, block, :] = cam[k] * gu + cam[4 + k] * gw
        grad[3, block, :] = (cam[0] * g0[0] + cam[4] * g1[0]) * d0
        grad[4, block, :] = cam[1] * g0[0] + cam[5] * g1[0]
        grad[5, block, :] = (cam[1] * g0[1] + cam[5] * g1[1]) * d1
        grad[6, block, :] = cam[2] * g0[0] + cam[6] * g1[0]
        grad[7, block, :] = cam[2] * g0[1] + cam[6] * g1[1]
        grad[8, block, :] = (cam[2] * g0[2] + cam[6] * g1[2]) * d2
        grad[9, block, :] = m1 - m1 / (1.0 + jnp.exp(-raw[9, block, :]))
        for c in range(3):
            grad[10 + c, block, :] = mom[6 + c, block, :]

    def give(tile, positions):
        for g, t in enumerate(tile):
            mine = sub[:, 0:positions] == group_ref[pl.ds(t, 1), :][:, 0:positions]
            spread = [
                jnp.where(mine, jnp.broadcast_to(grad[f, pl.ds(t, 1), :][:, 0:positions], (GROUPS, positions)), 0.0)
                for f in range(FIELDS)
            ]
            spread.append(jnp.zeros((lanes - used, positions), F32))
            buf[g, 0:positions, :] = jnp.transpose(jnp.concatenate(spread, axis=0))
        for g, t in enumerate(tile):

            def add(i, t=t, g=g):
                for k in range(0, GROUPS, len(accs)):
                    where = [row_ref[t * slots + i * GROUPS + k + n] for n in range(len(accs))]
                    olds = [accs[n][pl.ds(where[n], 1), :] for n in range(len(accs))]
                    news = [buf[g, pl.ds(i * GROUPS + k + n, 1), :] for n in range(len(accs))]
                    for n in range(len(accs)):
                        accs[n][pl.ds(where[n], 1), :] = olds[n] + news[n]

            repeat(chunk_rows(live_of(t)), 4, add)

    in_turn(give)

    def finish(q, _):
        for base, ref in ((0, grad_mine_ref), (half, grad_other_ref)):
            for d in range(column):
                start = pl.multiple_of((base + q * column + d) * lanes, lanes)
                total = accs[0][pl.ds(start, lanes), :]
                for acc in accs[1:]:
                    total = total + acc[pl.ds(start, lanes), :]
                ref[q * column + d] = jnp.transpose(total)[0:used]
        return 0

    lax.fori_loop(0, chips, finish, 0)


def tail_kernel(*refs):
    parts, (centres_ref, shape_ref, opacity_ref, colours_ref), total = refs[:-5], refs[-5:-1], refs[-1]
    lanes = total.shape[1]
    value = parts[0][...]
    for part in parts[1:]:
        value = value + part[...]
    total[...] = value
    field = 0
    for ref in (centres_ref, shape_ref, opacity_ref, colours_ref):
        for row in range(ref.shape[0]):
            for k in range(GROUPS):
                at = field * GROUPS + k
                ref[row : row + 1, k * lanes : (k + 1) * lanes] = total[at : at + 1, :]
            field += 1


def monomials(pixels):
    side = math.isqrt(pixels)
    index = np.arange(pixels)
    x = (index % side) - (side - 1) / 2.0
    y = (index // side) - (side - 1) / 2.0
    one = np.ones_like(x)
    zero = np.zeros_like(x)
    group = np.stack([x * x, x * y, y * y, x, y, one, zero, zero])
    return jnp.asarray(np.concatenate([group, group, group, np.zeros_like(group)]), BF16)


def gather(array, axis, masks):
    got = {mask: swap(array, axis, mask) for mask in sorted(masks, reverse=True)}
    return [got[mask] for mask in masks]


def swap(array, axis, mask):
    size = lax.axis_size(axis)
    return lax.ppermute(array, axis, [(i, i ^ mask) for i in range(size)])


def shards(centres, shape_raw, opacity_logit, colours, camera, target, intersection_ids, depth_order, live_count):
    view_group = lax.axis_size("view")
    tile_group = lax.axis_size("tile")
    devices = view_group * tile_group
    chips = tile_group // 2
    own_count = centres.shape[1]
    lanes = own_count // GROUPS
    views, tiles_view, slots = intersection_ids.shape
    tiles = views * tiles_view
    pixels = target.shape[3]
    view_index = lax.axis_index("view")
    tile_index = lax.axis_index("tile")
    me = (view_index * tile_group + tile_index).astype(jnp.int32)

    totals = jnp.sum(live_count, axis=1)
    within = jnp.cumsum(live_count, axis=1) - live_count

    smem = pl.BlockSpec(memory_space=pltpu.SMEM)
    vmem = pl.BlockSpec(memory_space=pltpu.VMEM)
    kept = tiles_view // 2
    part_tiles = views * kept
    dims = (log2_of(own_count), log2_of(lanes), log2_of(view_group), log2_of(tile_group))
    prep_options = dict(
        scratch_shapes=[
            pltpu.VMEM((3, part_tiles, slots), F32),
            pltpu.VMEM((part_tiles, slots), F32),
            pltpu.VMEM((part_tiles, slots), F32),
            pltpu.VMEM((UNROLL, 16, slots), F32),
            pltpu.VMEM((part_tiles, slots), jnp.int32),
            pltpu.VMEM((part_tiles, slots), F32),
        ],
        compiler_params=pltpu.CompilerParams(vmem_limit_bytes=8 * 1024 * 1024),
        cost_estimate=pl.CostEstimate(flops=4_000_000_000, bytes_accessed=8 * tiles * slots, transcendentals=0),
    )
    prep_own = pl.pallas_call(
        partial(prep_own_kernel, dims),
        out_shape=[
            jax.ShapeDtypeStruct((part_tiles, slots), jnp.int32),
            jax.ShapeDtypeStruct((part_tiles, slots), jnp.int32),
            jax.ShapeDtypeStruct((views * 8,), F32),
        ],
        in_specs=[smem] * 3 + [vmem] * 2,
        out_specs=[vmem, vmem, smem],
        name="prep_own",
        **prep_options,
    )
    prep_their = pl.pallas_call(
        partial(prep_their_kernel, dims),
        out_shape=[
            jax.ShapeDtypeStruct((part_tiles + 8, slots), jnp.int32),
            jax.ShapeDtypeStruct((part_tiles, slots), jnp.int32),
        ],
        in_specs=[smem] * 2 + [vmem],
        out_specs=[vmem] * 2,
        name="prep_their",
        **prep_options,
    )

    mirror = tile_group - 1
    target = target.transpose(0, 2, 1, 3)
    message = jnp.concatenate(
        [
            intersection_ids[:, kept:].reshape(part_tiles, slots).astype(F32),
            depth_order[:, kept:].reshape(part_tiles, slots).astype(F32),
            target[:, :, kept:].reshape(3 * part_tiles, pixels),
            jnp.pad(live_count[:, kept:].astype(F32), ((0, 8 - views), (0, slots - kept))),
        ]
    )
    fields = jnp.concatenate([centres, shape_raw, opacity_logit[None], colours], axis=0)
    block = fields.reshape(FIELDS * GROUPS, lanes)
    note = jnp.pad(totals.astype(F32)[None], ((0, 7), (0, lanes - views)))
    column = jnp.concatenate([block] + gather(block, "view", range(1, view_group)) + [note])
    message = swap(message, "tile", mirror)
    column, me = lax.optimization_barrier((column, me))
    mine = jnp.stack([column] + gather(column, "tile", range(2, tile_group, 2)))
    own_rows, own_group, cam = prep_own(me[None], live_count, camera, intersection_ids, depth_order)
    their_live = message[5 * part_tiles : 5 * part_tiles + views, :kept].astype(jnp.int32)
    live_now = jnp.concatenate([live_count[:, :kept].reshape(-1), their_live.reshape(-1)])
    their_rows, their_group = prep_their(me[None], live_now, message)
    rows = jnp.concatenate([own_rows, their_rows]).reshape(-1)
    mine, rows, own_group, their_group, cam = lax.optimization_barrier((mine, rows, own_group, their_group, cam))
    other = swap(mine, "tile", 1)

    table_rows = devices * lanes
    square = (BATCH, slots, pixels)
    half = (chips * view_group, FIELDS * GROUPS, lanes)
    accs = ACCS if devices <= 32 else 2
    room = 4 * table_rows * lanes * (accs + 2) + 16 * 1024 * 1024
    splat = pl.pallas_call(
        partial(splat_kernel, (views, tiles_view, slots, pixels, lanes, view_group)),
        out_shape=[
            jax.ShapeDtypeStruct((views, 3, kept, pixels), F32),
            jax.ShapeDtypeStruct((views, 3, tiles_view - kept, pixels), F32),
            jax.ShapeDtypeStruct(half, F32),
            jax.ShapeDtypeStruct(half, F32),
        ],
        in_specs=[smem] * 3 + [vmem] * 7,
        out_specs=[vmem] * 4,
        scratch_shapes=[
            pltpu.VMEM((table_rows, lanes), F32),
            pltpu.VMEM((BATCH, slots, lanes), F32),
            pltpu.VMEM((FIELDS, tiles, slots), F32),
            pltpu.VMEM((9, tiles, slots), F32),
            pltpu.VMEM((9, tiles, slots), F32),
            pltpu.VMEM((FIELDS, tiles, slots), F32),
            pltpu.VMEM(square, F32),
            pltpu.VMEM(square, F32),
        ]
        + [pltpu.VMEM(square, BF16)] * 5
        + [pltpu.VMEM((BATCH, 16, slots), F32), pltpu.VMEM((BATCH, 8, pixels), F32)]
        + [pltpu.VMEM((2 * views, 3, kept, pixels), F32)] * 2
        + [pltpu.VMEM((tiles, slots), jnp.int32)]
        + [pltpu.VMEM((table_rows, lanes), F32)] * accs,
        compiler_params=pltpu.CompilerParams(vmem_limit_bytes=room),
        name="splat",
    )
    image, their_image, grad_mine, grad_other = splat(
        cam,
        rows,
        live_now,
        own_group,
        their_group,
        mine,
        other,
        target,
        message,
        monomials(pixels),
    )

    whole = totals
    before = jnp.zeros_like(totals)
    for core, held in enumerate((mine, other)):
        for m in range(chips):
            mask = 2 * m + core
            if mask:
                theirs = held[m, view_group * FIELDS * GROUPS, 0:views].astype(jnp.int32)
                whole = whole + theirs
                before = before + jnp.where((tile_index ^ mask) < tile_index, theirs, 0)
    next_owner = (before[:, None] + within) * tile_group // whole[:, None]

    grad_other = swap(grad_other, "tile", 1)
    joined = grad_mine + grad_other
    joined, their_image = lax.optimization_barrier((joined, their_image))
    joined = joined.reshape(chips, view_group, FIELDS * GROUPS, lanes)
    part = joined[0]
    for m in reversed(range(1, chips)):
        part = part + swap(joined[m], "tile", 2 * m)
    rendered = jnp.concatenate([image, swap(their_image, "tile", mirror)], axis=2)
    parts = [part[0]] + [swap(part[m], "view", m) for m in reversed(range(1, view_group))]
    tail = pl.pallas_call(
        tail_kernel,
        out_shape=[jax.ShapeDtypeStruct((count, own_count), F32) for count in (3, 6, 1, 3)],
        in_specs=[vmem] * len(parts),
        out_specs=[vmem] * 4,
        scratch_shapes=[pltpu.VMEM((FIELDS * GROUPS, lanes), F32)],
        compiler_params=pltpu.CompilerParams(vmem_limit_bytes=8 * 1024 * 1024),
        name="tail",
    )
    grad_centres, grad_shape, grad_opacity, grad_colours = tail(*parts)
    return (
        rendered.transpose(0, 2, 1, 3),
        grad_centres,
        grad_shape,
        grad_opacity[0],
        grad_colours,
        next_owner,
    )


def solution(mesh):
    in_specs = (
        P(None, ("view", "tile")),
        P(None, ("view", "tile")),
        P(("view", "tile")),
        P(None, ("view", "tile")),
        P(),
        P("view", "tile", None, None),
        P("view", "tile", None),
        P("view", "tile", None),
        P("view", "tile"),
    )
    out_specs = (
        P("view", "tile", None, None),
        P(None, ("view", "tile")),
        P(None, ("view", "tile")),
        P(("view", "tile")),
        P(None, ("view", "tile")),
        P("view", "tile"),
    )
    return jax.shard_map(shards, mesh=mesh, in_specs=in_specs, out_specs=out_specs, check_vma=False)
```

```python
import functools
from functools import partial
import math

import jax
import jax.numpy as jnp
import numpy as np
from jax import lax
from jax.experimental import pallas as pl
from jax.experimental.pallas import tpu as pltpu
from jax.sharding import PartitionSpec as P

F32 = jnp.float32
BF16 = jnp.bfloat16
FIELDS = 13
GROUPS = 8
ACCS = 4
UNROLL = 8
SIZES = 3
BATCH = 8
LOG2E = math.log2(math.e)
OFF = -1e4


def log2_of(n):
    bits = n.bit_length() - 1
    assert n == 1 << bits
    return bits


def pieces_of(value, count):
    out = []
    rest = value
    for _ in range(count - 1):
        piece = rest.astype(BF16).astype(F32)
        out.append(piece)
        rest = rest - piece
    out.append(rest)
    return out


def dot_nn(a, b):
    return lax.dot_general(a, b, (((1,), (0,)), ((), ())), preferred_element_type=F32)


def dot_nt(a, b):
    return lax.dot_general(a, b, (((1,), (1,)), ((), ())), preferred_element_type=F32)


def dot_tn(a, b):
    return lax.dot_general(a, b, (((0,), (0,)), ((), ())), preferred_element_type=F32)


def chunk_rows(live):
    return (live + 7) >> 3


def repeat(count, step, body):
    def trip(i, _):
        for u in range(step):
            body(i * step + u)
        return 0

    lax.fori_loop(0, lax.div(count + (step - 1), step), trip, 0)


def place_slots(dims, me, live_at, ids, order, scratch):
    own_bits, lane_bits, view_bits, tile_bits = dims
    piece_ref, rho_ref, code_ref, lhs_ref, live_full, order_b = scratch
    tiles, slots = ids.shape
    for t in range(tiles):
        live_full[t : t + 1, :] = jnp.full((1, slots), live_at(t), jnp.int32)
    live = live_full[...]
    active = order < live
    upper = (
        lax.broadcasted_iota(jnp.int32, (slots, slots), 0)
        < lax.broadcasted_iota(jnp.int32, (slots, slots), 1)
    ).astype(F32).astype(BF16)
    place = dot_nn(active.astype(F32).astype(BF16), upper).astype(jnp.int32)
    rows = chunk_rows(live)
    chunk = jnp.zeros((tiles, slots), jnp.int32)
    for m in range(1, GROUPS):
        chunk = chunk + (place >= m * rows).astype(jnp.int32)
    rho_ref[...] = jnp.where(active, (place - chunk * rows) * GROUPS + chunk, -1).astype(F32)
    order_b[...] = order.astype(F32)
    owner = (ids >> own_bits) ^ me
    local = ids & ((1 << own_bits) - 1)
    xy_bits = tile_bits - 1
    core = owner & 1
    chip = (owner >> 1) & ((1 << xy_bits) - 1)
    view = owner >> tile_bits
    block = (((core << xy_bits) | chip) << view_bits) | view
    row = (block << lane_bits) | (local & ((1 << lane_bits) - 1))
    code = (row << 3) | (local >> lane_bits)
    piece_ref[0] = (code & 255).astype(F32)
    piece_ref[1] = ((code >> 8) & 255).astype(F32)
    piece_ref[2] = (code >> 16).astype(F32)
    lhs_ref[...] = jnp.zeros_like(lhs_ref)
    down = lax.broadcasted_iota(jnp.int32, (slots, slots), 0).astype(F32).astype(BF16)
    one = jnp.ones((slots, slots), BF16)
    nil = jnp.zeros((slots, slots), BF16)

    def some_tiles(s, _):
        for u in range(UNROLL):
            t = s * UNROLL + u
            for p in range(3):
                lhs_ref[u, p : p + 1, :] = piece_ref[p, pl.ds(t, 1), :]
            picked = jnp.where(down == order_b[pl.ds(t, 1), :].astype(BF16), one, nil)
            ordered = dot_nn(lhs_ref[u].astype(BF16), picked)
            placed = jnp.where(down == rho_ref[pl.ds(t, 1), :].astype(BF16), one, nil)
            out = dot_nt(ordered.astype(BF16), placed)
            code_ref[pl.ds(t, 1), :] = out[0:1] + 256.0 * out[1:2] + 65536.0 * out[2:3]
        return 0

    lax.fori_loop(0, tiles // UNROLL, some_tiles, 0)
    codes = code_ref[...].astype(jnp.int32)
    pos = lax.broadcasted_iota(jnp.int32, (tiles, slots), 1)
    here = (pos >> 3 < rows) & ((pos & 7) * rows + (pos >> 3) < live)
    return codes >> 3, jnp.where(here, codes & 7, GROUPS)


def prep_own_kernel(dims, me_ref, live_ref, camera_ref, ids_ref, order_ref, row_ref, group_ref, cam_ref, *scratch):
    views, tiles_view, _ = ids_ref.shape
    kept = tiles_view // 2
    me = me_ref[0]
    first = (me >> dims[3]) * views
    for v in range(views):
        for i in range(2):
            for j in range(4):
                cam_ref[v * 8 + i * 4 + j] = camera_ref[first + v, i, j]
    ids = jnp.concatenate([ids_ref[v, 0:kept, :] for v in range(views)], axis=0)
    order = jnp.concatenate([order_ref[v, 0:kept, :] for v in range(views)], axis=0)
    live_at = lambda t: live_ref[t // kept, t % kept]
    row_ref[...], group_ref[...] = place_slots(dims, me, live_at, ids, order, scratch)


def prep_their_kernel(dims, me_ref, live_ref, message_ref, row_ref, group_ref, *scratch):
    tiles, slots = group_ref.shape
    total = live_ref.shape[0]
    ids = message_ref[0:tiles, :].astype(jnp.int32)
    order = message_ref[tiles : 2 * tiles, :].astype(jnp.int32)
    live_at = lambda t: live_ref[total - tiles + t]
    row_ref[0:tiles, :], group_ref[...] = place_slots(dims, me_ref[0], live_at, ids, order, scratch)
    lane = lax.broadcasted_iota(jnp.int32, (total, slots), 1)
    above = lax.broadcasted_iota(jnp.int32, (total, slots), 0)
    across = jnp.full((total, slots), -1, jnp.int32)
    down = jnp.zeros((total, slots), jnp.int32)
    for t in range(total):
        across = jnp.where(lane == t, live_ref[t], across)
        down = jnp.where(above == t, live_ref[t], down)
    ahead = (across > down) | ((across == down) & (lane < above))
    rank = jnp.sum(ahead.astype(jnp.int32), axis=1, keepdims=True)
    ranked = jnp.sum(jnp.where(rank == lane, above, 0), axis=0, keepdims=True)
    for n in range(1, SIZES):
        over = jnp.sum((across > slots >> n).astype(jnp.int32), axis=1, keepdims=True)[0:1]
        ranked = jnp.where(lane[0:1] == total + n - 1, over, ranked)
    row_ref[tiles : tiles + 1, :] = ranked


def splat_kernel(
    dims,
    cam_ref,
    row_ref,
    live_ref,
    own_group_ref,
    their_group_ref,
    mine_ref,
    other_ref,
    target_ref,
    message_ref,
    mono_ref,
    image_ref,
    their_image_ref,
    grad_mine_ref,
    grad_other_ref,
    *scratch,
):
    views, tiles_view, slots, pixels, lanes, column = dims
    table, buf, raw, rec, mom, grad, c_s, h_s, w_hi, w_lo, g_1, g_2, g_3, row_s, row_2, want, got, group_ref = scratch[:18]
    accs = scratch[18:]
    tiles = views * tiles_view
    chips = mine_ref.shape[0]
    half = chips * column
    used = FIELDS * GROUPS
    pad = jnp.zeros((lanes - used, lanes), F32)

    for acc in accs:
        acc[...] = jnp.zeros_like(acc)
    for ref in (buf, w_hi, w_lo, g_1, g_2, g_3, row_s, row_2):
        ref[...] = jnp.zeros_like(ref)

    kept = tiles_view // 2
    part_tiles = views * kept
    for v in range(views):
        for c in range(3):
            want[v, c, :, :] = target_ref[v, c, 0:kept, :]
            start = 2 * part_tiles + (v * 3 + c) * kept
            want[views + v, c, :, :] = message_ref[start : start + kept, :]
    group_ref[0:part_tiles, :] = own_group_ref[...]
    group_ref[part_tiles:, :] = their_group_ref[...]

    def build(q, _):
        for base, ref in ((0, mine_ref), (half, other_ref)):
            for d in range(column):
                block = jnp.concatenate([ref[q, d * used : (d + 1) * used, :], pad], axis=0)
                start = pl.multiple_of((base + q * column + d) * lanes, lanes)
                table[pl.ds(start, lanes), :] = jnp.transpose(block)
        return 0

    lax.fori_loop(0, chips, build, 0)

    def live_of(t):
        return live_ref[t]

    sizes = [slots >> n for n in range(SIZES)]

    def in_turn(body):
        def trip(s, _, positions):
            body([row_ref[tiles * slots + s * BATCH + g] for g in range(BATCH)], positions)
            return 0

        start = 0
        for n, positions in enumerate(sizes):
            over = row_ref[tiles * slots + tiles + n] if n + 1 < len(sizes) else tiles
            end = lax.div(over + (BATCH - 1), BATCH)
            lax.fori_loop(start, end, partial(trip, positions=positions), 0)
            start = end

    sub = lax.broadcasted_iota(jnp.int32, (GROUPS, slots), 0)

    def widen(row):
        spare = slots - row.shape[1]
        return jnp.concatenate([row, jnp.zeros((1, spare), F32)], axis=1) if spare else row

    def fetch(tile, positions):
        for g, t in enumerate(tile):

            def copy(i, t=t, g=g):
                for k in range(GROUPS):
                    buf[g, pl.ds(i * GROUPS + k, 1), :] = table[pl.ds(row_ref[t * slots + i * GROUPS + k], 1), :]

            repeat(chunk_rows(live_of(t)), 4, copy)
        for g, t in enumerate(tile):
            turned = jnp.transpose(buf[g, 0:positions, :])
            mine = sub[:, 0:positions] == group_ref[pl.ds(t, 1), :][:, 0:positions]
            for f in range(FIELDS):
                part = jnp.where(mine, turned[f * GROUPS : (f + 1) * GROUPS], 0.0)
                raw[f, pl.ds(t, 1), :] = widen(jnp.sum(part, axis=0, keepdims=True))

    in_turn(fetch)

    def project(v):
        block = slice(v * kept, (v + 1) * kept)
        cam = [cam_ref[v % views * 8 + n] for n in range(8)]
        field = lambda f: raw[f, block, :]
        u = cam[0] * field(0) + cam[1] * field(1) + cam[2] * field(2) + cam[3]
        w = cam[4] * field(0) + cam[5] * field(1) + cam[6] * field(2) + cam[7]
        d0, d1, d2 = jnp.exp(field(3)), jnp.exp(field(5)), jnp.exp(field(8))
        factor = []
        for i in range(2):
            m = cam[4 * i : 4 * i + 3]
            factor.append(
                (
                    m[0] * d0 + m[1] * field(4) + m[2] * field(6),
                    m[1] * d1 + m[2] * field(7),
                    m[2] * d2,
                )
            )
        f0, f1 = factor
        s00 = f0[0] * f0[0] + f0[1] * f0[1] + f0[2] * f0[2] + 0.3
        s01 = f0[0] * f1[0] + f0[1] * f1[1] + f0[2] * f1[2]
        s11 = f1[0] * f1[0] + f1[1] * f1[1] + f1[2] * f1[2] + 0.3
        inverse = 1.0 / (s00 * s11 - s01 * s01)
        conic = (s11 * inverse, -s01 * inverse, s00 * inverse)
        here = group_ref[block, :] < GROUPS
        return here, cam, block, u, w, (d0, d1, d2), f0, f1, conic

    for v in range(2 * views):
        here, cam, block, u, w, _, _, _, (ka, kb, kc) = project(v)
        x_line = ka * u + kb * w
        y_line = kb * u + kc * w
        log_opacity = math.log(0.95) - jnp.log(1.0 + jnp.exp(-raw[9, block, :]))
        level = log_opacity - 0.5 * (u * x_line + w * y_line)
        terms = (-0.5 * ka, -kb, -0.5 * kc, x_line, y_line)
        for n, term in enumerate(terms):
            rec[n, block, :] = jnp.where(here, term * LOG2E, 0.0)
        rec[5, block, :] = jnp.where(here, level * LOG2E, OFF)
        for c in range(3):
            rec[6 + c, block, :] = raw[10 + c, block, :]

    lane_row = lax.broadcasted_iota(jnp.int32, (GROUPS, pixels), 0)
    own_chunk = (lax.broadcasted_iota(jnp.int32, (GROUPS, slots), 1) & 7) == sub
    zero_pix = jnp.zeros((8, pixels), F32)

    def paired(a, b):
        return a + pltpu.roll(b, 3, 0)

    def render(tile, positions):
        zero_rows = jnp.zeros((8, positions), F32)
        used = slice(0, positions)
        blocks = (chunk_rows(functools.reduce(jnp.maximum, [live_of(t) for t in tile])) + 3) >> 2
        for g, t in enumerate(tile):
            for n in range(6):
                row_s[g, n : n + 1, :] = rec[n, pl.ds(t, 1), :]
            for c in range(3):
                row_s[g, 8 + c : 9 + c, :] = rec[6 + c, pl.ds(t, 1), :]
        for g in range(BATCH):
            lhs = jnp.concatenate(pieces_of(row_s[g, 0:8, used], 3) + [zero_rows], axis=0).astype(BF16)
            c_s[g, used, :] = dot_tn(lhs, mono_ref[...])
        colour = [pieces_of(row_s[g, 8:16, used], 3) for g in range(BATCH)]

        def through(i, prods):
            rows = pl.ds(pl.multiple_of(i * 32, 32), 32)
            out = []
            for g in range(BATCH):
                cover = jnp.exp2(c_s[g, rows, :])
                c_s[g, rows, :] = cover
                keep = 1.0 - cover
                out.append(prods[g] * ((keep[0:8] * keep[8:16]) * (keep[16:24] * keep[24:32])))
            return tuple(out)

        ones = jnp.ones((GROUPS, pixels), F32)
        lead = list(lax.fori_loop(0, blocks, through, (ones,) * BATCH))
        for g in range(BATCH):
            scan = lead[g]
            for step in (1, 2, 4):
                scan = scan * jnp.where(lane_row >= step, pltpu.roll(scan, step, 0), 1.0)
            lead[g] = jnp.where(lane_row >= 1, pltpu.roll(scan, 1, 0), 1.0)

        def weights(cover, prod):
            out = []
            for h in range(4):
                weight = prod * cover[8 * h : 8 * h + 8]
                prod = prod - weight
                out.append(weight)
            return out, prod

        def weigh(i, prods):
            rows = pl.ds(pl.multiple_of(i * 32, 32), 32)
            out = []
            for g in range(BATCH):
                parts, prod = weights(c_s[g, rows, :], prods[g])
                weight = jnp.concatenate(parts, axis=0)
                high = weight.astype(BF16)
                w_hi[g, rows, :] = high
                w_lo[g, rows, :] = (weight - high.astype(F32)).astype(BF16)
                out.append(prod)
            return tuple(out)

        lax.fori_loop(0, blocks, weigh, tuple(lead))

        after = []
        for g, t in enumerate(tile):
            v, tl = lax.div(t, kept), lax.rem(t, kept)
            spread = [
                jnp.where(own_chunk[:, used], jnp.broadcast_to(piece[c : c + 1], (GROUPS, positions)), 0.0)
                for c in range(3)
                for piece in colour[g]
            ]
            lhs = jnp.concatenate(spread + [zero_rows], axis=0).astype(BF16)
            image = dot_nn(lhs, w_hi[g, used, :]) + dot_nn(lhs, w_lo[g, used, :])
            rest = jnp.zeros((GROUPS, pixels), F32)
            for c in range(3):
                part = image[24 * c : 24 * c + 8] + image[24 * c + 8 : 24 * c + 16] + image[24 * c + 16 : 24 * c + 24]
                whole = jnp.sum(part, axis=0, keepdims=True)
                got[v, c, pl.ds(tl, 1), :] = whole
                miss = whole - want[v, c, pl.ds(tl, 1), :]
                row_2[g, c : c + 1, :] = miss
                rest = rest + part * miss
            for step in (1, 2, 4):
                rest = rest + jnp.where(lane_row < GROUPS - step, pltpu.roll(rest, GROUPS - step, 0), 0.0)
            after.append(rest)
        missed = [pieces_of(row_2[g], 3) for g in range(BATCH)]
        for g in range(BATCH):
            c1, c2, c3 = colour[g]
            m1, m2, m3 = missed[g]
            lhs = jnp.concatenate([paired(c1, c1), paired(c2, c1), paired(c2, c3), zero_rows], axis=0)
            rhs = jnp.concatenate([paired(m1, m2), paired(m1, m3), paired(m2, m1), zero_pix], axis=0)
            h_s[g, used, :] = dot_tn(lhs.astype(BF16), rhs.astype(BF16))

        def settle(i, carry):
            rows = pl.ds(pl.multiple_of(i * 32, 32), 32)
            out = []
            for g in range(BATCH):
                prod, tail = carry[g]
                cover = c_s[g, rows, :]
                pull = h_s[g, rows, :]
                parts, prod = weights(cover, prod)
                ratio = cover / (1.0 - cover)
                slopes = []
                for h in range(4):
                    cut = slice(8 * h, 8 * h + 8)
                    part = parts[h] * pull[cut]
                    tail = tail - part
                    slopes.append(part - ratio[cut] * tail)
                slope = jnp.concatenate(slopes, axis=0)
                high = slope.astype(BF16)
                rest = slope - high.astype(F32)
                middle = rest.astype(BF16)
                g_1[g, rows, :] = high
                g_2[g, rows, :] = middle
                g_3[g, rows, :] = (rest - middle.astype(F32)).astype(BF16)
                out.append((prod, tail))
            return tuple(out)

        lax.fori_loop(0, blocks, settle, tuple(zip(lead, after)))
        mono = mono_ref[0:16, :]
        for g in range(BATCH):
            moments = dot_nt(mono, g_1[g, used, :]) + dot_nt(mono, g_2[g, used, :]) + dot_nt(mono, g_3[g, used, :])
            miss_lhs = jnp.concatenate(missed[g] + [zero_pix], axis=0).astype(BF16)
            tint = dot_nt(miss_lhs, w_hi[g, used, :]) + dot_nt(miss_lhs, w_lo[g, used, :])
            row_s[g, 0:8, used] = moments[0:8]
            row_s[g, 8:16, used] = tint[0:8] + tint[8:16] + tint[16:24]
        for g, t in enumerate(tile):
            for n in range(6):
                mom[n, pl.ds(t, 1), :] = row_s[g, n : n + 1, :]
            for c in range(3):
                mom[6 + c, pl.ds(t, 1), :] = row_s[g, 8 + c : 9 + c, :]

    in_turn(render)
    image_ref[...] = got[0:views]
    their_image_ref[...] = got[views:]

    for v in range(2 * views):
        here, cam, block, u, w, (d0, d1, d2), f0, f1, (ka, kb, kc) = project(v)
        mxx, mxy, myy, mx, my, m1 = [jnp.where(here, mom[n, block, :], 0.0) for n in range(6)]
        dx = mx - u * m1
        dy = my - w * m1
        dxx = mxx - 2.0 * u * mx + u * u * m1
        dxy = mxy - u * my - w * mx + u * w * m1
        dyy = myy - 2.0 * w * my + w * w * m1
        gu = ka * dx + kb * dy
        gw = kb * dx + kc * dy
        ax, ay = ka * dxx + kb * dxy, ka * dxy + kb * dyy
        bx, by = kb * dxx + kc * dxy, kb * dxy + kc * dyy
        h00 = ax * ka + ay * kb
        h01 = ax * kb + ay * kc
        h11 = bx * kb + by * kc
        g0 = [h00 * f0[j] + h01 * f1[j] for j in range(3)]
        g1 = [h01 * f0[j] + h11 * f1[j] for j in range(3)]
        for k in range(3):
            grad[k, block, :] = cam[k] * gu + cam[4 + k] * gw
        grad[3, block, :] = (cam[0] * g0[0] + cam[4] * g1[0]) * d0
        grad[4, block, :] = cam[1] * g0[0] + cam[5] * g1[0]
        grad[5, block, :] = (cam[1] * g0[1] + cam[5] * g1[1]) * d1
        grad[6, block, :] = cam[2] * g0[0] + cam[6] * g1[0]
        grad[7, block, :] = cam[2] * g0[1] + cam[6] * g1[1]
        grad[8, block, :] = (cam[2] * g0[2] + cam[6] * g1[2]) * d2
        grad[9, block, :] = m1 - m1 / (1.0 + jnp.exp(-raw[9, block, :]))
        for c in range(3):
            grad[10 + c, block, :] = mom[6 + c, block, :]

    def give(tile, positions):
        for g, t in enumerate(tile):
            mine = sub[:, 0:positions] == group_ref[pl.ds(t, 1), :][:, 0:positions]
            spread = [
                jnp.where(mine, jnp.broadcast_to(grad[f, pl.ds(t, 1), :][:, 0:positions], (GROUPS, positions)), 0.0)
                for f in range(FIELDS)
            ]
            spread.append(jnp.zeros((lanes - used, positions), F32))
            buf[g, 0:positions, :] = jnp.transpose(jnp.concatenate(spread, axis=0))
        for g, t in enumerate(tile):

            def add(i, t=t, g=g):
                for k in range(0, GROUPS, len(accs)):
                    where = [row_ref[t * slots + i * GROUPS + k + n] for n in range(len(accs))]
                    olds = [accs[n][pl.ds(where[n], 1), :] for n in range(len(accs))]
                    news = [buf[g, pl.ds(i * GROUPS + k + n, 1), :] for n in range(len(accs))]
                    for n in range(len(accs)):
                        accs[n][pl.ds(where[n], 1), :] = olds[n] + news[n]

            repeat(chunk_rows(live_of(t)), 4, add)

    in_turn(give)

    def finish(q, _):
        for base, ref in ((0, grad_mine_ref), (half, grad_other_ref)):
            for d in range(column):
                start = pl.multiple_of((base + q * column + d) * lanes, lanes)
                total = accs[0][pl.ds(start, lanes), :]
                for acc in accs[1:]:
                    total = total + acc[pl.ds(start, lanes), :]
                ref[q * column + d] = jnp.transpose(total)[0:used]
        return 0

    lax.fori_loop(0, chips, finish, 0)


def tail_kernel(*refs):
    parts, (centres_ref, shape_ref, opacity_ref, colours_ref), total = refs[:-5], refs[-5:-1], refs[-1]
    lanes = total.shape[1]
    value = parts[0][...]
    for part in parts[1:]:
        value = value + part[...]
    total[...] = value
    field = 0
    for ref in (centres_ref, shape_ref, opacity_ref, colours_ref):
        for row in range(ref.shape[0]):
            for k in range(GROUPS):
                at = field * GROUPS + k
                ref[row : row + 1, k * lanes : (k + 1) * lanes] = total[at : at + 1, :]
            field += 1


def monomials(pixels):
    side = math.isqrt(pixels)
    index = np.arange(pixels)
    x = (index % side) - (side - 1) / 2.0
    y = (index // side) - (side - 1) / 2.0
    one = np.ones_like(x)
    zero = np.zeros_like(x)
    group = np.stack([x * x, x * y, y * y, x, y, one, zero, zero])
    return jnp.asarray(np.concatenate([group, group, group, np.zeros_like(group)]), BF16)


def gather(array, axis, masks):
    got = {mask: swap(array, axis, mask) for mask in sorted(masks, reverse=True)}
    return [got[mask] for mask in masks]


def swap(array, axis, mask):
    size = lax.axis_size(axis)
    return lax.ppermute(array, axis, [(i, i ^ mask) for i in range(size)])


def shards(centres, shape_raw, opacity_logit, colours, camera, target, intersection_ids, depth_order, live_count):
    view_group = lax.axis_size("view")
    tile_group = lax.axis_size("tile")
    devices = view_group * tile_group
    chips = tile_group // 2
    own_count = centres.shape[1]
    lanes = own_count // GROUPS
    views, tiles_view, slots = intersection_ids.shape
    tiles = views * tiles_view
    pixels = target.shape[3]
    view_index = lax.axis_index("view")
    tile_index = lax.axis_index("tile")
    me = (view_index * tile_group + tile_index).astype(jnp.int32)

    totals = jnp.sum(live_count, axis=1)
    place = lax.broadcasted_iota(jnp.int32, (1, tiles_view, tiles_view), 2)
    earlier = place < lax.broadcasted_iota(jnp.int32, (1, tiles_view, tiles_view), 1)
    within = jnp.sum(jnp.where(earlier, live_count[:, None, :], 0), axis=2)

    smem = pl.BlockSpec(memory_space=pltpu.SMEM)
    vmem = pl.BlockSpec(memory_space=pltpu.VMEM)
    kept = tiles_view // 2
    part_tiles = views * kept
    dims = (log2_of(own_count), log2_of(lanes), log2_of(view_group), log2_of(tile_group))
    prep_options = dict(
        scratch_shapes=[
            pltpu.VMEM((3, part_tiles, slots), F32),
            pltpu.VMEM((part_tiles, slots), F32),
            pltpu.VMEM((part_tiles, slots), F32),
            pltpu.VMEM((UNROLL, 16, slots), F32),
            pltpu.VMEM((part_tiles, slots), jnp.int32),
            pltpu.VMEM((part_tiles, slots), F32),
        ],
        compiler_params=pltpu.CompilerParams(vmem_limit_bytes=8 * 1024 * 1024),
        cost_estimate=pl.CostEstimate(flops=4_000_000_000, bytes_accessed=8 * tiles * slots, transcendentals=0),
    )
    prep_own = pl.pallas_call(
        partial(prep_own_kernel, dims),
        out_shape=[
            jax.ShapeDtypeStruct((part_tiles, slots), jnp.int32),
            jax.ShapeDtypeStruct((part_tiles, slots), jnp.int32),
            jax.ShapeDtypeStruct((views * 8,), F32),
        ],
        in_specs=[smem] * 3 + [vmem] * 2,
        out_specs=[vmem, vmem, smem],
        name="prep_own",
        **prep_options,
    )
    prep_their = pl.pallas_call(
        partial(prep_their_kernel, dims),
        out_shape=[
            jax.ShapeDtypeStruct((part_tiles + 8, slots), jnp.int32),
            jax.ShapeDtypeStruct((part_tiles, slots), jnp.int32),
        ],
        in_specs=[smem] * 2 + [vmem],
        out_specs=[vmem] * 2,
        name="prep_their",
        **prep_options,
    )

    mirror = tile_group - 1
    target = target.transpose(0, 2, 1, 3)
    message = jnp.concatenate(
        [
            intersection_ids[:, kept:].reshape(part_tiles, slots).astype(F32),
            depth_order[:, kept:].reshape(part_tiles, slots).astype(F32),
            target[:, :, kept:].reshape(3 * part_tiles, pixels),
            jnp.pad(live_count[:, kept:].astype(F32), ((0, 8 - views), (0, slots - kept))),
        ]
    )
    fields = jnp.concatenate([centres, shape_raw, opacity_logit[None], colours], axis=0)
    block = fields.reshape(FIELDS * GROUPS, lanes)
    note = jnp.pad(totals.astype(F32)[None], ((0, 7), (0, lanes - views)))
    column = jnp.concatenate([block] + gather(block, "view", range(1, view_group)) + [note])
    message = swap(message, "tile", mirror)
    column, me = lax.optimization_barrier((column, me))
    mine = jnp.stack([column] + gather(column, "tile", range(2, tile_group, 2)))
    own_rows, own_group, cam = prep_own(me[None], live_count, camera, intersection_ids, depth_order)
    their_live = message[5 * part_tiles : 5 * part_tiles + views, :kept].astype(jnp.int32)
    live_now = jnp.concatenate([live_count[:, :kept].reshape(-1), their_live.reshape(-1)])
    their_rows, their_group = prep_their(me[None], live_now, message)
    rows = jnp.concatenate([own_rows, their_rows]).reshape(-1)
    mine, rows, own_group, their_group, cam = lax.optimization_barrier((mine, rows, own_group, their_group, cam))
    other = swap(mine, "tile", 1)

    table_rows = devices * lanes
    square = (BATCH, slots, pixels)
    half = (chips * view_group, FIELDS * GROUPS, lanes)
    accs = ACCS if devices <= 32 else 2
    room = 4 * table_rows * lanes * (accs + 2) + 16 * 1024 * 1024
    splat = pl.pallas_call(
        partial(splat_kernel, (views, tiles_view, slots, pixels, lanes, view_group)),
        out_shape=[
            jax.ShapeDtypeStruct((views, 3, kept, pixels), F32),
            jax.ShapeDtypeStruct((views, 3, tiles_view - kept, pixels), F32),
            jax.ShapeDtypeStruct(half, F32),
            jax.ShapeDtypeStruct(half, F32),
        ],
        in_specs=[smem] * 3 + [vmem] * 7,
        out_specs=[vmem] * 4,
        scratch_shapes=[
            pltpu.VMEM((table_rows, lanes), F32),
            pltpu.VMEM((BATCH, slots, lanes), F32),
            pltpu.VMEM((FIELDS, tiles, slots), F32),
            pltpu.VMEM((9, tiles, slots), F32),
            pltpu.VMEM((9, tiles, slots), F32),
            pltpu.VMEM((FIELDS, tiles, slots), F32),
            pltpu.VMEM(square, F32),
            pltpu.VMEM(square, F32),
        ]
        + [pltpu.VMEM(square, BF16)] * 5
        + [pltpu.VMEM((BATCH, 16, slots), F32), pltpu.VMEM((BATCH, 8, pixels), F32)]
        + [pltpu.VMEM((2 * views, 3, kept, pixels), F32)] * 2
        + [pltpu.VMEM((tiles, slots), jnp.int32)]
        + [pltpu.VMEM((table_rows, lanes), F32)] * accs,
        compiler_params=pltpu.CompilerParams(vmem_limit_bytes=room),
        name="splat",
    )
    image, their_image, grad_mine, grad_other = splat(
        cam,
        rows,
        live_now,
        own_group,
        their_group,
        mine,
        other,
        target,
        message,
        monomials(pixels),
    )

    row = view_group * FIELDS * GROUPS
    counts = jnp.stack([mine[:, row, 0:views], other[:, row, 0:views]], axis=1)
    counts = counts.reshape(tile_group, views).astype(jnp.int32)
    peer = lax.broadcasted_iota(jnp.int32, counts.shape, 0) ^ tile_index
    whole = jnp.sum(counts, axis=0)
    before = jnp.sum(jnp.where(peer < tile_index, counts, 0), axis=0)
    next_owner = (before[:, None] + within) * tile_group // whole[:, None]

    grad_other = swap(grad_other, "tile", 1)
    joined = grad_mine + grad_other
    joined, their_image = lax.optimization_barrier((joined, their_image))
    joined = joined.reshape(chips, view_group, FIELDS * GROUPS, lanes)
    part = joined[0]
    for m in reversed(range(1, chips)):
        part = part + swap(joined[m], "tile", 2 * m)
    rendered = jnp.concatenate([image, swap(their_image, "tile", mirror)], axis=2)
    parts = [part[0]] + [swap(part[m], "view", m) for m in reversed(range(1, view_group))]
    tail = pl.pallas_call(
        tail_kernel,
        out_shape=[jax.ShapeDtypeStruct((count, own_count), F32) for count in (3, 6, 1, 3)],
        in_specs=[vmem] * len(parts),
        out_specs=[vmem] * 4,
        scratch_shapes=[pltpu.VMEM((FIELDS * GROUPS, lanes), F32)],
        compiler_params=pltpu.CompilerParams(vmem_limit_bytes=8 * 1024 * 1024),
        name="tail",
    )
    grad_centres, grad_shape, grad_opacity, grad_colours = tail(*parts)
    return (
        rendered.transpose(0, 2, 1, 3),
        grad_centres,
        grad_shape,
        grad_opacity[0],
        grad_colours,
        next_owner,
    )


def solution(mesh):
    in_specs = (
        P(None, ("view", "tile")),
        P(None, ("view", "tile")),
        P(("view", "tile")),
        P(None, ("view", "tile")),
        P(),
        P("view", "tile", None, None),
        P("view", "tile", None),
        P("view", "tile", None),
        P("view", "tile"),
    )
    out_specs = (
        P("view", "tile", None, None),
        P(None, ("view", "tile")),
        P(None, ("view", "tile")),
        P(("view", "tile")),
        P(None, ("view", "tile")),
        P("view", "tile"),
    )
    return jax.shard_map(shards, mesh=mesh, in_specs=in_specs, out_specs=out_specs, check_vma=False)
```

```python
import functools
from functools import partial
import math

import jax
import jax.numpy as jnp
import numpy as np
from jax import lax
from jax.experimental import pallas as pl
from jax.experimental.pallas import tpu as pltpu
from jax.sharding import PartitionSpec as P

F32 = jnp.float32
BF16 = jnp.bfloat16
FIELDS = 13
GROUPS = 8
ACCS = 4
UNROLL = 8
SIZES = 3
BATCH = 8
SWEEP = 4
LOG2E = math.log2(math.e)
OFF = -1e4


def log2_of(n):
    bits = n.bit_length() - 1
    assert n == 1 << bits
    return bits


def pieces_of(value, count):
    out = []
    rest = value
    for _ in range(count - 1):
        piece = rest.astype(BF16).astype(F32)
        out.append(piece)
        rest = rest - piece
    out.append(rest)
    return out


def dot_nn(a, b):
    return lax.dot_general(a, b, (((1,), (0,)), ((), ())), preferred_element_type=F32)


def dot_nt(a, b):
    return lax.dot_general(a, b, (((1,), (1,)), ((), ())), preferred_element_type=F32)


def dot_tn(a, b):
    return lax.dot_general(a, b, (((0,), (0,)), ((), ())), preferred_element_type=F32)


def chunk_rows(live):
    return (live + 7) >> 3


def repeat(count, step, body):
    def trip(i, _):
        for u in range(step):
            body(i * step + u)
        return 0

    lax.fori_loop(0, lax.div(count + (step - 1), step), trip, 0)


def place_slots(dims, me, live_at, ids, order, scratch):
    own_bits, lane_bits, view_bits, tile_bits = dims
    piece_ref, rho_ref, code_ref, lhs_ref, live_full, order_b = scratch
    tiles, slots = ids.shape
    for t in range(tiles):
        live_full[t : t + 1, :] = jnp.full((1, slots), live_at(t), jnp.int32)
    live = live_full[...]
    active = order < live
    upper = (
        lax.broadcasted_iota(jnp.int32, (slots, slots), 0)
        < lax.broadcasted_iota(jnp.int32, (slots, slots), 1)
    ).astype(F32).astype(BF16)
    place = dot_nn(active.astype(F32).astype(BF16), upper).astype(jnp.int32)
    rows = chunk_rows(live)
    chunk = jnp.zeros((tiles, slots), jnp.int32)
    for m in range(1, GROUPS):
        chunk = chunk + (place >= m * rows).astype(jnp.int32)
    rho_ref[...] = jnp.where(active, (place - chunk * rows) * GROUPS + chunk, -1).astype(F32)
    order_b[...] = order.astype(F32)
    owner = (ids >> own_bits) ^ me
    local = ids & ((1 << own_bits) - 1)
    xy_bits = tile_bits - 1
    core = owner & 1
    chip = (owner >> 1) & ((1 << xy_bits) - 1)
    view = owner >> tile_bits
    block = (((core << xy_bits) | chip) << view_bits) | view
    row = (block << lane_bits) | (local & ((1 << lane_bits) - 1))
    code = (row << 3) | (local >> lane_bits)
    piece_ref[0] = (code & 255).astype(F32)
    piece_ref[1] = ((code >> 8) & 255).astype(F32)
    piece_ref[2] = (code >> 16).astype(F32)
    lhs_ref[...] = jnp.zeros_like(lhs_ref)
    down = lax.broadcasted_iota(jnp.int32, (slots, slots), 0).astype(F32).astype(BF16)
    one = jnp.ones((slots, slots), BF16)
    nil = jnp.zeros((slots, slots), BF16)

    def some_tiles(s, _):
        for u in range(UNROLL):
            t = s * UNROLL + u
            for p in range(3):
                lhs_ref[u, p : p + 1, :] = piece_ref[p, pl.ds(t, 1), :]
            picked = jnp.where(down == order_b[pl.ds(t, 1), :].astype(BF16), one, nil)
            ordered = dot_nn(lhs_ref[u].astype(BF16), picked)
            placed = jnp.where(down == rho_ref[pl.ds(t, 1), :].astype(BF16), one, nil)
            out = dot_nt(ordered.astype(BF16), placed)
            code_ref[pl.ds(t, 1), :] = out[0:1] + 256.0 * out[1:2] + 65536.0 * out[2:3]
        return 0

    lax.fori_loop(0, tiles // UNROLL, some_tiles, 0)
    codes = code_ref[...].astype(jnp.int32)
    pos = lax.broadcasted_iota(jnp.int32, (tiles, slots), 1)
    here = (pos >> 3 < rows) & ((pos & 7) * rows + (pos >> 3) < live)
    return codes >> 3, jnp.where(here, codes & 7, GROUPS)


def prep_own_kernel(dims, me_ref, live_ref, camera_ref, ids_ref, order_ref, row_ref, group_ref, cam_ref, *scratch):
    views, tiles_view, _ = ids_ref.shape
    kept = tiles_view // 2
    me = me_ref[0]
    first = (me >> dims[3]) * views
    for v in range(views):
        for i in range(2):
            for j in range(4):
                cam_ref[v * 8 + i * 4 + j] = camera_ref[first + v, i, j]
    ids = jnp.concatenate([ids_ref[v, 0:kept, :] for v in range(views)], axis=0)
    order = jnp.concatenate([order_ref[v, 0:kept, :] for v in range(views)], axis=0)
    live_at = lambda t: live_ref[t // kept, t % kept]
    row_ref[...], group_ref[...] = place_slots(dims, me, live_at, ids, order, scratch)


def prep_their_kernel(dims, me_ref, live_ref, message_ref, row_ref, group_ref, *scratch):
    tiles, slots = group_ref.shape
    total = live_ref.shape[0]
    ids = message_ref[0:tiles, :].astype(jnp.int32)
    order = message_ref[tiles : 2 * tiles, :].astype(jnp.int32)
    live_at = lambda t: live_ref[total - tiles + t]
    row_ref[0:tiles, :], group_ref[...] = place_slots(dims, me_ref[0], live_at, ids, order, scratch)
    lane = lax.broadcasted_iota(jnp.int32, (total, slots), 1)
    above = lax.broadcasted_iota(jnp.int32, (total, slots), 0)
    across = jnp.full((total, slots), -1, jnp.int32)
    down = jnp.zeros((total, slots), jnp.int32)
    for t in range(total):
        across = jnp.where(lane == t, live_ref[t], across)
        down = jnp.where(above == t, live_ref[t], down)
    ahead = (across > down) | ((across == down) & (lane < above))
    rank = jnp.sum(ahead.astype(jnp.int32), axis=1, keepdims=True)
    ranked = jnp.sum(jnp.where(rank == lane, above, 0), axis=0, keepdims=True)
    for n in range(1, SIZES):
        over = jnp.sum((across > slots >> n).astype(jnp.int32), axis=1, keepdims=True)[0:1]
        ranked = jnp.where(lane[0:1] == total + n - 1, over, ranked)
    row_ref[tiles : tiles + 1, :] = ranked


def splat_kernel(
    dims,
    cam_ref,
    row_ref,
    live_ref,
    own_group_ref,
    their_group_ref,
    mine_ref,
    other_ref,
    target_ref,
    message_ref,
    mono_ref,
    image_ref,
    their_image_ref,
    grad_mine_ref,
    grad_other_ref,
    *scratch,
):
    views, tiles_view, slots, pixels, lanes, column = dims
    table, buf, raw, rec, mom, grad, c_s, h_s, w_hi, w_lo, g_1, g_2, g_3, row_s, row_2, want, got, group_ref = scratch[:18]
    accs = scratch[18:]
    tiles = views * tiles_view
    chips = mine_ref.shape[0]
    half = chips * column
    used = FIELDS * GROUPS
    pad = jnp.zeros((lanes - used, lanes), F32)

    for acc in accs:
        acc[...] = jnp.zeros_like(acc)
    for ref in (w_hi, w_lo, row_s, row_2):
        ref[...] = jnp.zeros_like(ref)

    kept = tiles_view // 2
    part_tiles = views * kept
    for v in range(views):
        for c in range(3):
            want[v, c, :, :] = target_ref[v, c, 0:kept, :]
            start = 2 * part_tiles + (v * 3 + c) * kept
            want[views + v, c, :, :] = message_ref[start : start + kept, :]
    group_ref[0:part_tiles, :] = own_group_ref[...]
    group_ref[part_tiles:, :] = their_group_ref[...]

    def build(q, _):
        for base, ref in ((0, mine_ref), (half, other_ref)):
            for d in range(column):
                block = jnp.concatenate([ref[q, d * used : (d + 1) * used, :], pad], axis=0)
                start = pl.multiple_of((base + q * column + d) * lanes, lanes)
                table[pl.ds(start, lanes), :] = jnp.transpose(block)
        return 0

    lax.fori_loop(0, chips, build, 0)

    def live_of(t):
        return live_ref[t]

    sizes = [slots >> n for n in range(SIZES)]

    def in_turn(body):
        def trip(s, _, positions):
            body([row_ref[tiles * slots + s * BATCH + g] for g in range(BATCH)], positions)
            return 0

        start = 0
        for n, positions in enumerate(sizes):
            over = row_ref[tiles * slots + tiles + n] if n + 1 < len(sizes) else tiles
            end = lax.div(over + (BATCH - 1), BATCH)
            lax.fori_loop(start, end, partial(trip, positions=positions), 0)
            start = end

    sub = lax.broadcasted_iota(jnp.int32, (GROUPS, slots), 0)

    def widen(row):
        spare = slots - row.shape[1]
        return jnp.concatenate([row, jnp.zeros((1, spare), F32)], axis=1) if spare else row

    def fetch(tile, positions):
        for g, t in enumerate(tile):

            def copy(i, t=t, g=g):
                for k in range(GROUPS):
                    buf[g, pl.ds(i * GROUPS + k, 1), :] = table[pl.ds(row_ref[t * slots + i * GROUPS + k], 1), :]

            repeat(chunk_rows(live_of(t)), 4, copy)
        for g, t in enumerate(tile):
            turned = jnp.transpose(buf[g, 0:positions, :])
            mine = sub[:, 0:positions] == group_ref[pl.ds(t, 1), :][:, 0:positions]
            for f in range(FIELDS):
                part = jnp.where(mine, turned[f * GROUPS : (f + 1) * GROUPS], 0.0)
                raw[f, pl.ds(t, 1), :] = widen(jnp.sum(part, axis=0, keepdims=True))

    in_turn(fetch)

    def project(v):
        block = slice(v * kept, (v + 1) * kept)
        cam = [cam_ref[v % views * 8 + n] for n in range(8)]
        field = lambda f: raw[f, block, :]
        u = cam[0] * field(0) + cam[1] * field(1) + cam[2] * field(2) + cam[3]
        w = cam[4] * field(0) + cam[5] * field(1) + cam[6] * field(2) + cam[7]
        d0, d1, d2 = jnp.exp(field(3)), jnp.exp(field(5)), jnp.exp(field(8))
        factor = []
        for i in range(2):
            m = cam[4 * i : 4 * i + 3]
            factor.append(
                (
                    m[0] * d0 + m[1] * field(4) + m[2] * field(6),
                    m[1] * d1 + m[2] * field(7),
                    m[2] * d2,
                )
            )
        f0, f1 = factor
        s00 = f0[0] * f0[0] + f0[1] * f0[1] + f0[2] * f0[2] + 0.3
        s01 = f0[0] * f1[0] + f0[1] * f1[1] + f0[2] * f1[2]
        s11 = f1[0] * f1[0] + f1[1] * f1[1] + f1[2] * f1[2] + 0.3
        inverse = 1.0 / (s00 * s11 - s01 * s01)
        conic = (s11 * inverse, -s01 * inverse, s00 * inverse)
        here = group_ref[block, :] < GROUPS
        return here, cam, block, u, w, (d0, d1, d2), f0, f1, conic

    for v in range(2 * views):
        here, cam, block, u, w, _, _, _, (ka, kb, kc) = project(v)
        x_line = ka * u + kb * w
        y_line = kb * u + kc * w
        log_opacity = math.log(0.95) - jnp.log(1.0 + jnp.exp(-raw[9, block, :]))
        level = log_opacity - 0.5 * (u * x_line + w * y_line)
        terms = (-0.5 * ka, -kb, -0.5 * kc, x_line, y_line)
        for n, term in enumerate(terms):
            rec[n, block, :] = jnp.where(here, term * LOG2E, 0.0)
        rec[5, block, :] = jnp.where(here, level * LOG2E, OFF)
        for c in range(3):
            rec[6 + c, block, :] = raw[10 + c, block, :]

    lane_row = lax.broadcasted_iota(jnp.int32, (GROUPS, pixels), 0)
    own_chunk = (lax.broadcasted_iota(jnp.int32, (GROUPS, slots), 1) & 7) == sub
    zero_pix = jnp.zeros((8, pixels), F32)

    def paired(a, b):
        return a + pltpu.roll(b, 3, 0)

    def render(tile, positions):
        zero_rows = jnp.zeros((8, positions), F32)
        used = slice(0, positions)
        lives = [live_of(t) for t in tile]
        sweeps = [range(g, g + SWEEP) for g in range(0, BATCH, SWEEP)]

        def sweep(body, carry):
            out = []
            for group in sweeps:
                blocks = (chunk_rows(functools.reduce(jnp.maximum, [lives[g] for g in group])) + 3) >> 2
                out += lax.fori_loop(0, blocks, partial(body, group), tuple(carry[g] for g in group))
            return out
        for g, t in enumerate(tile):
            for n in range(6):
                row_s[g, n : n + 1, :] = rec[n, pl.ds(t, 1), :]
            for c in range(3):
                row_s[g, 8 + c : 9 + c, :] = rec[6 + c, pl.ds(t, 1), :]
        for g in range(BATCH):
            lhs = jnp.concatenate(pieces_of(row_s[g, 0:8, used], 3) + [zero_rows], axis=0).astype(BF16)
            c_s[g, used, :] = dot_tn(lhs, mono_ref[...])
        colour = [pieces_of(row_s[g, 8:16, used], 3) for g in range(BATCH)]

        def through(group, i, prods):
            rows = pl.ds(pl.multiple_of(i * 32, 32), 32)
            out = []
            for g, last in zip(group, prods):
                cover = jnp.exp2(c_s[g, rows, :])
                c_s[g, rows, :] = cover
                keep = 1.0 - cover
                out.append(last * ((keep[0:8] * keep[8:16]) * (keep[16:24] * keep[24:32])))
            return tuple(out)

        ones = jnp.ones((GROUPS, pixels), F32)
        lead = sweep(through, [ones] * BATCH)
        for g in range(BATCH):
            scan = lead[g]
            for step in (1, 2, 4):
                scan = scan * jnp.where(lane_row >= step, pltpu.roll(scan, step, 0), 1.0)
            lead[g] = jnp.where(lane_row >= 1, pltpu.roll(scan, 1, 0), 1.0)

        def weights(cover, prod):
            out = []
            for h in range(4):
                weight = prod * cover[8 * h : 8 * h + 8]
                prod = prod - weight
                out.append(weight)
            return out, prod

        def weigh(group, i, prods):
            rows = pl.ds(pl.multiple_of(i * 32, 32), 32)
            out = []
            for g, last in zip(group, prods):
                parts, prod = weights(c_s[g, rows, :], last)
                weight = jnp.concatenate(parts, axis=0)
                high = weight.astype(BF16)
                w_hi[g, rows, :] = high
                w_lo[g, rows, :] = (weight - high.astype(F32)).astype(BF16)
                out.append(prod)
            return tuple(out)

        sweep(weigh, lead)

        after = []
        for g, t in enumerate(tile):
            v, tl = lax.div(t, kept), lax.rem(t, kept)
            spread = [
                jnp.where(own_chunk[:, used], jnp.broadcast_to(piece[c : c + 1], (GROUPS, positions)), 0.0)
                for c in range(3)
                for piece in colour[g]
            ]
            lhs = jnp.concatenate(spread + [zero_rows], axis=0).astype(BF16)
            image = dot_nn(lhs, w_hi[g, used, :]) + dot_nn(lhs, w_lo[g, used, :])
            rest = jnp.zeros((GROUPS, pixels), F32)
            for c in range(3):
                part = image[24 * c : 24 * c + 8] + image[24 * c + 8 : 24 * c + 16] + image[24 * c + 16 : 24 * c + 24]
                whole = jnp.sum(part, axis=0, keepdims=True)
                got[v, c, pl.ds(tl, 1), :] = whole
                miss = whole - want[v, c, pl.ds(tl, 1), :]
                row_2[g, c : c + 1, :] = miss
                rest = rest + part * miss
            for step in (1, 2, 4):
                rest = rest + jnp.where(lane_row < GROUPS - step, pltpu.roll(rest, GROUPS - step, 0), 0.0)
            after.append(rest)
        missed = [pieces_of(row_2[g], 3) for g in range(BATCH)]
        for g in range(BATCH):
            c1, c2, c3 = colour[g]
            m1, m2, m3 = missed[g]
            lhs = jnp.concatenate([paired(c1, c1), paired(c2, c1), paired(c2, c3), zero_rows], axis=0)
            rhs = jnp.concatenate([paired(m1, m2), paired(m1, m3), paired(m2, m1), zero_pix], axis=0)
            h_s[g, used, :] = dot_tn(lhs.astype(BF16), rhs.astype(BF16))

        def settle(group, i, carry):
            rows = pl.ds(pl.multiple_of(i * 32, 32), 32)
            out = []
            for g, (prod, tail) in zip(group, carry):
                cover = c_s[g, rows, :]
                pull = h_s[g, rows, :]
                parts, prod = weights(cover, prod)
                ratio = cover / (1.0 - cover)
                slopes = []
                for h in range(4):
                    cut = slice(8 * h, 8 * h + 8)
                    part = parts[h] * pull[cut]
                    tail = tail - part
                    slopes.append(part - ratio[cut] * tail)
                slope = jnp.concatenate(slopes, axis=0)
                high = slope.astype(BF16)
                rest = slope - high.astype(F32)
                middle = rest.astype(BF16)
                g_1[g, rows, :] = high
                g_2[g, rows, :] = middle
                g_3[g, rows, :] = (rest - middle.astype(F32)).astype(BF16)
                out.append((prod, tail))
            return tuple(out)

        sweep(settle, list(zip(lead, after)))
        mono = mono_ref[0:16, :]
        for g in range(BATCH):
            moments = dot_nt(mono, g_1[g, used, :]) + dot_nt(mono, g_2[g, used, :]) + dot_nt(mono, g_3[g, used, :])
            miss_lhs = jnp.concatenate(missed[g] + [zero_pix], axis=0).astype(BF16)
            tint = dot_nt(miss_lhs, w_hi[g, used, :]) + dot_nt(miss_lhs, w_lo[g, used, :])
            row_s[g, 0:6, used] = moments[0:6]
            row_s[g, 8:11, used] = (tint[0:8] + tint[8:16] + tint[16:24])[0:3]
        for g, t in enumerate(tile):
            for n in range(6):
                mom[n, pl.ds(t, 1), :] = row_s[g, n : n + 1, :]
            for c in range(3):
                mom[6 + c, pl.ds(t, 1), :] = row_s[g, 8 + c : 9 + c, :]

    in_turn(render)
    image_ref[...] = got[0:views]
    their_image_ref[...] = got[views:]

    for v in range(2 * views):
        here, cam, block, u, w, (d0, d1, d2), f0, f1, (ka, kb, kc) = project(v)
        mxx, mxy, myy, mx, my, m1 = [jnp.where(here, mom[n, block, :], 0.0) for n in range(6)]
        dx = mx - u * m1
        dy = my - w * m1
        dxx = mxx - 2.0 * u * mx + u * u * m1
        dxy = mxy - u * my - w * mx + u * w * m1
        dyy = myy - 2.0 * w * my + w * w * m1
        gu = ka * dx + kb * dy
        gw = kb * dx + kc * dy
        ax, ay = ka * dxx + kb * dxy, ka * dxy + kb * dyy
        bx, by = kb * dxx + kc * dxy, kb * dxy + kc * dyy
        h00 = ax * ka + ay * kb
        h01 = ax * kb + ay * kc
        h11 = bx * kb + by * kc
        g0 = [h00 * f0[j] + h01 * f1[j] for j in range(3)]
        g1 = [h01 * f0[j] + h11 * f1[j] for j in range(3)]
        for k in range(3):
            grad[k, block, :] = cam[k] * gu + cam[4 + k] * gw
        grad[3, block, :] = (cam[0] * g0[0] + cam[4] * g1[0]) * d0
        grad[4, block, :] = cam[1] * g0[0] + cam[5] * g1[0]
        grad[5, block, :] = (cam[1] * g0[1] + cam[5] * g1[1]) * d1
        grad[6, block, :] = cam[2] * g0[0] + cam[6] * g1[0]
        grad[7, block, :] = cam[2] * g0[1] + cam[6] * g1[1]
        grad[8, block, :] = (cam[2] * g0[2] + cam[6] * g1[2]) * d2
        grad[9, block, :] = m1 - m1 / (1.0 + jnp.exp(-raw[9, block, :]))
        for c in range(3):
            grad[10 + c, block, :] = mom[6 + c, block, :]

    def give(tile, positions):
        for g, t in enumerate(tile):
            mine = sub[:, 0:positions] == group_ref[pl.ds(t, 1), :][:, 0:positions]
            spread = [
                jnp.where(mine, jnp.broadcast_to(grad[f, pl.ds(t, 1), :][:, 0:positions], (GROUPS, positions)), 0.0)
                for f in range(FIELDS)
            ]
            spread.append(jnp.zeros((lanes - used, positions), F32))
            buf[g, 0:positions, :] = jnp.transpose(jnp.concatenate(spread, axis=0))
        for g, t in enumerate(tile):

            def add(i, t=t, g=g):
                for k in range(0, GROUPS, len(accs)):
                    where = [row_ref[t * slots + i * GROUPS + k + n] for n in range(len(accs))]
                    olds = [accs[n][pl.ds(where[n], 1), :] for n in range(len(accs))]
                    news = [buf[g, pl.ds(i * GROUPS + k + n, 1), :] for n in range(len(accs))]
                    for n in range(len(accs)):
                        accs[n][pl.ds(where[n], 1), :] = olds[n] + news[n]

            repeat(chunk_rows(live_of(t)), 4, add)

    in_turn(give)

    def finish(q, _):
        for base, ref in ((0, grad_mine_ref), (half, grad_other_ref)):
            for d in range(column):
                start = pl.multiple_of((base + q * column + d) * lanes, lanes)
                sums = [acc[pl.ds(start, lanes), :] for acc in accs]
                while len(sums) > 1:
                    sums = [a + b for a, b in zip(sums[::2], sums[1::2])]
                total = sums[0]
                ref[q * column + d] = jnp.transpose(total)[0:used]
        return 0

    lax.fori_loop(0, chips, finish, 0)


def tail_kernel(*refs):
    parts, (centres_ref, shape_ref, opacity_ref, colours_ref), total = refs[:-5], refs[-5:-1], refs[-1]
    lanes = total.shape[1]
    value = parts[0][...]
    for part in parts[1:]:
        value = value + part[...]
    total[...] = value
    field = 0
    for ref in (centres_ref, shape_ref, opacity_ref, colours_ref):
        for row in range(ref.shape[0]):
            for k in range(GROUPS):
                at = field * GROUPS + k
                ref[row : row + 1, k * lanes : (k + 1) * lanes] = total[at : at + 1, :]
            field += 1


def monomials(pixels):
    side = math.isqrt(pixels)
    index = np.arange(pixels)
    x = (index % side) - (side - 1) / 2.0
    y = (index // side) - (side - 1) / 2.0
    one = np.ones_like(x)
    zero = np.zeros_like(x)
    group = np.stack([x * x, x * y, y * y, x, y, one, zero, zero])
    return jnp.asarray(np.concatenate([group, group, group, np.zeros_like(group)]), BF16)


def gather(array, axis, masks):
    got = {mask: swap(array, axis, mask) for mask in sorted(masks, reverse=True)}
    return [got[mask] for mask in masks]


def swap(array, axis, mask):
    size = lax.axis_size(axis)
    return lax.ppermute(array, axis, [(i, i ^ mask) for i in range(size)])


def shards(centres, shape_raw, opacity_logit, colours, camera, target, intersection_ids, depth_order, live_count):
    view_group = lax.axis_size("view")
    tile_group = lax.axis_size("tile")
    devices = view_group * tile_group
    chips = tile_group // 2
    own_count = centres.shape[1]
    lanes = own_count // GROUPS
    views, tiles_view, slots = intersection_ids.shape
    tiles = views * tiles_view
    pixels = target.shape[3]
    view_index = lax.axis_index("view")
    tile_index = lax.axis_index("tile")
    me = (view_index * tile_group + tile_index).astype(jnp.int32)

    totals = jnp.sum(live_count, axis=1)
    place = lax.broadcasted_iota(jnp.int32, (1, tiles_view, tiles_view), 2)
    earlier = place < lax.broadcasted_iota(jnp.int32, (1, tiles_view, tiles_view), 1)
    within = jnp.sum(jnp.where(earlier, live_count[:, None, :], 0), axis=2)

    smem = pl.BlockSpec(memory_space=pltpu.SMEM)
    vmem = pl.BlockSpec(memory_space=pltpu.VMEM)
    kept = tiles_view // 2
    part_tiles = views * kept
    dims = (log2_of(own_count), log2_of(lanes), log2_of(view_group), log2_of(tile_group))
    prep_options = dict(
        scratch_shapes=[
            pltpu.VMEM((3, part_tiles, slots), F32),
            pltpu.VMEM((part_tiles, slots), F32),
            pltpu.VMEM((part_tiles, slots), F32),
            pltpu.VMEM((UNROLL, 16, slots), F32),
            pltpu.VMEM((part_tiles, slots), jnp.int32),
            pltpu.VMEM((part_tiles, slots), F32),
        ],
        compiler_params=pltpu.CompilerParams(vmem_limit_bytes=8 * 1024 * 1024),
        cost_estimate=pl.CostEstimate(flops=4_000_000_000, bytes_accessed=8 * tiles * slots, transcendentals=0),
    )
    prep_own = pl.pallas_call(
        partial(prep_own_kernel, dims),
        out_shape=[
            jax.ShapeDtypeStruct((part_tiles, slots), jnp.int32),
            jax.ShapeDtypeStruct((part_tiles, slots), jnp.int32),
            jax.ShapeDtypeStruct((views * 8,), F32),
        ],
        in_specs=[smem] * 3 + [vmem] * 2,
        out_specs=[vmem, vmem, smem],
        name="prep_own",
        **prep_options,
    )
    prep_their = pl.pallas_call(
        partial(prep_their_kernel, dims),
        out_shape=[
            jax.ShapeDtypeStruct((part_tiles + 8, slots), jnp.int32),
            jax.ShapeDtypeStruct((part_tiles, slots), jnp.int32),
        ],
        in_specs=[smem] * 2 + [vmem],
        out_specs=[vmem] * 2,
        name="prep_their",
        **prep_options,
    )

    mirror = tile_group - 1
    target = target.transpose(0, 2, 1, 3)
    message = jnp.concatenate(
        [
            intersection_ids[:, kept:].reshape(part_tiles, slots).astype(F32),
            depth_order[:, kept:].reshape(part_tiles, slots).astype(F32),
            target[:, :, kept:].reshape(3 * part_tiles, pixels),
            jnp.pad(live_count[:, kept:].astype(F32), ((0, 8 - views), (0, slots - kept))),
        ]
    )
    fields = jnp.concatenate([centres, shape_raw, opacity_logit[None], colours], axis=0)
    block = fields.reshape(FIELDS * GROUPS, lanes)
    note = jnp.pad(totals.astype(F32)[None], ((0, 7), (0, lanes - views)))
    column = jnp.concatenate([block] + gather(block, "view", range(1, view_group)) + [note])
    message = swap(message, "tile", mirror)
    column, me = lax.optimization_barrier((column, me))
    mine = jnp.stack([column] + gather(column, "tile", range(2, tile_group, 2)))
    own_rows, own_group, cam = prep_own(me[None], live_count, camera, intersection_ids, depth_order)
    their_live = message[5 * part_tiles : 5 * part_tiles + views, :kept].astype(jnp.int32)
    live_now = jnp.concatenate([live_count[:, :kept].reshape(-1), their_live.reshape(-1)])
    their_rows, their_group = prep_their(me[None], live_now, message)
    rows = jnp.concatenate([own_rows, their_rows]).reshape(-1)
    mine, rows, own_group, their_group, cam = lax.optimization_barrier((mine, rows, own_group, their_group, cam))
    other = swap(mine, "tile", 1)

    table_rows = devices * lanes
    square = (BATCH, slots, pixels)
    half = (chips * view_group, FIELDS * GROUPS, lanes)
    accs = ACCS if devices <= 32 else 2
    room = 4 * table_rows * lanes * (accs + 2) + 16 * 1024 * 1024
    splat = pl.pallas_call(
        partial(splat_kernel, (views, tiles_view, slots, pixels, lanes, view_group)),
        out_shape=[
            jax.ShapeDtypeStruct((views, 3, kept, pixels), F32),
            jax.ShapeDtypeStruct((views, 3, tiles_view - kept, pixels), F32),
            jax.ShapeDtypeStruct(half, F32),
            jax.ShapeDtypeStruct(half, F32),
        ],
        in_specs=[smem] * 3 + [vmem] * 7,
        out_specs=[vmem] * 4,
        scratch_shapes=[
            pltpu.VMEM((table_rows, lanes), F32),
            pltpu.VMEM((BATCH, slots, lanes), F32),
            pltpu.VMEM((FIELDS, tiles, slots), F32),
            pltpu.VMEM((9, tiles, slots), F32),
            pltpu.VMEM((9, tiles, slots), F32),
            pltpu.VMEM((FIELDS, tiles, slots), F32),
            pltpu.VMEM(square, F32),
            pltpu.VMEM(square, F32),
        ]
        + [pltpu.VMEM(square, BF16)] * 5
        + [pltpu.VMEM((BATCH, 16, slots), F32), pltpu.VMEM((BATCH, 8, pixels), F32)]
        + [pltpu.VMEM((2 * views, 3, kept, pixels), F32)] * 2
        + [pltpu.VMEM((tiles, slots), jnp.int32)]
        + [pltpu.VMEM((table_rows, lanes), F32)] * accs,
        compiler_params=pltpu.CompilerParams(vmem_limit_bytes=room),
        name="splat",
    )
    image, their_image, grad_mine, grad_other = splat(
        cam,
        rows,
        live_now,
        own_group,
        their_group,
        mine,
        other,
        target,
        message,
        monomials(pixels),
    )

    row = view_group * FIELDS * GROUPS
    counts = jnp.stack([mine[:, row, 0:views], other[:, row, 0:views]], axis=1)
    counts = counts.reshape(tile_group, views).astype(jnp.int32)
    peer = lax.broadcasted_iota(jnp.int32, counts.shape, 0) ^ tile_index
    whole = jnp.sum(counts, axis=0)
    before = jnp.sum(jnp.where(peer < tile_index, counts, 0), axis=0)
    next_owner = (before[:, None] + within) * tile_group // whole[:, None]

    grad_other = swap(grad_other, "tile", 1)
    joined = grad_mine + grad_other
    joined, their_image = lax.optimization_barrier((joined, their_image))
    joined = joined.reshape(chips, view_group, FIELDS * GROUPS, lanes)
    part = joined[0]
    for m in reversed(range(1, chips)):
        part = part + swap(joined[m], "tile", 2 * m)
    rendered = jnp.concatenate([image, swap(their_image, "tile", mirror)], axis=2)
    parts = [part[0]] + [swap(part[m], "view", m) for m in reversed(range(1, view_group))]
    tail = pl.pallas_call(
        tail_kernel,
        out_shape=[jax.ShapeDtypeStruct((count, own_count), F32) for count in (3, 6, 1, 3)],
        in_specs=[vmem] * len(parts),
        out_specs=[vmem] * 4,
        scratch_shapes=[pltpu.VMEM((FIELDS * GROUPS, lanes), F32)],
        compiler_params=pltpu.CompilerParams(vmem_limit_bytes=8 * 1024 * 1024),
        name="tail",
    )
    grad_centres, grad_shape, grad_opacity, grad_colours = tail(*parts)
    return (
        rendered.transpose(0, 2, 1, 3),
        grad_centres,
        grad_shape,
        grad_opacity[0],
        grad_colours,
        next_owner,
    )


def solution(mesh):
    in_specs = (
        P(None, ("view", "tile")),
        P(None, ("view", "tile")),
        P(("view", "tile")),
        P(None, ("view", "tile")),
        P(),
        P("view", "tile", None, None),
        P("view", "tile", None),
        P("view", "tile", None),
        P("view", "tile"),
    )
    out_specs = (
        P("view", "tile", None, None),
        P(None, ("view", "tile")),
        P(None, ("view", "tile")),
        P(("view", "tile")),
        P(None, ("view", "tile")),
        P("view", "tile"),
    )
    return jax.shard_map(shards, mesh=mesh, in_specs=in_specs, out_specs=out_specs, check_vma=False)
```
